32 devices in a mesh: dp: 16 (over z, y, x), tensor: 2 (over core).
Axes of the slice: x: 2, y: 2, z: 4, core: 2. Of those that a mesh axis runs over, the one named last changes fastest.
Arguments:
- tokens: bfloat16 [16384, 768], P('dp'), may hold values from -6 to 6
- token_slot: int32 [16, 1024], P('dp'), may hold values from 0 to 1023, each once within a row
- seq_lengths: int32 [16, 4], P('dp'), may hold values from 1 to 512, 1024 in all within a row
- query_weight: bfloat16 [768, 768], P(None, 'tensor'), may hold values from -0.3125 to 0.3125
- query_bias: float32 [768], P('tensor'), may hold values from -3 to 3
- key_weight: bfloat16 [768, 768], P(None, 'tensor'), may hold values from -0.3125 to 0.3125
- value_weight: bfloat16 [768, 768], P(None, 'tensor'), may hold values from -0.21875 to 0.21875
- value_bias: float32 [768], P('tensor'), may hold values from -3 to 3
- out_weight: bfloat16 [768, 768], P('tensor'), may hold values from -1.25 to 1.25
- out_bias: float32 [768], replicated, may hold values from -3 to 3
- first_gain: float32 [768], replicated, may hold values from 0.25 to 1.75
- first_shift: float32 [768], replicated, may hold values from -3 to 3
- up_weight: bfloat16 [768, 3072], P(None, 'tensor'), may hold values from -0.21875 to 0.21875
- up_bias: float32 [3072], P('tensor'), may hold values from -3 to 3
- down_weight: bfloat16 [3072, 768], P('tensor'), may hold values from -0.109375 to 0.109375
- down_bias: float32 [768], replicated, may hold values from -3 to 3
- second_gain: float32 [768], replicated, may hold values from 0.25 to 1.75
- second_shift: float32 [768], replicated, may hold values from -3 to 3
- cotangent: bfloat16 [16384, 768], P('dp'), may hold values from -6 to 6
Outputs:
- layer_out: bfloat16 [16384, 768], P('dp')
- input_gradient: bfloat16 [16384, 768], P('dp')
- query_weight_gradient: float32 [768, 768], P('dp', 'tensor')
- query_bias_gradient: float32 [768], P(('dp', 'tensor'))
- key_weight_gradient: float32 [768, 768], P('dp', 'tensor')
- value_weight_gradient: float32 [768, 768], P('dp', 'tensor')
- value_bias_gradient: float32 [768], P(('dp', 'tensor'))
- out_weight_gradient: float32 [768, 768], P('tensor', 'dp')
- out_bias_gradient: float32 [768], P(('dp', 'tensor'))
- first_gain_gradient: float32 [768], P(('dp', 'tensor'))
- first_shift_gradient: float32 [768], P(('dp', 'tensor'))
- up_weight_gradient: float32 [768, 3072], P('dp', 'tensor')
- up_bias_gradient: float32 [3072], P(('dp', 'tensor'))
- down_weight_gradient: float32 [3072, 768], P('tensor', 'dp')
- down_bias_gradient: float32 [768], P(('dp', 'tensor'))
- second_gain_gradient: float32 [768], P(('dp', 'tensor'))
- second_shift_gradient: float32 [768], P(('dp', 'tensor'))
The draws below stay inside these ranges and needn't reach their ends.
Inputs may be any that keep to these rules, and one draw needn't show every extreme that they name: `token_slot`: each row orders the 1024 rows that one group receives. `seq_lengths`: each row holds one group's 4 sequence lengths in order; they sum to 1024 and the longest is 512.
All inputs are finite; a program needn't handle non-finite values.
Results may differ from the reference program's by a relative error of at most 0.015.
The reference program's roundings to bfloat16 on the way count: a program that leaves them out, or rounds other values in their place, can miss the bound.
Values may be sent and summed in bfloat16 or wider, within the bound.
No kernel may reach another device: no remote copies, remote signals or barrier semaphores. Data moves between devices by JAX's collectives and lax.ppermute only.
A program may use at most 192 MiB of HBM per device.

```python
import math
import jax
import jax.numpy as jnp
import numpy as np
from jax import lax

D = 768
HEADS = 12
HD = 64
FF = 3072
TOK_DEV = 1024
SEQS = 4
MAXLEN = 512
TOKENS = 16384
N_DP = 16


def shard_levels(rng, shape, cuts, low, high):
    def one(dim, parts):
        steps = jax.random.uniform(jax.random.fold_in(jax.random.fold_in(rng, 6), dim), (parts,), jnp.float32, low / len(cuts), high / len(cuts))
        return jnp.repeat(jnp.exp(steps), shape[dim] // parts).reshape((-1,) + (1,) * (len(shape) - dim - 1))

    loudness = one(*cuts[0])
    for cut in cuts[1:]:
        loudness = loudness * one(*cut)
    return loudness


def profile(amount, total, bound, slope):
    portions = [(1 << 20) // math.isqrt(standing ** slope) + 1 for standing in range(2, amount + 1)]
    rest, holding = total - bound - (amount - 1), [1] * (amount - 1)
    while rest > 0:
        candidates = [i for i in range(amount - 1) if holding[i] < bound]
        whole, remaining = sum([portions[i] for i in candidates]), rest
        for i in candidates:
            more = min(bound - holding[i], max(1, remaining * portions[i] // whole), rest)
            holding[i] = holding[i] + more
            rest = rest - more
    return np.array([bound] + holding)


def uneven(stream_key, count, total, reach, skew):
    if count == 2:
        one = jax.random.randint(stream_key, (), max(1, total - reach), min(reach, total - 1) + 1)
        return jnp.stack([one, total - one])
    tallies = jnp.asarray(profile(count, total, reach, skew), jnp.int32)
    twos = (count - 1) // 2
    giver, sink = tallies[1:1 + 2 * twos:2], tallies[2:2 + 2 * twos:2]
    room = jnp.minimum(giver - 1, reach - sink)
    passed = jax.random.randint(jax.random.fold_in(stream_key, 1), (twos,), 0, 1 << 20) % (room + 1)
    tallies = tallies.at[1:1 + 2 * twos:2].set(giver - passed).at[2:2 + 2 * twos:2].set(sink + passed)
    return tallies[jax.random.permutation(jax.random.fold_in(stream_key, 2), count)]


def normal_values(rng, extent, spread, limit, cuts=(), kind=jnp.bfloat16):
    values = jax.random.normal(rng, extent, jnp.float32) * spread
    if len(cuts) > 0:
        values = shard_levels(rng, extent, cuts, -0.22, 0.18) * values
    return jnp.clip(values, min=-limit, max=limit).astype(kind)


def setup_inputs(seed: int = 0) -> dict:
    splits = jax.random.split(jax.random.key(seed), 20)
    tokens = normal_values(splits[0], (TOKENS, D), 1.0, 6.0, ((0, 16),))
    token_slot = jax.vmap(lambda own: jax.random.permutation(own, TOK_DEV))(jax.random.split(splits[1], N_DP)).reshape((N_DP, TOK_DEV)).astype(jnp.int32)
    seq_lengths = jax.vmap(lambda own: uneven(own, SEQS, TOK_DEV, MAXLEN, 2))(jax.random.split(splits[2], N_DP)).reshape((N_DP, SEQS)).astype(jnp.int32)
    query_weight = normal_values(splits[3], (D, D), (D // 2) ** -0.5, 0.3125, ((1, 2),))
    query_bias = normal_values(splits[4], (D,), 0.5, 3.0, ((0, 2),), jnp.float32)
    key_weight = normal_values(splits[5], (D, D), (D // 2) ** -0.5, 0.3125, ((1, 2),))
    value_weight = normal_values(splits[6], (D, D), D ** -0.5, 0.21875, ((1, 2),))
    value_bias = normal_values(splits[7], (D,), 0.5, 3.0, ((0, 2),), jnp.float32)
    out_weight = normal_values(splits[8], (D, D), (D // 32) ** -0.5, 1.25, ((0, 2),))
    out_bias = normal_values(splits[9], (D,), 0.5, 3.0, (), jnp.float32)
    first_gain = jnp.clip(1.0 + 0.15 * jax.random.normal(splits[10], (D,), jnp.float32), 0.25, 1.75)
    first_shift = normal_values(splits[11], (D,), 0.5, 3.0, (), jnp.float32)
    up_weight = normal_values(splits[12], (D, FF), D ** -0.5, 0.21875, ((1, 2),))
    up_bias = normal_values(splits[13], (FF,), 0.5, 3.0, ((0, 2),), jnp.float32)
    down_weight = normal_values(splits[14], (FF, D), FF ** -0.5, 0.109375, ((0, 2),))
    down_bias = normal_values(splits[15], (D,), 0.5, 3.0, (), jnp.float32)
    second_gain = jnp.clip(1.0 + 0.15 * jax.random.normal(splits[16], (D,), jnp.float32), 0.25, 1.75)
    second_shift = normal_values(splits[17], (D,), 0.5, 3.0, (), jnp.float32)
    cotangent = normal_values(splits[18], (TOKENS, D), 1.0, 6.0, ((0, 16),))
    return dict(tokens=tokens, token_slot=token_slot, seq_lengths=seq_lengths, query_weight=query_weight, query_bias=query_bias, key_weight=key_weight, value_weight=value_weight, value_bias=value_bias, out_weight=out_weight, out_bias=out_bias, first_gain=first_gain, first_shift=first_shift, up_weight=up_weight, up_bias=up_bias, down_weight=down_weight, down_bias=down_bias, second_gain=second_gain, second_shift=second_shift, cotangent=cotangent)


@jax.custom_vjp
def low(v):
    return lax.optimization_barrier(v.astype(jnp.bfloat16)).astype(jnp.float32)

@jax.custom_vjp
def low_back(v):
    return v

def low_keep(v):
    return (low(v), None)

def low_pass(kept, grad):
    return (grad,)

def back_keep(v):
    return (v, None)

def back_low(kept, grad):
    return (low(grad),)
low.defvjp(low_keep, low_pass)
low_back.defvjp(back_keep, back_low)
EPSILON = 1e-12
MASKED = -1e+30

def matmul(first_op, second_op):
    return jnp.dot(first_op, second_op, precision=lax.Precision.HIGHEST, preferred_element_type=jnp.float32)

def layer_norm(values, gain, shift):
    centre = values - lax.optimization_barrier(jnp.mean(values, axis=-1, keepdims=True))
    inv_scale = lax.rsqrt(lax.optimization_barrier(jnp.mean(centre * centre, axis=-1, keepdims=True)) + EPSILON)
    return centre * inv_scale * gain + shift

def block_forward(tokens, segment, params):
    query_weight, query_bias, key_weight, value_weight, value_bias, out_weight, out_bias, first_gain, first_shift, up_weight, up_bias, down_weight, down_bias, second_gain, second_shift = params
    row_count = tokens.shape[0]
    score_scale = HD ** (-0.5)
    query_rows = low_back(low(matmul(tokens, query_weight) + query_bias)).reshape(row_count, HEADS, HD)
    key_rows = low_back(low(matmul(tokens, key_weight))).reshape(row_count, HEADS, HD)
    value_rows = low_back(low(matmul(tokens, value_weight) + value_bias)).reshape(row_count, HEADS, HD)
    scores = jnp.einsum('qhd,khd->hqk', query_rows, key_rows, precision=lax.Precision.HIGHEST) * score_scale
    same_segment = segment[:, None] == segment[None, :]
    scores = low_back(jnp.where(same_segment[None], scores, MASKED))
    weights = jax.nn.softmax(scores, axis=-1)
    mixed_heads = jnp.einsum('hqk,khd->qhd', low(weights), value_rows, precision=lax.Precision.HIGHEST)
    mixed_heads = low_back(low(mixed_heads.reshape(row_count, HEADS * HD)))
    attended = low_back(matmul(mixed_heads, out_weight)) + out_bias
    hidden = layer_norm(tokens + attended, first_gain, first_shift)
    inner_sum = low_back(matmul(low(hidden), up_weight) + up_bias)
    activated = low(jax.nn.gelu(inner_sum, approximate=False))
    branch = low_back(matmul(activated, down_weight)) + down_bias
    return layer_norm(hidden + branch, second_gain, second_shift)

def reference(tokens, token_slot, seq_lengths, query_weight, query_bias, key_weight, value_weight, value_bias, out_weight, out_bias, first_gain, first_shift, up_weight, up_bias, down_weight, down_bias, second_gain, second_shift, cotangent):
    run_rows = TOK_DEV // N_DP
    group_ids = jnp.arange(N_DP, dtype=jnp.int32)[:, None]
    source_rows = (token_slot // run_rows * TOK_DEV + group_ids * run_rows + token_slot % run_rows).astype(jnp.int32)
    params = tuple((weight.astype(jnp.float32) for weight in (query_weight, query_bias, key_weight, value_weight, value_bias, out_weight, out_bias, first_gain, first_shift, up_weight, up_bias, down_weight, down_bias, second_gain, second_shift)))
    positions = jnp.arange(TOK_DEV, dtype=jnp.int32)

    def one_group(running, pieces):
        rows_index, lengths = pieces
        ends = jnp.cumsum(lengths).astype(jnp.int32)
        segment = lax.optimization_barrier(jnp.sum((positions[:, None] >= ends[None, :]).astype(jnp.int32), axis=1))
        group_tokens = jnp.take(tokens, rows_index, axis=0).astype(jnp.float32)
        group_cotangent = jnp.take(cotangent, rows_index, axis=0).astype(jnp.float32)

        def forward(token_values, weight_values):
            return block_forward(token_values, segment, weight_values)
        output, pullback = jax.vjp(forward, group_tokens, params)
        token_grad, weight_grads = pullback(group_cotangent)
        running = tuple((earlier + addend for earlier, addend in zip(running, weight_grads)))
        return (running, (output.astype(jnp.bfloat16), token_grad.astype(jnp.bfloat16)))
    start_sums = tuple((jnp.zeros_like(weight) for weight in params))
    totals, (outputs, token_grads) = lax.scan(one_group, start_sums, (source_rows, seq_lengths))
    flat_index = source_rows.reshape(-1)
    layer_out = jnp.zeros((TOKENS, D), jnp.bfloat16).at[flat_index].set(outputs.reshape(TOKENS, D))
    input_gradient = jnp.zeros((TOKENS, D), jnp.bfloat16).at[flat_index].set(token_grads.reshape(TOKENS, D))
    return (layer_out, input_gradient, totals[0], totals[1], totals[2], totals[3], totals[4], totals[5], totals[6], totals[7], totals[8], totals[9], totals[10], totals[11], totals[12], totals[13], totals[14])
```

```python
import jax
import jax.numpy as jnp
from jax import lax
from jax.sharding import PartitionSpec as P

HD = 64


EPSILON = 1e-12
MASKED = -1e30
F32 = jnp.float32
BF16 = jnp.bfloat16
SWAP = [(0, 1), (1, 0)]


def product(first_op, second_op):
    return jnp.dot(first_op, second_op, preferred_element_type=F32)


def contract_rows(first_op, second_op):
    return lax.dot_general(
        first_op, second_op, (((0,), (0,)), ((), ())), preferred_element_type=F32
    )


def contract_cols(first_op, second_op):
    return lax.dot_general(
        first_op, second_op, (((1,), (1,)), ((), ())), preferred_element_type=F32
    )


def gelu_slope(values):
    cumulative = 0.5 * (1.0 + lax.erf(values * 0.7071067811865476))
    density = jnp.exp(-0.5 * values * values) * 0.3989422804014327
    return cumulative + values * density


def norm_forward(values, gain, shift):
    centre = values - jnp.mean(values, axis=-1, keepdims=True)
    inv_scale = lax.rsqrt(jnp.mean(centre * centre, axis=-1, keepdims=True) + EPSILON)
    normed = centre * inv_scale
    return (normed * gain + shift, normed, inv_scale)


def norm_backward(upstream, normed, inv_scale, gain):
    scaled = upstream * gain
    return inv_scale * (
        scaled
        - jnp.mean(scaled, axis=-1, keepdims=True)
        - normed * jnp.mean(scaled * normed, axis=-1, keepdims=True)
    )


def swap(values):
    return lax.ppermute(values, "tensor", SWAP)


def masked_scores(query_block, key_rows, segment_block, segment, score_scale):
    scores = (
        jnp.einsum("qhd,khd->hqk", query_block, key_rows, preferred_element_type=F32)
        * score_scale
    )
    return jnp.where(segment_block[None, :, None] == segment[None, None, :], scores, MASKED)


def attention_forward(query_rows, key_rows, value_rows, segment):
    row_count, head_count, head_size = query_rows.shape
    score_scale = head_size ** (-0.5)
    block_rows = min(512, row_count)
    block_count = row_count // block_rows

    def one_block(pieces):
        query_block, segment_block = pieces
        scores = masked_scores(query_block, key_rows, segment_block, segment, score_scale)
        row_peak = jnp.max(scores, axis=-1, keepdims=True)
        exp_scores = jnp.exp(scores - row_peak)
        row_total = jnp.sum(exp_scores, axis=-1, keepdims=True)
        weights = (exp_scores / row_total).astype(BF16)
        mixed_block = jnp.einsum("hqk,khd->qhd", weights, value_rows, preferred_element_type=F32)
        return (mixed_block.astype(BF16), (row_peak + jnp.log(row_total))[..., 0])

    mixed_heads, logsum = lax.map(
        one_block,
        (
            query_rows.reshape(block_count, block_rows, head_count, head_size),
            segment.reshape(block_count, block_rows),
        ),
    )
    return (mixed_heads.reshape(row_count, head_count * head_size), logsum)


def attention_backward(query_rows, key_rows, value_rows, segment, logsum, mixed_grad):
    row_count, head_count, head_size = query_rows.shape
    score_scale = head_size ** (-0.5)
    block_rows = min(512, row_count)
    block_count = row_count // block_rows

    def one_block(totals_pair, pieces):
        key_total, value_total = totals_pair
        query_block, segment_block, logsum_block, grad_block = pieces
        scores = masked_scores(query_block, key_rows, segment_block, segment, score_scale)
        softmax_rows = jnp.exp(scores - logsum_block[..., None])
        weights = softmax_rows.astype(BF16)
        value_total = value_total + jnp.einsum(
            "hqk,qhd->khd", weights, grad_block, preferred_element_type=F32
        )
        pulled = jnp.einsum("qhd,khd->hqk", grad_block, value_rows, preferred_element_type=F32)
        centred = jnp.sum(softmax_rows * pulled, axis=-1, keepdims=True)
        slopes = (softmax_rows * (pulled - centred)).astype(BF16)
        query_part = (
            jnp.einsum("hqk,khd->qhd", slopes, key_rows, preferred_element_type=F32) * score_scale
        )
        key_total = (
            key_total
            + jnp.einsum("hqk,qhd->khd", slopes, query_block, preferred_element_type=F32)
            * score_scale
        )
        return ((key_total, value_total), query_part.astype(BF16))

    zero_rows = jnp.zeros((row_count, head_count, head_size), F32)
    (key_total, value_total), query_grad = lax.scan(
        one_block,
        (zero_rows, zero_rows),
        (
            query_rows.reshape(block_count, block_rows, head_count, head_size),
            segment.reshape(block_count, block_rows),
            logsum,
            mixed_grad.reshape(block_count, block_rows, head_count, head_size),
        ),
    )
    flat_width = head_count * head_size
    return (
        query_grad.reshape(row_count, flat_width),
        key_total.astype(BF16).reshape(row_count, flat_width),
        value_total.astype(BF16).reshape(row_count, flat_width),
    )


def near_groups(groups):
    near = 4 if groups % 4 == 0 else 1
    return near, groups // near


def scatter_sum(terms):
    groups = lax.axis_size("dp")
    near, far = near_groups(groups)
    rows, columns = terms.shape
    share = rows // groups
    terms = terms.reshape(far, near, share, columns).transpose(1, 0, 2, 3)
    terms = terms.reshape(rows, columns).astype(BF16)
    within = [[f * near + n for n in range(near)] for f in range(far)]
    across = [[f * near + n for f in range(far)] for n in range(near)]
    terms = lax.psum_scatter(
        terms, "dp", scatter_dimension=0, tiled=True, axis_index_groups=within
    )
    return lax.psum_scatter(
        terms, "dp", scatter_dimension=0, tiled=True, axis_index_groups=across
    )


def local(
    tokens,
    token_slot,
    seq_lengths,
    query_weight,
    query_bias,
    key_weight,
    value_weight,
    value_bias,
    out_weight,
    out_bias,
    first_gain,
    first_shift,
    up_weight,
    up_bias,
    down_weight,
    down_bias,
    second_gain,
    second_shift,
    cotangent,
):
    groups = lax.axis_size("dp")
    row_count, feature_count = tokens.shape
    run_rows = row_count // groups
    half_run = run_rows // 2
    half = row_count // 2
    mine = lax.axis_index("tensor")

    def deal(values):
        part = lax.dynamic_slice_in_dim(
            values.reshape(groups, run_rows, feature_count), mine * half_run, half_run, 1
        )
        part = lax.all_to_all(part, "dp", split_axis=0, concat_axis=0, tiled=True)
        return part.reshape(half, feature_count)

    slots = token_slot[0]
    slots = jnp.where(mine == 0, slots, jnp.concatenate([slots[half:], slots[:half]]))
    run, place = slots // run_rows, slots % run_rows
    held = (place // half_run + mine) % 2
    column = held * half + run * half_run + place % half_run
    pick = (column[:, None] == jnp.arange(row_count, dtype=jnp.int32)[None, :]).astype(BF16)
    place_mine = (column[:, None] == jnp.arange(half, dtype=jnp.int32)[None, :]).astype(BF16)

    key_other, query_other, value_other = swap(key_weight), swap(query_weight), swap(value_weight)
    out_other, up_other, down_other = swap(out_weight), swap(up_weight), swap(down_weight)
    up_bias_other = swap(up_bias)

    token_rows = deal(tokens)
    token_rows = jnp.concatenate([token_rows, swap(token_rows)], axis=0)
    cot_rows = deal(cotangent)
    cot_rows = jnp.concatenate([cot_rows, swap(cot_rows)], axis=0)
    inputs = product(pick, token_rows).astype(BF16)
    upstream = product(pick[:half], cot_rows)

    positions = (jnp.arange(row_count, dtype=jnp.int32) + mine * half) % row_count
    ends = jnp.cumsum(seq_lengths[0])
    segment = jnp.sum((positions[:, None] >= ends[None, :]).astype(jnp.int32), axis=1)
    local_heads = query_weight.shape[1] // HD
    query_rows = (
        (product(inputs, query_weight) + query_bias)
        .astype(BF16)
        .reshape(row_count, local_heads, HD)
    )
    key_rows = product(inputs, key_weight).astype(BF16).reshape(row_count, local_heads, HD)
    value_rows = (
        (product(inputs, value_weight) + value_bias)
        .astype(BF16)
        .reshape(row_count, local_heads, HD)
    )
    mixed_flat, logsum = attention_forward(query_rows, key_rows, value_rows, segment)
    mixed_mine, mixed_other = mixed_flat[:half], swap(mixed_flat[half:])
    attended = product(mixed_mine, out_weight) + product(mixed_other, out_other)
    first_in = inputs[:half].astype(F32) + attended + out_bias
    hidden, first_normed, first_inv = norm_forward(first_in, first_gain, first_shift)
    hidden_low = hidden.astype(BF16)
    inner_mine = product(hidden_low, up_weight) + up_bias
    inner_other = product(hidden_low, up_other) + up_bias_other
    act_mine = jax.nn.gelu(inner_mine, approximate=False).astype(BF16)
    act_other = jax.nn.gelu(inner_other, approximate=False).astype(BF16)
    branch = product(act_mine, down_weight) + product(act_other, down_other)
    second_in = hidden + branch + down_bias
    output, second_normed, second_inv = norm_forward(second_in, second_gain, second_shift)
    output_low = output.astype(BF16)

    def give_back(values, extra=None):
        rows = jnp.concatenate([values, swap(values)], axis=0)
        part = contract_rows(place_mine, rows).astype(BF16)
        part = part.reshape(groups, half_run, feature_count)
        if extra is not None:
            part = jnp.concatenate([part, extra], axis=1)
        part = lax.all_to_all(part, "dp", split_axis=0, concat_axis=0, tiled=True)
        if extra is not None:
            part, extra = part[:, :half_run], part[:, half_run:]
        other = swap(part)
        low = jnp.where(mine == 0, part, other)
        high = jnp.where(mine == 0, other, part)
        whole = jnp.concatenate([low, high], axis=1).reshape(row_count, feature_count)
        return whole if extra is None else (whole, extra)

    layer_out = give_back(output_low)
    second_grad = norm_backward(upstream, second_normed, second_inv, second_gain)
    second_gain_grad = jnp.sum(upstream * second_normed, axis=0)
    second_shift_grad = jnp.sum(upstream, axis=0)
    down_bias_grad = jnp.sum(second_grad, axis=0)
    second_low = second_grad.astype(BF16)
    down_grad_mine = contract_rows(second_low, act_mine)
    down_grad_other = contract_rows(second_low, act_other)
    inner_grad_mine = (contract_cols(second_low, down_weight) * gelu_slope(inner_mine)).astype(BF16)
    inner_grad_other = (contract_cols(second_low, down_other) * gelu_slope(inner_other)).astype(
        BF16
    )
    up_bias_mine = jnp.sum(inner_grad_mine, axis=0, dtype=F32)
    up_bias_theirs = jnp.sum(inner_grad_other, axis=0, dtype=F32)
    up_grad_mine = contract_rows(hidden_low, inner_grad_mine)
    up_grad_other = contract_rows(hidden_low, inner_grad_other)
    down_sum = scatter_sum(down_grad_mine + swap(down_grad_other.astype(BF16)).astype(F32))
    up_sum = scatter_sum(up_grad_mine + swap(up_grad_other.astype(BF16)).astype(F32))

    hidden_grad = (
        second_grad
        + contract_cols(inner_grad_mine, up_weight)
        + contract_cols(inner_grad_other, up_other)
    )
    first_grad = norm_backward(hidden_grad, first_normed, first_inv, first_gain)
    first_gain_grad = jnp.sum(hidden_grad * first_normed, axis=0)
    first_shift_grad = jnp.sum(hidden_grad, axis=0)
    out_bias_grad = jnp.sum(first_grad, axis=0)
    first_low = first_grad.astype(BF16)
    out_grad_mine = contract_rows(first_low, mixed_mine)
    out_grad_other = contract_rows(first_low, mixed_other).astype(BF16)
    out_grad = out_grad_mine + swap(out_grad_other).astype(F32)
    mixed_grad_mine = contract_cols(first_low, out_weight).astype(BF16)
    mixed_grad_other = swap(contract_cols(first_low, out_other).astype(BF16))
    mixed_grad = jnp.concatenate([mixed_grad_mine, mixed_grad_other], axis=0)
    query_grad, key_grad, value_grad = attention_backward(
        query_rows,
        key_rows,
        value_rows,
        segment,
        logsum,
        mixed_grad.reshape(row_count, local_heads, HD),
    )
    query_bias_grad = jnp.sum(query_grad, axis=0, dtype=F32)
    value_bias_grad = jnp.sum(value_grad, axis=0, dtype=F32)
    query_weight_grad = contract_rows(inputs, query_grad)
    key_weight_grad = contract_rows(inputs, key_grad)
    value_weight_grad = contract_rows(inputs, value_grad)
    qkv_sum = jnp.concatenate(
        [out_grad, query_weight_grad, key_weight_grad, value_weight_grad], axis=1
    )
    qkv_sum = scatter_sum(qkv_sum).astype(F32)

    input_part = (
        contract_cols(query_grad[:half], query_weight)
        + contract_cols(key_grad[:half], key_weight)
        + contract_cols(value_grad[:half], value_weight)
        + contract_cols(swap(query_grad[half:]), query_other)
        + contract_cols(swap(key_grad[half:]), key_other)
        + contract_cols(swap(value_grad[half:]), value_other)
    )

    def padded(values):
        return lax.dynamic_update_slice_in_dim(
            jnp.zeros((2 * values.shape[0],), F32), values, mine * values.shape[0], 0
        )

    up_bias_both = padded(up_bias_mine) + lax.dynamic_update_slice_in_dim(
        jnp.zeros((2 * up_bias.shape[0],), F32), up_bias_theirs, (1 - mine) * up_bias.shape[0], 0
    )
    wide = [
        padded(query_bias_grad),
        padded(value_bias_grad),
        out_bias_grad,
        first_gain_grad,
        first_shift_grad,
        down_bias_grad,
        second_gain_grad,
        second_shift_grad,
        up_bias_both,
    ]
    terms = jnp.concatenate([v.reshape(groups, 2, -1) for v in wide], axis=2)
    pieces, rest = [], terms
    for _ in range(3):
        pieces.append(rest.astype(BF16))
        rest = rest - pieces[-1].astype(F32)
    pieces = jnp.stack(pieces, axis=1).reshape(groups, -1)
    extra_rows = -(-pieces.shape[1] // (8 * feature_count)) * 8
    pieces = jnp.pad(pieces, ((0, 0), (0, extra_rows * feature_count - pieces.shape[1])))
    input_gradient, pieces = give_back(
        (first_grad + input_part).astype(BF16),
        pieces.reshape(groups, extra_rows, feature_count),
    )
    count = terms.shape[1] * terms.shape[2]
    pieces = pieces.reshape(groups, -1)[:, : 3 * count].astype(F32)
    sums = jnp.sum(pieces, axis=0).reshape((3,) + terms.shape[1:])
    sums = sums[2] + sums[1] + sums[0]
    packed = lax.dynamic_index_in_dim(sums + swap(sums), mine, 0, keepdims=False)
    devices = 2 * groups
    small, start = [], 0
    for v in wide:
        small.append(packed[start : start + v.shape[0] // devices])
        start += v.shape[0] // devices
    (
        query_bias_sum,
        value_bias_sum,
        out_bias_sum,
        first_gain_sum,
        first_shift_sum,
        down_bias_sum,
        second_gain_sum,
        second_shift_sum,
        up_bias_sum,
    ) = small
    heads_width = query_weight.shape[1]
    return (
        layer_out,
        input_gradient,
        qkv_sum[:, heads_width : 2 * heads_width],
        query_bias_sum,
        qkv_sum[:, 2 * heads_width : 3 * heads_width],
        qkv_sum[:, 3 * heads_width :],
        value_bias_sum,
        qkv_sum[:, :heads_width].T,
        out_bias_sum,
        first_gain_sum,
        first_shift_sum,
        up_sum.astype(F32),
        up_bias_sum,
        down_sum.T.astype(F32),
        down_bias_sum,
        second_gain_sum,
        second_shift_sum,
    )


def solution(mesh):
    rows = P("dp", None)
    in_specs = (
        rows,
        rows,
        rows,
        P(None, "tensor"),
        P("tensor"),
        P(None, "tensor"),
        P(None, "tensor"),
        P("tensor"),
        P("tensor", None),
        P(),
        P(),
        P(),
        P(None, "tensor"),
        P("tensor"),
        P("tensor", None),
        P(),
        P(),
        P(),
        rows,
    )
    spread = P(("dp", "tensor"))
    out_specs = (
        rows,
        rows,
        P("dp", "tensor"),
        spread,
        P("dp", "tensor"),
        P("dp", "tensor"),
        spread,
        P("tensor", "dp"),
        spread,
        spread,
        spread,
        P("dp", "tensor"),
        spread,
        P("tensor", "dp"),
        spread,
        spread,
        spread,
    )
    return jax.shard_map(local, mesh=mesh, in_specs=in_specs, out_specs=out_specs, check_vma=False)
```

```python
import functools
import jax
import jax.numpy as jnp
from jax import lax
from jax.experimental import pallas as pl
from jax.experimental.pallas import tpu as pltpu
from jax.sharding import PartitionSpec as P

HD = 64
LANES = 128
SEG_MAX = 8
QB = 256
KB = 256
ROW_TILE = 64


EPSILON = 1e-12
MASKED = -1e30
F32 = jnp.float32
BF16 = jnp.bfloat16
SWAP = [(0, 1), (1, 0)]
VMEM_LIMIT = 60 << 20


def swap(values):
    return lax.ppermute(values, "tensor", SWAP)


def nt(a, b):
    return lax.dot_general(a, b, (((1,), (1,)), ((), ())), preferred_element_type=F32)


def nn(a, b):
    return jnp.dot(a, b, preferred_element_type=F32)


def segment_ends(lengths):
    ends, end = [], jnp.int32(0)
    for n in range(lengths.shape[1]):
        end = end + lengths[0, n]
        ends.append(end)
    return ends


def bounds(ends, rows, first, last):
    low, high = jnp.int32(0), jnp.int32(rows)
    for end in ends:
        low = jnp.where(end <= first, jnp.maximum(low, end), low)
        high = jnp.where(end > last, jnp.minimum(high, end), high)
    return low, high


def lane_bounds(ends, rows):
    lane = lax.broadcasted_iota(jnp.int32, (1, LANES), 1)
    start = jnp.full((1, LANES), 2 * rows, jnp.int32)
    stop = jnp.zeros((1, LANES), jnp.int32)
    begin = 0
    for n, end in enumerate(ends):
        start = jnp.where(lane == n, begin, start)
        stop = jnp.where(lane == n, end, stop)
        begin = end
    return start, stop


def key_marks(ends, rows, offset):
    start, stop = lane_bounds(ends, rows)
    pos = lax.broadcasted_iota(jnp.int32, (rows, LANES), 0) + offset
    pos = jnp.where(pos >= rows, pos - rows, pos)
    return ((pos >= start) & (pos < stop)).astype(F32).astype(BF16)


def query_marks(ends, rows, first, count):
    start, stop = lane_bounds(ends, rows)
    lane = lax.broadcasted_iota(jnp.int32, (1, LANES), 1)
    pos = lax.broadcasted_iota(jnp.int32, (count, LANES), 0) + first
    return jnp.where((lane < len(ends)) & ((pos < start) | (pos >= stop)), MASKED, 0.0)


def lane_mask(half):
    lane = lax.broadcasted_iota(jnp.int32, (1, LANES), 1)
    return ((lane // HD) == half).astype(F32).astype(BF16)


def of_pair(h):
    return slice(h // 2 * LANES, (h // 2 + 1) * LANES)


def forward_kernel(
    lengths, core, q_ref, k_ref, v_ref, o_ref, lse_ref, keys, values_t, mixed, peaks, totals
):
    rows, width = k_ref.shape
    heads = width // HD
    step = pl.program_id(0)
    ends = segment_ends(lengths)
    offset = core[0] * (rows // 2)

    @pl.when(step == 0)
    def _():
        marks = key_marks(ends, rows, offset)
        for p in range(heads // 2):
            keys[p, :, :LANES] = k_ref[:, of_pair(2 * p)]
            keys[p, :, LANES:] = marks
        for block in range(rows // KB):
            at = slice(block * KB, (block + 1) * KB)
            values_t[block] = v_ref[at, :].astype(F32).T.astype(BF16)

    first = lax.rem(step * QB + offset, rows)
    low, high = bounds(ends, rows, first, first + QB - 1)
    block_low, block_high = low // KB, (high + KB - 1) // KB
    marked = query_marks(ends, rows, first, QB).astype(BF16)
    queries = []
    for p in range(heads // 2):
        query = q_ref[:, of_pair(2 * p)] * BF16(HD**-0.5)
        both = [jnp.concatenate([query * lane_mask(n), marked], axis=1) for n in range(2)]
        queries.append(jnp.concatenate(both, axis=0))
    mixed[...] = jnp.zeros_like(mixed)
    peaks[...] = jnp.full_like(peaks, MASKED)
    totals[...] = jnp.zeros_like(totals)

    def block_step(i, carry):
        start = lax.rem(i * KB + rows - offset, rows)
        at = pl.ds(pl.multiple_of(start, KB), KB)
        block = start // KB
        for p in range(heads // 2):
            scores = nt(keys[p, at, :], queries[p])
            row = slice(p, p + 1)
            peak = jnp.maximum(peaks[row, :], jnp.max(scores, axis=0, keepdims=True))
            shrink = jnp.exp(peaks[row, :] - peak)
            weights = jnp.exp(scores - peak)
            peaks[row, :] = peak
            totals[row, :] = totals[row, :] * shrink + jnp.sum(weights, axis=0, keepdims=True)
            part = nn(values_t[block, of_pair(2 * p), :], weights.astype(BF16))
            for n in range(2):
                h = slice((2 * p + n) * HD, (2 * p + n + 1) * HD)
                q = slice(n * QB, (n + 1) * QB)
                mixed[h, :] = mixed[h, :] * shrink[:, q] + part[n * HD : (n + 1) * HD, q]
        return carry

    lax.fori_loop(block_low, block_high, block_step, 0)
    inverse = 1.0 / totals[...]
    lse = peaks[...] + jnp.log(totals[...])
    for h in range(heads):
        wide = slice(h * HD, (h + 1) * HD)
        p, q = h // 2, slice(h % 2 * QB, (h % 2 + 1) * QB)
        mixed[wide, :] = mixed[wide, :] * inverse[p : p + 1, q]
        lse_ref[h : h + 1, :] = lse[p : p + 1, q]
    o_ref[...] = mixed[...].T.astype(BF16)


def whole(shape):
    return pl.BlockSpec(shape, lambda *_: (0,) * len(shape))


def attention_forward(lengths, core, query_rows, key_rows, value_rows):
    rows, width = query_rows.shape
    heads = width // HD
    tile = pl.BlockSpec((QB, width), lambda i, *_: (i, 0))
    return pl.pallas_call(
        forward_kernel,
        grid_spec=pltpu.PrefetchScalarGridSpec(
            num_scalar_prefetch=2,
            grid=(rows // QB,),
            in_specs=[tile, whole((rows, width)), whole((rows, width))],
            out_specs=[tile, pl.BlockSpec((8, QB), lambda i, *_: (0, i))],
            scratch_shapes=[
                pltpu.VMEM((heads // 2, rows, 2 * LANES), BF16),
                pltpu.VMEM((rows // KB, width, KB), BF16),
                pltpu.VMEM((width, QB), F32),
                pltpu.VMEM((8, 2 * QB), F32),
                pltpu.VMEM((8, 2 * QB), F32),
            ],
        ),
        out_shape=(
            jax.ShapeDtypeStruct((rows, width), BF16),
            jax.ShapeDtypeStruct((8, rows), F32),
        ),
        cost_estimate=pl.CostEstimate(
            flops=8 * rows * rows * LANES * heads,
            bytes_accessed=8 * rows * width,
            transcendentals=rows * rows * heads // 2,
        ),
        compiler_params=params(),
        name="attend",
    )(lengths, core, query_rows, key_rows, value_rows)


def backward_kernel(
    lengths, core, q_ref, do_mine, do_other, o_ref, lse_ref, k_ref, v_ref,
    grad_ref, sums_ref, keys, values, keys_t, dk_sum, dv_sum, dq_sum
):
    rows, width = k_ref.shape
    heads = width // HD
    step = pl.program_id(0)
    steps = rows // QB
    ends = segment_ends(lengths)
    offset = core[0] * (rows // 2)
    scale = HD**-0.5

    @pl.when(step == 0)
    def _():
        marks = key_marks(ends, rows, offset)
        for p in range(heads // 2):
            keys[p, :, :LANES] = k_ref[:, of_pair(2 * p)]
            keys[p, :, LANES:] = marks
            values[p] = v_ref[:, of_pair(2 * p)]
        for block in range(rows // KB):
            at = slice(block * KB, (block + 1) * KB)
            keys_t[block] = k_ref[at, :].astype(F32).T.astype(BF16)
        dk_sum[...] = jnp.zeros_like(dk_sum)
        dv_sum[...] = jnp.zeros_like(dv_sum)

    first = lax.rem(step * QB + offset, rows)
    low, high = bounds(ends, rows, first, first + QB - 1)
    block_low, block_high = low // KB, (high + KB - 1) // KB
    marked = query_marks(ends, rows, first, QB).astype(BF16)
    early = jnp.full((1, width), step, jnp.int32) < steps // 2
    use_mine = early.astype(F32).astype(BF16)
    use_other = (~early).astype(F32).astype(BF16)
    grad_rows = do_mine[...] * use_mine + do_other[...] * use_other
    lane = lax.broadcasted_iota(jnp.int32, (8, LANES), 1)
    row = lax.broadcasted_iota(jnp.int32, (8, LANES), 0)
    by_head = (lane // HD == row).astype(F32).astype(BF16)
    queries, grads, marked_queries, logsums, centres = [], [], [], [], []
    for p in range(heads // 2):
        pair = of_pair(2 * p)
        query = [q_ref[:, pair] * (lane_mask(n) * BF16(scale)) for n in range(2)]
        grad = grad_rows[:, pair]
        exact = grad.astype(F32) * o_ref[:, pair].astype(F32)
        high_term = exact.astype(BF16)
        low_term = (exact - high_term.astype(F32)).astype(BF16)
        centre = nt(by_head, high_term) + nt(by_head, low_term)
        centres.append(jnp.concatenate([centre[0:1, :], centre[1:2, :]], axis=1))
        logsums.append(
            jnp.concatenate([lse_ref[2 * p : 2 * p + 1, :], lse_ref[2 * p + 1 : 2 * p + 2, :]], axis=1)
        )
        queries.append(jnp.concatenate(query, axis=0))
        grads.append(jnp.concatenate([grad * lane_mask(n) for n in range(2)], axis=0))
        marked_queries.append(
            jnp.concatenate([queries[p], jnp.concatenate([marked, marked], axis=0)], axis=1)
        )
    dq_sum[...] = jnp.zeros_like(dq_sum)

    def block_step(i, carry):
        start = lax.rem(i * KB + rows - offset, rows)
        at = pl.ds(pl.multiple_of(start, KB), KB)
        block = start // KB
        for p in range(heads // 2):
            weights = jnp.exp(nt(keys[p, at, :], marked_queries[p]) - logsums[p])
            pulled = nt(values[p, at, :], grads[p])
            dv_sum[at, of_pair(2 * p)] += nn(weights.astype(BF16), grads[p])
            slopes = (weights * (pulled - centres[p])).astype(BF16)
            dk_sum[at, of_pair(2 * p)] += nn(slopes, queries[p])
            part = nn(keys_t[block, of_pair(2 * p), :], slopes)
            for n in range(2):
                h = slice((2 * p + n) * HD, (2 * p + n + 1) * HD)
                dq_sum[h, :] += part[n * HD : (n + 1) * HD, n * QB : (n + 1) * QB]
        return carry

    lax.fori_loop(block_low, block_high, block_step, 0)
    made = (dq_sum[...] * scale).T.astype(BF16)
    grad_ref[pl.ds(pl.multiple_of(step * QB, QB), QB), :width] = made
    total = jnp.sum(made.astype(F32), axis=0, keepdims=True)

    @pl.when(step == 0)
    def _():
        sums_ref[...] = jnp.zeros_like(sums_ref)

    sums_ref[0:1, :] += total

    @pl.when(step == steps - 1)
    def _():
        grad_ref[:, width : 2 * width] = dk_sum[...].astype(BF16)
        made = dv_sum[...].astype(BF16)
        grad_ref[:, 2 * width :] = made
        sums_ref[1:2, :] = jnp.sum(made.astype(F32), axis=0, keepdims=True)


def attention_backward(
    lengths, core, query_rows, key_rows, value_rows, mixed, lse, grad_mine, grad_other
):
    rows, width = query_rows.shape
    heads = width // HD
    steps = rows // QB
    tile = pl.BlockSpec((QB, width), lambda i, *_: (i, 0))
    full = whole((rows, width))
    outs = [jax.ShapeDtypeStruct((rows, 3 * width), BF16), jax.ShapeDtypeStruct((8, width), F32)]
    return pl.pallas_call(
        backward_kernel,
        grid_spec=pltpu.PrefetchScalarGridSpec(
            num_scalar_prefetch=2,
            grid=(steps,),
            in_specs=[
                tile,
                pl.BlockSpec((QB, width), lambda i, *_: (jnp.minimum(i, steps // 2 - 1), 0)),
                pl.BlockSpec((QB, width), lambda i, *_: (jnp.maximum(i - steps // 2, 0), 0)),
                tile,
                pl.BlockSpec((8, QB), lambda i, *_: (0, i)),
                full,
                full,
            ],
            out_specs=[whole(o.shape) for o in outs],
            scratch_shapes=[
                pltpu.VMEM((heads // 2, rows, 2 * LANES), BF16),
                pltpu.VMEM((heads // 2, rows, LANES), BF16),
                pltpu.VMEM((rows // KB, width, KB), BF16),
                pltpu.VMEM((rows, width), F32),
                pltpu.VMEM((rows, width), F32),
                pltpu.VMEM((width, QB), F32),
            ],
        ),
        out_shape=outs,
        cost_estimate=pl.CostEstimate(
            flops=20 * rows * rows * LANES * heads,
            bytes_accessed=16 * rows * width,
            transcendentals=rows * rows * heads // 2,
        ),
        compiler_params=params(),
        name="attend_back",
    )(lengths, core, query_rows, grad_mine, grad_other, mixed, lse, key_rows, value_rows)


def params():
    return pltpu.CompilerParams(vmem_limit_bytes=VMEM_LIMIT)


def cost(flops, moved, transcendentals=0):
    return pl.CostEstimate(flops=flops, bytes_accessed=moved, transcendentals=transcendentals)


def columns_of(slots, core, run_rows, half):
    half_run = run_rows // 2
    run, place = slots // run_rows, slots % run_rows
    held = (place // half_run + core) % 2
    return held * half + run * half_run + place % half_run


def one_hot(column, width, base):
    count = column.shape[1]
    down = jnp.broadcast_to(column, (8, count)).T[:, :1]
    lane = lax.broadcasted_iota(jnp.int32, (count, width), 1) + base
    return (down == lane).astype(F32).astype(BF16)


def intake_kernel(
    run_rows, core, slots, mine_ref, other_ref, q_weight, k_weight, v_weight, q_bias, v_bias,
    x_ref, q_ref, k_ref, v_ref
):
    half = mine_ref.shape[0]
    column = columns_of(slots[...], core[0], run_rows, half)
    rows = nn(one_hot(column, half, 0), mine_ref[...])
    rows = (rows + nn(one_hot(column, half, half), other_ref[...])).astype(BF16)
    x_ref[...] = rows
    q_ref[...] = (nn(rows, q_weight[...]) + q_bias[...]).astype(BF16)
    k_ref[...] = nn(rows, k_weight[...]).astype(BF16)
    v_ref[...] = (nn(rows, v_weight[...]) + v_bias[...]).astype(BF16)


def intake(core, slots, run_rows, mine_rows, other_rows, weights, biases):
    half, features = mine_rows.shape
    rows = 2 * half
    width = weights[0].shape[1]
    count = 256
    blocks = rows // count

    def tile(n):
        return pl.BlockSpec((count, n), lambda i, core: (i, 0))

    return pl.pallas_call(
        functools.partial(intake_kernel, run_rows),
        grid_spec=pltpu.PrefetchScalarGridSpec(
            num_scalar_prefetch=1,
            grid=(blocks,),
            in_specs=[
                pl.BlockSpec(
                    (1, count), lambda i, core: (0, (i + core[0] * (blocks // 2)) % blocks)
                ),
                whole((half, features)),
                whole((half, features)),
            ]
            + [whole((features, width))] * 3
            + [whole((1, width))] * 2,
            out_specs=[tile(features), tile(width), tile(width), tile(width)],
        ),
        out_shape=[jax.ShapeDtypeStruct((rows, features), BF16)]
        + [jax.ShapeDtypeStruct((rows, width), BF16)] * 3,
        cost_estimate=cost(2 * rows * features * (rows + 3 * width), 8 * rows * features),
        compiler_params=params(),
        name="intake",
    )(core, slots, mine_rows, other_rows, *weights, *biases)


def centred(values):
    centre = values - jnp.mean(values, axis=-1, keepdims=True)
    inverse = lax.rsqrt(jnp.mean(centre * centre, axis=-1, keepdims=True) + EPSILON)
    return centre * inverse, inverse


def norm_back(upstream, normed, inverse, gain):
    scaled = upstream * gain
    return inverse * (
        scaled
        - jnp.mean(scaled, axis=-1, keepdims=True)
        - normed * jnp.mean(scaled * normed, axis=-1, keepdims=True)
    )


def add_rows(ref, row, values):
    ref[row : row + 1, :] += jnp.sum(values, axis=0, keepdims=True)


def rows_kernel(
    run_rows, core, x_ref, mixed_mine, mixed_other, slots, cot_mine, cot_other,
    out_bias, first_gain, first_shift, down_bias, second_gain, second_shift, bias_mine, bias_other,
    out_mine, out_other, up_mine, up_other, down_mine, down_other,
    y_ref, hb_ref, second_ref, act_mine, act_other, du_mine, du_other, first_ref, low_ref,
    back_mine, back_other, sums, up_sums,
    w_out, w_up, w_down, sems, hidden, first_inv, total, slope, grad, pulled
):
    half, features = x_ref.shape
    width = mixed_mine.shape[1]
    chunks, _, chunk = w_up.shape
    per_half = chunks // 2
    tiles = half // ROW_TILE
    copies = [
        pltpu.make_async_copy(out_mine, w_out.at[0], sems.at[0]),
        pltpu.make_async_copy(out_other, w_out.at[1], sems.at[1]),
    ]
    up_copies, down_copies = [], []
    for c in range(chunks):
        up, down = ((up_mine, down_mine), (up_other, down_other))[c // per_half]
        at = pl.ds(c % per_half * chunk, chunk)
        up_copies.append(pltpu.make_async_copy(up.at[:, at], w_up.at[c], sems.at[2 + c]))
        down_copies.append(
            pltpu.make_async_copy(down.at[at, :], w_down.at[c], sems.at[2 + chunks + c])
        )
    for copy in copies:
        copy.start()
    for up, down in zip(up_copies, down_copies):
        up.start()
        down.start()
    out_bias, first_gain, first_shift = out_bias[...], first_gain[...], first_shift[...]
    down_bias, second_gain, second_shift = down_bias[...], second_gain[...], second_shift[...]
    sums[...] = jnp.zeros_like(sums)
    up_sums[...] = jnp.zeros_like(up_sums)

    column = columns_of(slots[...], core[0], run_rows, half)
    grad[...] = nn(one_hot(column, half, 0), cot_mine[...])
    grad[...] += nn(one_hot(column, half, half), cot_other[...])

    def of_chunk(refs, c):
        return refs[c // per_half], slice(c % per_half * chunk, (c % per_half + 1) * chunk)

    for copy in copies:
        copy.wait()
    total[...] = nn(mixed_mine[...], w_out[0]) + nn(mixed_other[...], w_out[1])

    @pl.loop(0, tiles)
    def _(i):
        at = pl.ds(pl.multiple_of(i * ROW_TILE, ROW_TILE), ROW_TILE)
        normed, inverse = centred(x_ref[at, :].astype(F32) + total[at, :] + out_bias)
        rows = normed * first_gain + first_shift
        hidden[at, :] = rows
        hb_ref[at, :] = rows.astype(BF16)
        first_ref[at, :] = normed
        first_inv[at, :] = inverse

    block = half // 2
    items = [(c, slice(r * block, (r + 1) * block)) for c in range(chunks) for r in range(2)]
    for n in range(len(items) + 2):
        if n < len(items):
            c, at = items[n]
            if at.start == 0:
                up_copies[c].wait()
            ref, wide = of_chunk((bias_mine, bias_other), c)
            slope[c, at, :] = nn(hb_ref[at, :], w_up[c]) + ref[:, wide]
        if 1 <= n <= len(items):
            c, at = items[n - 1]
            inner = slope[c, at, :]
            share = 0.5 * (1.0 + lax.erf(inner * 0.7071067811865476))
            density = jnp.exp(-0.5 * inner * inner) * 0.3989422804014327
            ref, wide = of_chunk((act_mine, act_other), c)
            ref[at, wide] = (inner * share).astype(BF16)
            slope[c, at, :] = share + inner * density
        if n >= 2:
            c, at = items[n - 2]
            if at.start == 0:
                down_copies[c].wait()
            ref, wide = of_chunk((act_mine, act_other), c)
            part = nn(ref[at, wide], w_down[c])
            total[at, :] = part if c == 0 else total[at, :] + part

    @pl.loop(0, tiles)
    def _(i):
        at = pl.ds(pl.multiple_of(i * ROW_TILE, ROW_TILE), ROW_TILE)
        normed, inverse = centred(hidden[at, :] + total[at, :] + down_bias)
        y_ref[at, :] = (normed * second_gain + second_shift).astype(BF16)
        upstream = grad[at, :]
        add_rows(sums, 4, upstream * normed)
        add_rows(sums, 5, upstream)
        back = norm_back(upstream, normed, inverse, second_gain)
        add_rows(sums, 3, back)
        second_ref[at, :] = back.astype(BF16)
        grad[at, :] = back

    for n in range(len(items) + 2):
        if n < len(items):
            c, at = items[n]
            pulled[n % 2] = nt(second_ref[at, :], w_down[c])
        if 1 <= n <= len(items):
            c, at = items[n - 1]
            back = (pulled[(n - 1) % 2] * slope[c, at, :]).astype(BF16)
            ref, wide = of_chunk((du_mine, du_other), c)
            ref[at, wide] = back
            row = (c // per_half ^ core[0]) * per_half + c % per_half
            up_sums[pl.ds(row, 1), :] += jnp.sum(back.astype(F32), axis=0, keepdims=True)
        if n >= 2:
            c, at = items[n - 2]
            ref, wide = of_chunk((du_mine, du_other), c)
            grad[at, :] += nt(ref[at, wide], w_up[c])

    @pl.loop(0, tiles)
    def _(i):
        at = pl.ds(pl.multiple_of(i * ROW_TILE, ROW_TILE), ROW_TILE)
        upstream, normed = grad[at, :], first_ref[at, :]
        add_rows(sums, 1, upstream * normed)
        add_rows(sums, 2, upstream)
        back = norm_back(upstream, normed, first_inv[at, :], first_gain)
        add_rows(sums, 0, back)
        first_ref[at, :] = back

    low = first_ref[...].astype(BF16)
    low_ref[...] = low
    back_mine[...] = nt(low, w_out[0]).astype(BF16)
    back_other[...] = nt(low, w_out[1]).astype(BF16)


def row_pass(
    core, inputs, mixed, mixed_other, slots, run_rows, cot_mine, cot_other, vectors,
    out_mine, out_other, up_mine, up_other, down_mine, down_other
):
    half, features = cot_mine.shape
    width = mixed.shape[1]
    chunk = features
    chunks = 2 * up_mine.shape[1] // chunk
    any_space = pl.BlockSpec(memory_space=pl.ANY)

    def low(*shape):
        return jax.ShapeDtypeStruct(shape, BF16)

    outs = [
        low(half, features),
        low(half, features),
        low(half, features),
        low(half, up_mine.shape[1]),
        low(half, up_mine.shape[1]),
        low(half, up_mine.shape[1]),
        low(half, up_mine.shape[1]),
        jax.ShapeDtypeStruct((half, features), F32),
        low(half, features),
        low(half, width),
        low(half, width),
        jax.ShapeDtypeStruct((8, features), F32),
        jax.ShapeDtypeStruct((chunks, chunk), F32),
    ]
    return pl.pallas_call(
        functools.partial(rows_kernel, run_rows),
        grid_spec=pltpu.PrefetchScalarGridSpec(
            num_scalar_prefetch=1,
            grid=(1,),
            in_specs=[
                whole((half, features)),
                whole((half, width)),
                whole((half, width)),
                pl.BlockSpec((1, half), lambda i, core: (0, core[0])),
                whole((half, features)),
                whole((half, features)),
            ]
            + [whole(v.shape) for v in vectors]
            + [any_space] * 6,
            out_specs=[whole(o.shape) for o in outs],
            scratch_shapes=[
                pltpu.VMEM((2, width, features), BF16),
                pltpu.VMEM((chunks, features, chunk), BF16),
                pltpu.VMEM((chunks, chunk, features), BF16),
                pltpu.SemaphoreType.DMA((2 + 2 * chunks,)),
                pltpu.VMEM((half, features), F32),
                pltpu.VMEM((half, 1), F32),
                pltpu.VMEM((half, features), F32),
                pltpu.VMEM((chunks, half, chunk), F32),
                pltpu.VMEM((half, features), F32),
                pltpu.VMEM((2, half // 2, chunk), F32),
            ],
        ),
        out_shape=outs,
        cost_estimate=cost(
            8 * half * features * chunk * chunks + 10 * half * features * features,
            30 * half * features + 8 * features * chunk * chunks,
            half * chunk * chunks,
        ),
        compiler_params=params(),
        name="row_pass",
    )(
        core, inputs, mixed, mixed_other, slots, cot_mine, cot_other, *vectors,
        out_mine, out_other, up_mine, up_other, down_mine, down_other
    )


def after(values, others):
    return lax.optimization_barrier((values, others))[0]


def near_groups(groups):
    near = 4 if groups % 4 == 0 else 1
    return near, groups // near


def tn(left, right):
    return lax.dot_general(left, right, (((0,), (0,)), ((), ())), preferred_element_type=F32)


def by_place(terms, groups):
    near, far = near_groups(groups)
    place = lax.axis_index("dp") % near
    terms = terms.reshape(far, near, terms.shape[0] // groups, terms.shape[1])
    return [lax.dynamic_index_in_dim(terms, place ^ n, 1, keepdims=False) for n in range(near)]


def pairs(groups, distance):
    return [(i, i ^ distance) for i in range(groups)]


def far_halves(total, groups, bit):
    total = total.reshape(-1, 2, *total.shape[1:])
    side = (lax.axis_index("dp") // near_groups(groups)[0] >> bit) & 1
    kept = lax.dynamic_index_in_dim(total, side, 1, keepdims=False)
    return kept, lax.dynamic_index_in_dim(total, 1 - side, 1, keepdims=False).astype(BF16)


def far_rest(halves, groups, bit, first_wait=None):
    near, far = near_groups(groups)
    while True:
        kept, sent = halves
        got = lax.ppermute(sent, "dp", pairs(groups, near << bit))
        if first_wait is not None:
            got, first_wait = after(got, first_wait), None
        total = kept.astype(F32) + got.astype(F32)
        bit += 1
        if 1 << bit >= far:
            return total[0]
        halves = far_halves(total, groups, bit)


def near_sends(terms, groups):
    return [lax.ppermute(t, "dp", pairs(groups, n + 1)) for n, t in enumerate(terms)]


def sum_of(kept, got):
    for term in got:
        kept = kept + term.astype(F32)
    return kept


def input_kernel(first_ref, mine_ref, other_ref, *refs):
    weights, out_ref = refs[:-1], refs[-1]
    total = first_ref[...]
    width = weights[0].shape[1]
    for n, weight in enumerate(weights):
        rows = (mine_ref, other_ref)[n // 3]
        total = total + nt(rows[:, n % 3 * width : (n % 3 + 1) * width], weight[...])
    out_ref[...] = total.astype(BF16)


def input_rows(first_grad, mine_rows, other_rows, weights):
    half, features = first_grad.shape
    wide = other_rows.shape[1]
    count = 256

    def tile(n):
        return pl.BlockSpec((count, n), lambda i: (i, 0))

    return pl.pallas_call(
        input_kernel,
        grid=(half // count,),
        in_specs=[tile(features), tile(wide), tile(wide)] + [whole(w.shape) for w in weights],
        out_specs=tile(features),
        out_shape=jax.ShapeDtypeStruct((half, features), BF16),
        cost_estimate=cost(4 * half * features * wide, 8 * half * features + 4 * features * wide),
        compiler_params=params(),
        name="input_rows",
    )(first_grad, mine_rows, other_rows, *weights)


def route_kernel(share, has_extra, core, slots_mine, slots_other, mine_ref, other_ref, *refs):
    out_ref = refs[-1]
    groups, run = out_ref.shape[0], mine_ref.shape[0] // out_ref.shape[0]
    half = mine_ref.shape[0]
    row = lax.broadcasted_iota(jnp.int32, (half, half), 0)
    column_mine = columns_of(slots_mine[...], core[0], 2 * run, half)
    column_other = columns_of(slots_other[...], core[0], 2 * run, half)
    put_mine = (column_mine == row).astype(F32).astype(BF16)
    put_other = (column_other == row).astype(F32).astype(BF16)
    rows = (nn(put_mine, mine_ref[...]) + nn(put_other, other_ref[...])).astype(BF16)
    out_ref[:, :run, :] = rows.reshape(groups, run, rows.shape[1])
    if has_extra:
        sums, up_sums, qv_sums, wide, wide_up = refs[:5]
        features = sums.shape[1]
        width = qv_sums.shape[1]
        wide[...] = jnp.zeros_like(wide)
        wide_up[...] = jnp.zeros_like(wide_up)
        wide[:, :features] = sums[...]
        wide_up[:4, :features] = up_sums[...]
        at = pl.ds(pl.multiple_of(core[0] * width, LANES), width)
        wide[6:8, at] = qv_sums[:2, :]
        for g in range(groups):
            block = wide[:, share * g : share * g + LANES]
            start = 4 * share * g
            blocks = [block]
            parts = []
            for r in range(4):
                line = (start + share * r) // features
                lane = (start + share * r) % features
                parts.append(wide_up[line : line + 1, lane : lane + LANES])
            blocks.append(jnp.concatenate(parts + [jnp.zeros((4, LANES), F32)], axis=0))
            for b, rest in enumerate(blocks):
                for piece in range(3):
                    term = rest.astype(BF16)
                    rest = rest - term.astype(F32)
                    q = 2 * piece + b
                    out_ref[g, run : run + 8, q * LANES : (q + 1) * LANES] = term


def route(core, slots, mine_rows, other_rows, groups, extra=None):
    half, features = mine_rows.shape
    run = half // groups
    share = features // groups
    extra = extra or ()
    args = [core, slots, slots, mine_rows, other_rows, *extra]
    in_specs = [
        pl.BlockSpec((1, half), lambda i, core: (0, core[0])),
        pl.BlockSpec((1, half), lambda i, core: (0, 1 - core[0])),
    ] + [whole(a.shape) for a in args[3:]]
    scratch = [pltpu.VMEM((8, features + LANES), F32)] * 2 if extra else []
    shape = (groups, run + (8 if extra else 0), features)

    def kernel(*refs):
        ins, (out_ref, *more) = refs[: len(args)], refs[len(args) :]
        route_kernel(share, len(extra) > 0, *ins, *more, out_ref)

    return pl.pallas_call(
        kernel,
        grid_spec=pltpu.PrefetchScalarGridSpec(
            num_scalar_prefetch=1,
            grid=(1,),
            in_specs=in_specs,
            out_specs=whole(shape),
            scratch_shapes=scratch,
        ),
        out_shape=jax.ShapeDtypeStruct(shape, BF16),
        cost_estimate=cost(4 * half * half * features, 6 * half * features),
        compiler_params=params(),
        name="route",
    )(*args)


def exchange(values):
    return lax.all_to_all(values, "dp", split_axis=0, concat_axis=0, tiled=True)


def unpack_kernel(core, mine_ref, other_ref, *outs):
    share = outs[0].shape[1] * 2
    total = mine_ref[...] + other_ref[...]
    each = share // 2
    low = core[0] == 0

    def half_of(values):
        return jnp.where(low, values[:, :each], values[:, each:share])

    order = (6, 7, 0, 1, 2, 3, 4, 5)
    for out, row in zip(outs[:8], order):
        out[...] = half_of(total[row : row + 1, :])
    pair = jnp.where(low, total[8:10, :share], total[10:12, :share])
    outs[8][:, :share] = pair[0:1, :]
    outs[8][:, share:] = pair[1:2, :]


def unpack(core, extra, groups):
    extra = jnp.sum(extra.astype(F32), axis=0)
    pieces = [
        jnp.concatenate([extra[:, 2 * p * LANES : (2 * p + 1) * LANES],
                         extra[:, (2 * p + 1) * LANES : (2 * p + 2) * LANES]], axis=0)
        for p in range(3)
    ]
    total = pieces[2] + pieces[1] + pieces[0]
    features = extra.shape[1]
    each = features // groups // 2
    outs = [jax.ShapeDtypeStruct((1, each), F32)] * 8 + [
        jax.ShapeDtypeStruct((1, 4 * each), F32)
    ]
    made = pl.pallas_call(
        unpack_kernel,
        in_specs=[
            pl.BlockSpec(memory_space=pltpu.SMEM),
            pl.BlockSpec(memory_space=pltpu.VMEM),
            pl.BlockSpec(memory_space=pltpu.VMEM),
        ],
        out_shape=outs,
        name="unpack",
    )(core, total, swap(total))
    return [m.reshape(-1) for m in made]


def local(
    tokens,
    token_slot,
    seq_lengths,
    query_weight,
    query_bias,
    key_weight,
    value_weight,
    value_bias,
    out_weight,
    out_bias,
    first_gain,
    first_shift,
    up_weight,
    up_bias,
    down_weight,
    down_bias,
    second_gain,
    second_shift,
    cotangent,
):
    groups = lax.axis_size("dp")
    row_count, features = tokens.shape
    run_rows = row_count // groups
    half_run = run_rows // 2
    half = row_count // 2
    mine = lax.axis_index("tensor")
    core = mine.reshape(1)
    near, far = near_groups(groups)

    def deal(values):
        part = lax.dynamic_slice_in_dim(
            values.reshape(groups, run_rows, features), mine * half_run, half_run, 1
        )
        return exchange(part).reshape(half, features)

    token_rows = deal(tokens)
    cot_raw = deal(cotangent)

    qkv_weights = [query_weight, key_weight, value_weight]
    out_other, up_other, down_other = swap(out_weight), swap(up_weight), swap(down_weight)
    vectors = [out_bias, first_gain, first_shift, down_bias, second_gain, second_shift]
    vectors = [v.reshape(1, -1) for v in vectors + [up_bias, swap(up_bias)]]

    inputs, query_rows, key_rows, value_rows = intake(
        core, token_slot, run_rows, token_rows, swap(token_rows), qkv_weights,
        (query_bias.reshape(1, -1), value_bias.reshape(1, -1)),
    )
    mixed, logsum = attention_forward(seq_lengths, core, query_rows, key_rows, value_rows)
    cot_rows = after(cot_raw, mixed)
    mixed_other = swap(mixed[half:])
    (
        output_low, hidden_low, second_low, act_mine, act_other, inner_mine, inner_other, first_grad,
        first_low, mixed_grad_mine, mixed_grad_other, sums, up_sums,
    ) = row_pass(
        core, inputs, mixed, mixed_other, token_slot, run_rows, cot_rows, swap(cot_rows), vectors,
        out_weight, out_other, up_weight, up_other, down_weight, down_other,
    )
    mixed_grad_got = swap(mixed_grad_other)

    def weave(part):
        other = swap(part)
        low = jnp.where(mine == 0, part, other)
        high = jnp.where(mine == 0, other, part)
        return jnp.concatenate([low, high], axis=1).reshape(row_count, features)

    width = query_weight.shape[1]
    ff_width = up_weight.shape[1]
    second_got, act_got = swap(second_low), swap(act_other)
    hidden_got, inner_got = swap(hidden_low), swap(inner_other)
    first_got, mixed_got = swap(first_low), mixed[half:]
    returned = route(core, token_slot, output_low, swap(output_low), groups)
    down_terms = by_place(tn(second_low, act_mine) + tn(second_got, act_got), groups)
    up_terms = by_place(tn(hidden_low, inner_mine) + tn(hidden_got, inner_got), groups)
    out_terms = by_place(tn(first_low, mixed[:half]) + tn(first_got, mixed_got), groups)
    left_terms = down_terms
    right_terms = [jnp.concatenate(t, axis=2) for t in zip(up_terms, out_terms)]
    if near == 4:
        kept = [
            jnp.stack([left_terms[0], left_terms[2]]),
            jnp.stack([right_terms[0], right_terms[1]]),
        ]
        sent = [
            jnp.stack([left_terms[1], left_terms[3]]).astype(BF16),
            jnp.stack([right_terms[2], right_terms[3]]).astype(BF16),
        ]
    else:
        kept, sent = [left_terms[0][None], right_terms[0][None]], []
    mixed_grad_mine, mixed_grad_got = after(
        (mixed_grad_mine, mixed_grad_got), (returned, kept, sent)
    )
    returned = exchange(returned)
    got = [lax.ppermute(v, "dp", pairs(groups, n + 1)) for n, v in enumerate(sent)]
    qkv_grad, qv_sums = attention_backward(
        seq_lengths, core, query_rows, key_rows, value_rows, mixed, logsum,
        mixed_grad_mine, mixed_grad_got,
    )
    other_grad = swap(qkv_grad[half:])
    qkv_terms = by_place(tn(inputs, qkv_grad), groups)
    qkv_terms = qkv_terms[:1] + [t.astype(BF16) for t in qkv_terms[1:]]
    got, returned = after((got, returned), qkv_terms)
    sent = [(k[1] + g[1].astype(F32)).astype(BF16) for k, g in zip(kept, got)]
    kept = [k[0] + g[0].astype(F32) for k, g in zip(kept, got)] if got else [k[0] for k in kept]
    first_grad = after(first_grad, (qkv_terms, sent, kept))
    qkv_got = near_sends(qkv_terms[1:], groups)
    got = [lax.ppermute(v, "dp", pairs(groups, 2 - n)) for n, v in enumerate(sent)]
    input_low = input_rows(
        first_grad, qkv_grad, other_grad, qkv_weights + [swap(w) for w in qkv_weights]
    )
    got = after(got, input_low)
    if got:
        kept = [k + g.astype(F32) for k, g in zip(kept, got)]
    ffn_terms = far_halves(jnp.concatenate(kept, axis=2), groups, 0)
    input_low = after(input_low, ffn_terms)
    given = route(core, token_slot, input_low, swap(input_low), groups, (sums, up_sums, qv_sums))
    ffn_sum = far_rest(ffn_terms, groups, 0, given)
    qkv_got = after(qkv_got, given)
    qkv_sum = far_rest(far_halves(sum_of(qkv_terms[0], qkv_got), groups, 0), groups, 0)
    given = exchange(given)
    layer_out = weave(returned)
    input_gradient = weave(given[:, :half_run])
    (
        query_bias_sum, value_bias_sum, out_bias_sum, first_gain_sum, first_shift_sum,
        down_bias_sum, second_gain_sum, second_shift_sum, up_bias_sum,
    ) = unpack(core, given[:, half_run:], groups)
    return (
        layer_out,
        input_gradient,
        qkv_sum[:, :width],
        query_bias_sum,
        qkv_sum[:, width : 2 * width],
        qkv_sum[:, 2 * width :],
        value_bias_sum,
        ffn_sum[:, 2 * ff_width :].T,
        out_bias_sum,
        first_gain_sum,
        first_shift_sum,
        ffn_sum[:, ff_width : 2 * ff_width],
        up_bias_sum,
        ffn_sum[:, :ff_width].T,
        down_bias_sum,
        second_gain_sum,
        second_shift_sum,
    )


def solution(mesh):
    rows = P("dp", None)
    in_specs = (
        rows,
        rows,
        rows,
        P(None, "tensor"),
        P("tensor"),
        P(None, "tensor"),
        P(None, "tensor"),
        P("tensor"),
        P("tensor", None),
        P(),
        P(),
        P(),
        P(None, "tensor"),
        P("tensor"),
        P("tensor", None),
        P(),
        P(),
        P(),
        rows,
    )
    spread = P(("dp", "tensor"))
    out_specs = (
        rows,
        rows,
        P("dp", "tensor"),
        spread,
        P("dp", "tensor"),
        P("dp", "tensor"),
        spread,
        P("tensor", "dp"),
        spread,
        spread,
        spread,
        P("dp", "tensor"),
        spread,
        P("tensor", "dp"),
        spread,
        spread,
        spread,
    )
    return jax.shard_map(local, mesh=mesh, in_specs=in_specs, out_specs=out_specs, check_vma=False)
```

```python
import functools
import jax
import jax.numpy as jnp
from jax import lax
from jax.experimental import pallas as pl
from jax.experimental.pallas import tpu as pltpu
from jax.sharding import PartitionSpec as P

HD = 64
LANES = 128
SEG_MAX = 8
FORWARD_ROWS = 512
FORWARD_KEYS = 512
QB = 256
KB = 256
ROW_TILE = 64


EPSILON = 1e-12
MASKED = -1e30
F32 = jnp.float32
BF16 = jnp.bfloat16
SWAP = [(0, 1), (1, 0)]
VMEM_LIMIT = 60 << 20


def swap(values):
    return lax.ppermute(values, "tensor", SWAP)


def nt(a, b):
    return lax.dot_general(a, b, (((1,), (1,)), ((), ())), preferred_element_type=F32)


def nn(a, b):
    return jnp.dot(a, b, preferred_element_type=F32)


def segment_ends(lengths):
    ends, end = [], jnp.int32(0)
    for n in range(lengths.shape[1]):
        end = end + lengths[0, n]
        ends.append(end)
    return ends


def bounds(ends, rows, first, last):
    low, high = jnp.int32(0), jnp.int32(rows)
    for end in ends:
        low = jnp.where(end <= first, jnp.maximum(low, end), low)
        high = jnp.where(end > last, jnp.minimum(high, end), high)
    return low, high


def lane_bounds(ends, rows):
    lane = lax.broadcasted_iota(jnp.int32, (1, LANES), 1)
    start = jnp.full((1, LANES), 2 * rows, jnp.int32)
    stop = jnp.zeros((1, LANES), jnp.int32)
    begin = 0
    for n, end in enumerate(ends):
        start = jnp.where(lane == n, begin, start)
        stop = jnp.where(lane == n, end, stop)
        begin = end
    return start, stop


def key_marks(ends, rows, offset):
    start, stop = lane_bounds(ends, rows)
    pos = lax.broadcasted_iota(jnp.int32, (rows, LANES), 0) + offset
    pos = jnp.where(pos >= rows, pos - rows, pos)
    return ((pos >= start) & (pos < stop)).astype(F32).astype(BF16)


def query_marks(ends, rows, first, count):
    start, stop = lane_bounds(ends, rows)
    lane = lax.broadcasted_iota(jnp.int32, (1, LANES), 1)
    pos = lax.broadcasted_iota(jnp.int32, (count, LANES), 0) + first
    return jnp.where((lane < len(ends)) & ((pos < start) | (pos >= stop)), MASKED, 0.0)


def lane_mask(half):
    lane = lax.broadcasted_iota(jnp.int32, (1, LANES), 1)
    return ((lane // HD) == half).astype(F32).astype(BF16)


def of_pair(h):
    return slice(h // 2 * LANES, (h // 2 + 1) * LANES)


def forward_kernel(
    lengths, core, q_ref, k_ref, v_ref, o_mine, o_other, lse_ref, keys, values_t, mixed, peaks, totals
):
    rows, width = k_ref.shape
    heads = width // HD
    step = pl.program_id(0)
    ends = segment_ends(lengths)
    offset = core[0] * (rows // 2)

    @pl.when(step == 0)
    def _():
        marks = key_marks(ends, rows, offset)
        for p in range(heads // 2):
            keys[p, :, :LANES] = k_ref[:, of_pair(2 * p)]
            keys[p, :, LANES:] = marks
        for block in range(rows // FORWARD_KEYS):
            at = slice(block * FORWARD_KEYS, (block + 1) * FORWARD_KEYS)
            values_t[block] = v_ref[at, :].astype(F32).T.astype(BF16)

    first = lax.rem(step * FORWARD_ROWS + offset, rows)
    low, high = bounds(ends, rows, first, first + FORWARD_ROWS - 1)
    block_low, block_high = low // FORWARD_KEYS, (high + FORWARD_KEYS - 1) // FORWARD_KEYS
    marked = query_marks(ends, rows, first, FORWARD_ROWS).astype(BF16)
    queries = []
    for p in range(heads // 2):
        query = q_ref[:, of_pair(2 * p)] * BF16(HD**-0.5)
        both = [jnp.concatenate([query * lane_mask(n), marked], axis=1) for n in range(2)]
        queries.append(jnp.concatenate(both, axis=0))
    mixed[...] = jnp.zeros_like(mixed)
    peaks[...] = jnp.full_like(peaks, MASKED)
    totals[...] = jnp.zeros_like(totals)

    def block_step(i, carry):
        start = lax.rem(i * FORWARD_KEYS + rows - offset, rows)
        at = pl.ds(pl.multiple_of(start, FORWARD_KEYS), FORWARD_KEYS)
        block = start // FORWARD_KEYS
        made = [nt(keys[p, at, :], queries[p]) for p in range(heads // 2)]
        for p in range(heads // 2):
            scores = made[p]
            row = slice(p, p + 1)
            peak = jnp.maximum(peaks[row, :], jnp.max(scores, axis=0, keepdims=True))
            shrink = jnp.exp(peaks[row, :] - peak)
            weights = jnp.exp(scores - peak)
            peaks[row, :] = peak
            totals[row, :] = totals[row, :] * shrink + jnp.sum(weights, axis=0, keepdims=True)
            part = nn(values_t[block, of_pair(2 * p), :], weights.astype(BF16))
            for n in range(2):
                h = slice((2 * p + n) * HD, (2 * p + n + 1) * HD)
                q = slice(n * FORWARD_ROWS, (n + 1) * FORWARD_ROWS)
                mixed[h, :] = mixed[h, :] * shrink[:, q] + part[n * HD : (n + 1) * HD, q]
        return carry

    lax.fori_loop(block_low, block_high, block_step, 0)
    inverse = 1.0 / totals[...]
    lse = peaks[...] + jnp.log(totals[...])
    for h in range(heads):
        wide = slice(h * HD, (h + 1) * HD)
        p, q = h // 2, slice(h % 2 * FORWARD_ROWS, (h % 2 + 1) * FORWARD_ROWS)
        mixed[wide, :] = mixed[wide, :] * inverse[p : p + 1, q]
        lse_ref[h : h + 1, :] = lse[p : p + 1, q]
    made = mixed[...].T.astype(BF16)
    half = rows // 2
    for n in range(rows // FORWARD_ROWS):
        start = n * FORWARD_ROWS % half

        @pl.when(step == n)
        def _():
            ref = (o_mine, o_other)[n * FORWARD_ROWS // half]
            ref[start : start + FORWARD_ROWS, :] = made


def whole(shape):
    return pl.BlockSpec(shape, lambda *_: (0,) * len(shape))


def attention_forward(lengths, core, query_rows, key_rows, value_rows):
    rows, width = query_rows.shape
    heads = width // HD
    tile = pl.BlockSpec((FORWARD_ROWS, width), lambda i, *_: (i, 0))
    return pl.pallas_call(
        forward_kernel,
        grid_spec=pltpu.PrefetchScalarGridSpec(
            num_scalar_prefetch=2,
            grid=(rows // FORWARD_ROWS,),
            in_specs=[tile, whole((rows, width)), whole((rows, width))],
            out_specs=[whole((rows // 2, width))] * 2
            + [pl.BlockSpec((8, FORWARD_ROWS), lambda i, *_: (0, i))],
            scratch_shapes=[
                pltpu.VMEM((heads // 2, rows, 2 * LANES), BF16),
                pltpu.VMEM((rows // FORWARD_KEYS, width, FORWARD_KEYS), BF16),
                pltpu.VMEM((width, FORWARD_ROWS), F32),
                pltpu.VMEM((8, 2 * FORWARD_ROWS), F32),
                pltpu.VMEM((8, 2 * FORWARD_ROWS), F32),
            ],
        ),
        out_shape=[jax.ShapeDtypeStruct((rows // 2, width), BF16)] * 2
        + [jax.ShapeDtypeStruct((8, rows), F32)],
        cost_estimate=pl.CostEstimate(
            flops=8 * rows * rows * LANES * heads,
            bytes_accessed=8 * rows * width,
            transcendentals=rows * rows * heads // 2,
        ),
        compiler_params=params(),
        name="attend",
    )(lengths, core, query_rows, key_rows, value_rows)


def backward_kernel(
    lengths, core, q_ref, do_mine, do_other, o_mine, o_other, lse_ref, k_ref, v_ref,
    grad_mine, grad_other, sums_ref, keys, values, keys_t, dk_sum, dv_sum, dq_sum
):
    rows, width = k_ref.shape
    heads = width // HD
    step = pl.program_id(0)
    steps = rows // QB
    ends = segment_ends(lengths)
    offset = core[0] * (rows // 2)
    scale = HD**-0.5

    @pl.when(step == 0)
    def _():
        marks = key_marks(ends, rows, offset)
        for p in range(heads // 2):
            keys[p, :, :LANES] = k_ref[:, of_pair(2 * p)]
            keys[p, :, LANES:] = marks
            values[p] = v_ref[:, of_pair(2 * p)]
        for block in range(rows // KB):
            at = slice(block * KB, (block + 1) * KB)
            keys_t[block] = k_ref[at, :].astype(F32).T.astype(BF16)
        dk_sum[...] = jnp.zeros_like(dk_sum)
        dv_sum[...] = jnp.zeros_like(dv_sum)

    first = lax.rem(step * QB + offset, rows)
    low, high = bounds(ends, rows, first, first + QB - 1)
    block_low, block_high = low // KB, (high + KB - 1) // KB
    marked = query_marks(ends, rows, first, QB).astype(BF16)
    early = jnp.full((1, width), step, jnp.int32) < steps // 2
    use_mine = early.astype(F32).astype(BF16)
    use_other = (~early).astype(F32).astype(BF16)
    grad_rows = do_mine[...] * use_mine + do_other[...] * use_other
    mixed_rows = o_mine[...] * use_mine + o_other[...] * use_other
    lane = lax.broadcasted_iota(jnp.int32, (8, LANES), 1)
    row = lax.broadcasted_iota(jnp.int32, (8, LANES), 0)
    by_head = (lane // HD == row).astype(F32).astype(BF16)
    queries, grads, marked_queries, logsums, centres = [], [], [], [], []
    for p in range(heads // 2):
        pair = of_pair(2 * p)
        query = [q_ref[:, pair] * (lane_mask(n) * BF16(scale)) for n in range(2)]
        grad = grad_rows[:, pair]
        exact = grad.astype(F32) * mixed_rows[:, pair].astype(F32)
        high_term = exact.astype(BF16)
        low_term = (exact - high_term.astype(F32)).astype(BF16)
        centre = nt(by_head, high_term) + nt(by_head, low_term)
        centres.append(jnp.concatenate([centre[0:1, :], centre[1:2, :]], axis=1))
        logsums.append(
            jnp.concatenate([lse_ref[2 * p : 2 * p + 1, :], lse_ref[2 * p + 1 : 2 * p + 2, :]], axis=1)
        )
        queries.append(jnp.concatenate(query, axis=0))
        grads.append(jnp.concatenate([grad * lane_mask(n) for n in range(2)], axis=0))
        marked_queries.append(
            jnp.concatenate([queries[p], jnp.concatenate([marked, marked], axis=0)], axis=1)
        )
    dq_sum[...] = jnp.zeros_like(dq_sum)

    def block_step(i, carry):
        start = lax.rem(i * KB + rows - offset, rows)
        at = pl.ds(pl.multiple_of(start, KB), KB)
        block = start // KB
        scores = [nt(keys[p, at, :], marked_queries[p]) for p in range(heads // 2)]
        pulls = [nt(values[p, at, :], grads[p]) for p in range(heads // 2)]
        for p in range(heads // 2):
            weights = jnp.exp(scores[p] - logsums[p])
            pulled = pulls[p]
            dv_sum[at, of_pair(2 * p)] += nn(weights.astype(BF16), grads[p])
            slopes = (weights * (pulled - centres[p])).astype(BF16)
            dk_sum[at, of_pair(2 * p)] += nn(slopes, queries[p])
            part = nn(keys_t[block, of_pair(2 * p), :], slopes)
            for n in range(2):
                h = slice((2 * p + n) * HD, (2 * p + n + 1) * HD)
                dq_sum[h, :] += part[n * HD : (n + 1) * HD, n * QB : (n + 1) * QB]
        return carry

    lax.fori_loop(block_low, block_high, block_step, 0)
    made = (dq_sum[...] * scale).T.astype(BF16)
    half = rows // 2
    for n in range(steps):
        start = n * QB % half

        @pl.when(step == n)
        def _():
            (grad_mine, grad_other)[n * QB // half][start : start + QB, :width] = made

    total = jnp.sum(made.astype(F32), axis=0, keepdims=True)

    @pl.when(step == 0)
    def _():
        sums_ref[...] = jnp.zeros_like(sums_ref)

    sums_ref[0:1, :] += total

    @pl.when(step == steps - 1)
    def _():
        for n, ref in enumerate((grad_mine, grad_other)):
            at = slice(n * half, (n + 1) * half)
            ref[:, width : 2 * width] = dk_sum[at, :].astype(BF16)
            made = dv_sum[at, :].astype(BF16)
            ref[:, 2 * width :] = made
            sums_ref[1:2, :] += jnp.sum(made.astype(F32), axis=0, keepdims=True)


def attention_backward(
    lengths, core, query_rows, key_rows, value_rows, mixed, lse, grad_mine, grad_other
):
    rows, width = query_rows.shape
    heads = width // HD
    steps = rows // QB
    tile = pl.BlockSpec((QB, width), lambda i, *_: (i, 0))
    full = whole((rows, width))
    early = pl.BlockSpec((QB, width), lambda i, *_: (jnp.minimum(i, steps // 2 - 1), 0))
    late = pl.BlockSpec((QB, width), lambda i, *_: (jnp.maximum(i - steps // 2, 0), 0))
    outs = [jax.ShapeDtypeStruct((rows // 2, 3 * width), BF16)] * 2
    outs.append(jax.ShapeDtypeStruct((8, width), F32))
    return pl.pallas_call(
        backward_kernel,
        grid_spec=pltpu.PrefetchScalarGridSpec(
            num_scalar_prefetch=2,
            grid=(steps,),
            in_specs=[
                tile,
                early,
                late,
                early,
                late,
                pl.BlockSpec((8, QB), lambda i, *_: (0, i)),
                full,
                full,
            ],
            out_specs=[whole(o.shape) for o in outs],
            scratch_shapes=[
                pltpu.VMEM((heads // 2, rows, 2 * LANES), BF16),
                pltpu.VMEM((heads // 2, rows, LANES), BF16),
                pltpu.VMEM((rows // KB, width, KB), BF16),
                pltpu.VMEM((rows, width), F32),
                pltpu.VMEM((rows, width), F32),
                pltpu.VMEM((width, QB), F32),
            ],
        ),
        out_shape=outs,
        cost_estimate=pl.CostEstimate(
            flops=20 * rows * rows * LANES * heads,
            bytes_accessed=16 * rows * width,
            transcendentals=rows * rows * heads // 2,
        ),
        compiler_params=params(),
        name="attend_back",
    )(lengths, core, query_rows, grad_mine, grad_other, *mixed, lse, key_rows, value_rows)


def params():
    return pltpu.CompilerParams(vmem_limit_bytes=VMEM_LIMIT)


def cost(flops, moved, transcendentals=0):
    return pl.CostEstimate(flops=flops, bytes_accessed=moved, transcendentals=transcendentals)


def columns_of(slots, core, run_rows, half):
    half_run = run_rows // 2
    run, place = slots // run_rows, slots % run_rows
    held = (place // half_run + core) % 2
    return held * half + run * half_run + place % half_run


def one_hot(column, width, base):
    count = column.shape[1]
    down = jnp.broadcast_to(column, (8, count)).T[:, :1]
    lane = lax.broadcasted_iota(jnp.int32, (count, width), 1) + base
    return (down == lane).astype(F32).astype(BF16)


def intake_kernel(
    run_rows, core, slots, mine_ref, other_ref, q_weight, k_weight, v_weight, q_bias, v_bias,
    x_ref, q_ref, k_ref, v_ref
):
    half = mine_ref.shape[0]
    column = columns_of(slots[...], core[0], run_rows, half)
    rows = nn(one_hot(column, half, 0), mine_ref[...])
    rows = (rows + nn(one_hot(column, half, half), other_ref[...])).astype(BF16)
    x_ref[...] = rows
    q_ref[...] = (nn(rows, q_weight[...]) + q_bias[...]).astype(BF16)
    k_ref[...] = nn(rows, k_weight[...]).astype(BF16)
    v_ref[...] = (nn(rows, v_weight[...]) + v_bias[...]).astype(BF16)


def intake(core, slots, run_rows, mine_rows, other_rows, weights, biases):
    half, features = mine_rows.shape
    rows = 2 * half
    width = weights[0].shape[1]
    count = 512
    blocks = rows // count

    def tile(n):
        return pl.BlockSpec((count, n), lambda i, core: (i, 0))

    return pl.pallas_call(
        functools.partial(intake_kernel, run_rows),
        grid_spec=pltpu.PrefetchScalarGridSpec(
            num_scalar_prefetch=1,
            grid=(blocks,),
            in_specs=[
                pl.BlockSpec(
                    (1, count), lambda i, core: (0, (i + core[0] * (blocks // 2)) % blocks)
                ),
                whole((half, features)),
                whole((half, features)),
            ]
            + [whole((features, width))] * 3
            + [whole((1, width))] * 2,
            out_specs=[tile(features), tile(width), tile(width), tile(width)],
        ),
        out_shape=[jax.ShapeDtypeStruct((rows, features), BF16)]
        + [jax.ShapeDtypeStruct((rows, width), BF16)] * 3,
        cost_estimate=cost(2 * rows * features * (rows + 3 * width), 8 * rows * features),
        compiler_params=params(),
        name="intake",
    )(core, slots, mine_rows, other_rows, *weights, *biases)


def centred(values):
    centre = values - jnp.mean(values, axis=-1, keepdims=True)
    inverse = lax.rsqrt(jnp.mean(centre * centre, axis=-1, keepdims=True) + EPSILON)
    return centre * inverse, inverse


def norm_back(upstream, normed, inverse, gain):
    scaled = upstream * gain
    return inverse * (
        scaled
        - jnp.mean(scaled, axis=-1, keepdims=True)
        - normed * jnp.mean(scaled * normed, axis=-1, keepdims=True)
    )


def add_rows(ref, row, values):
    ref[row : row + 1, :] += jnp.sum(values, axis=0, keepdims=True)


def rows_kernel(
    run_rows, core, x_ref, mixed_mine, mixed_other, slots, cot_mine, cot_other,
    out_bias, first_gain, first_shift, down_bias, second_gain, second_shift, bias_mine, bias_other,
    out_mine, out_other, up_mine, up_other, down_mine, down_other,
    y_out, hb_out, second_out, act_out_mine, act_out_other, du_out_mine, du_out_other, first_out, low_out,
    back_out_mine, back_out_other, sums, up_sums,
    w_out, w_up, w_down, sems, out_sems, hidden, first_inv, total, slope, grad, pulled,
    y_ref, hb_ref, second_ref, act, du, first_ref, low_ref, back
):
    half, features = x_ref.shape
    width = mixed_mine.shape[1]
    chunks, _, chunk = w_up.shape
    per_half = chunks // 2
    tiles = half // ROW_TILE
    copies = [
        pltpu.make_async_copy(out_mine, w_out.at[0], sems.at[0]),
        pltpu.make_async_copy(out_other, w_out.at[1], sems.at[1]),
    ]
    up_copies, down_copies = [], []
    for c in range(chunks):
        up, down = ((up_mine, down_mine), (up_other, down_other))[c // per_half]
        at = pl.ds(c % per_half * chunk, chunk)
        up_copies.append(pltpu.make_async_copy(up.at[:, at], w_up.at[c], sems.at[2 + c]))
        down_copies.append(
            pltpu.make_async_copy(down.at[at, :], w_down.at[c], sems.at[2 + chunks + c])
        )
    outgoing = []

    def send(source, target):
        copy = pltpu.make_async_copy(source, target, out_sems.at[len(outgoing)])
        copy.start()
        outgoing.append(copy)

    for copy in copies:
        copy.start()
    for up, down in zip(up_copies, down_copies):
        up.start()
        down.start()
    out_bias, first_gain, first_shift = out_bias[...], first_gain[...], first_shift[...]
    down_bias, second_gain, second_shift = down_bias[...], second_gain[...], second_shift[...]
    sums[...] = jnp.zeros_like(sums)
    up_sums[...] = jnp.zeros_like(up_sums)

    column = columns_of(slots[...], core[0], run_rows, half)
    grad[...] = nn(one_hot(column, half, 0), cot_mine[...])
    grad[...] += nn(one_hot(column, half, half), cot_other[...])

    def of_chunk(refs, c):
        return refs[c // per_half], pl.ds(c % per_half * chunk, chunk)

    for copy in copies:
        copy.wait()
    total[...] = nn(mixed_mine[...], w_out[0]) + nn(mixed_other[...], w_out[1])

    @pl.loop(0, tiles, unroll=2)
    def _(i):
        at = pl.ds(pl.multiple_of(i * ROW_TILE, ROW_TILE), ROW_TILE)
        normed, inverse = centred(x_ref[at, :].astype(F32) + total[at, :] + out_bias)
        rows = normed * first_gain + first_shift
        hidden[at, :] = rows
        hb_ref[at, :] = rows.astype(BF16)
        first_ref[at, :] = normed
        first_inv[at, :] = inverse

    send(hb_ref, hb_out)

    block = half // 2
    items = [(c, slice(r * block, (r + 1) * block)) for c in range(chunks) for r in range(2)]
    for n in range(len(items) + 2):
        if n < len(items):
            c, at = items[n]
            if at.start == 0:
                up_copies[c].wait()
            ref, wide = of_chunk((bias_mine, bias_other), c)
            slope[c, at, :] = nn(hb_ref[at, :], w_up[c]) + ref[:, wide]
        if 1 <= n <= len(items):
            c, at = items[n - 1]
            inner = slope[c, at, :]
            share = 0.5 * (1.0 + lax.erf(inner * 0.7071067811865476))
            density = jnp.exp(-0.5 * inner * inner) * 0.3989422804014327
            act[c, at, :] = (inner * share).astype(BF16)
            slope[c, at, :] = share + inner * density
            if at.start > 0:
                ref, wide = of_chunk((act_out_mine, act_out_other), c)
                send(act.at[c], ref.at[:, wide])
        if n >= 2:
            c, at = items[n - 2]
            if at.start == 0:
                down_copies[c].wait()
            part = nn(act[c, at, :], w_down[c])
            total[at, :] = part if c == 0 else total[at, :] + part

    @pl.loop(0, tiles, unroll=2)
    def _(i):
        at = pl.ds(pl.multiple_of(i * ROW_TILE, ROW_TILE), ROW_TILE)
        normed, inverse = centred(hidden[at, :] + total[at, :] + down_bias)
        y_ref[at, :] = (normed * second_gain + second_shift).astype(BF16)
        upstream = grad[at, :]
        add_rows(sums, 4, upstream * normed)
        add_rows(sums, 5, upstream)
        back = norm_back(upstream, normed, inverse, second_gain)
        add_rows(sums, 3, back)
        second_ref[at, :] = back.astype(BF16)
        grad[at, :] = back

    send(y_ref, y_out)
    send(second_ref, second_out)
    for n in range(len(items) + 2):
        if n < len(items):
            c, at = items[n]
            pulled[n % 2] = nt(second_ref[at, :], w_down[c])
        if 1 <= n <= len(items):
            c, at = items[n - 1]
            low = (pulled[(n - 1) % 2] * slope[c, at, :]).astype(BF16)
            du[c, at, :] = low
            row = (c // per_half ^ core[0]) * per_half + c % per_half
            up_sums[pl.ds(row, 1), :] += jnp.sum(low.astype(F32), axis=0, keepdims=True)
            if at.start > 0:
                ref, wide = of_chunk((du_out_mine, du_out_other), c)
                send(du.at[c], ref.at[:, wide])
        if n >= 2:
            c, at = items[n - 2]
            grad[at, :] += nt(du[c, at, :], w_up[c])

    @pl.loop(0, tiles, unroll=2)
    def _(i):
        at = pl.ds(pl.multiple_of(i * ROW_TILE, ROW_TILE), ROW_TILE)
        upstream, normed = grad[at, :], first_ref[at, :]
        add_rows(sums, 1, upstream * normed)
        add_rows(sums, 2, upstream)
        back = norm_back(upstream, normed, first_inv[at, :], first_gain)
        add_rows(sums, 0, back)
        first_ref[at, :] = back

    send(first_ref, first_out)
    low_ref[...] = first_ref[...].astype(BF16)
    send(low_ref, low_out)
    for n, out in enumerate((back_out_mine, back_out_other)):
        back[n] = nt(low_ref[...], w_out[n]).astype(BF16)
        send(back.at[n], out)
    for copy in outgoing:
        copy.wait()


def row_pass(
    core, inputs, mixed, mixed_other, slots, run_rows, cot_mine, cot_other, vectors,
    out_mine, out_other, up_mine, up_other, down_mine, down_other
):
    half, features = cot_mine.shape
    width = mixed.shape[1]
    chunk = features
    chunks = 2 * up_mine.shape[1] // chunk
    any_space = pl.BlockSpec(memory_space=pl.ANY)

    def low(*shape):
        return jax.ShapeDtypeStruct(shape, BF16)

    outs = [
        low(half, features),
        low(half, features),
        low(half, features),
        low(half, up_mine.shape[1]),
        low(half, up_mine.shape[1]),
        low(half, up_mine.shape[1]),
        low(half, up_mine.shape[1]),
        jax.ShapeDtypeStruct((half, features), F32),
        low(half, features),
        low(half, width),
        low(half, width),
        jax.ShapeDtypeStruct((8, features), F32),
        jax.ShapeDtypeStruct((chunks, chunk), F32),
    ]
    return pl.pallas_call(
        functools.partial(rows_kernel, run_rows),
        grid_spec=pltpu.PrefetchScalarGridSpec(
            num_scalar_prefetch=1,
            grid=(1,),
            in_specs=[
                whole((half, features)),
                whole((half, width)),
                whole((half, width)),
                pl.BlockSpec((1, half), lambda i, core: (0, core[0])),
                whole((half, features)),
                whole((half, features)),
            ]
            + [whole(v.shape) for v in vectors]
            + [any_space] * 6,
            out_specs=[any_space] * (len(outs) - 2) + [whole(o.shape) for o in outs[-2:]],
            scratch_shapes=[
                pltpu.VMEM((2, width, features), BF16),
                pltpu.VMEM((chunks, features, chunk), BF16),
                pltpu.VMEM((chunks, chunk, features), BF16),
                pltpu.SemaphoreType.DMA((2 + 2 * chunks,)),
                pltpu.SemaphoreType.DMA((7 + 2 * chunks,)),
                pltpu.VMEM((half, features), F32),
                pltpu.VMEM((half, 1), F32),
                pltpu.VMEM((half, features), F32),
                pltpu.VMEM((chunks, half, chunk), F32),
                pltpu.VMEM((half, features), F32),
                pltpu.VMEM((2, half // 2, chunk), F32),
                pltpu.VMEM((half, features), BF16),
                pltpu.VMEM((half, features), BF16),
                pltpu.VMEM((half, features), BF16),
                pltpu.VMEM((chunks, half, chunk), BF16),
                pltpu.VMEM((chunks, half, chunk), BF16),
                pltpu.VMEM((half, features), F32),
                pltpu.VMEM((half, features), BF16),
                pltpu.VMEM((2, half, width), BF16),
            ],
        ),
        out_shape=outs,
        cost_estimate=cost(
            8 * half * features * chunk * chunks + 10 * half * features * features,
            30 * half * features + 8 * features * chunk * chunks,
            half * chunk * chunks,
        ),
        compiler_params=params(),
        name="row_pass",
    )(
        core, inputs, mixed, mixed_other, slots, cot_mine, cot_other, *vectors,
        out_mine, out_other, up_mine, up_other, down_mine, down_other
    )


def after(values, others):
    return lax.optimization_barrier((values, others))[0]


def near_groups(groups):
    near = 4 if groups % 4 == 0 else 1
    return near, groups // near


def tn(left, right):
    return lax.dot_general(left, right, (((0,), (0,)), ((), ())), preferred_element_type=F32)


def by_place(terms, groups):
    near, far = near_groups(groups)
    place = lax.axis_index("dp") % near
    terms = terms.reshape(far, near, terms.shape[0] // groups, terms.shape[1])
    return [lax.dynamic_index_in_dim(terms, place ^ n, 1, keepdims=False) for n in range(near)]


def gradient_kernel(chunks, near, share, halving, me, *refs):
    operands, outs, acc = refs[: 4 * len(chunks)], refs[4 * len(chunks) : -1], refs[-1]
    step = pl.program_id(0)
    first, column = 0, 0
    for n, (chunk, count) in enumerate(chunks):
        left, left_more, right, right_more = operands[4 * n : 4 * n + 4]
        for j in range(count):

            @pl.when(step == first + j)
            def _():
                acc[:, :chunk] = tn(left[...], right[...])
                acc[:, :chunk] += tn(left_more[...], right_more[...])
                at = slice(column + j * chunk, column + (j + 1) * chunk)

                def place(out, place):
                    for f in range(out.shape[0]):
                        row = share * (f * near + (me[0] ^ place))
                        row = pl.ds(pl.multiple_of(row, 16), share)
                        out[f, :, at] = acc[row, :chunk].astype(out.dtype)

                if halving:
                    for out, (a, b) in zip(outs, ((0, 3 - halving), (halving, 3))):
                        place(out.at[0], a)
                        place(out.at[1], b)
                else:
                    for m, out in enumerate(outs):
                        place(out, m)

        first += count
        column += count * chunk


def gradients(pieces, groups, halving=0):
    near, far = near_groups(groups)
    features = pieces[0][0][0].shape[1]
    share = features // groups
    if near != 4 or share % 16 != 0:

        def rows_of(left, rows):
            return lax.slice_in_dim(left[0], left[1] * rows, (left[1] + 1) * rows, axis=0)

        terms = [
            tn(rows_of(p[0], p[2].shape[0]), p[2]) + tn(rows_of(p[1], p[3].shape[0]), p[3])
            for p in pieces
        ]
        made = [t.astype(BF16) for t in by_place(jnp.concatenate(terms, axis=1), groups)]
        if halving:
            made = [
                jnp.stack([made[0], made[3 - halving]]), jnp.stack([made[halving], made[3]])
            ]
        return made
    in_specs, operands, chunks, base, columns = [], [], [], 0, 0
    for left, left_more, right, right_more in pieces:
        rows = right.shape[0]
        chunk = min(features, right.shape[1])
        if right.shape[1] % chunk:
            chunk = right.shape[1] // 3
        count = right.shape[1] // chunk

        def at(j, me, base=base, count=count):
            return 0, jnp.clip(j - base, 0, count - 1)

        for array, block in (left, left_more):
            in_specs.append(
                pl.BlockSpec((rows, features), lambda j, me, block=block: (block, 0))
            )
            operands.append(array)
        in_specs += [pl.BlockSpec((rows, chunk), at)] * 2
        operands += [right, right_more]
        chunks.append((chunk, count))
        base += count
        columns += count * chunk
    if halving:
        outs = [jax.ShapeDtypeStruct((2, far, share, columns), BF16)] * 2
    else:
        outs = [jax.ShapeDtypeStruct((far, share, columns), BF16)] * near
    return pl.pallas_call(
        functools.partial(gradient_kernel, chunks, near, share, halving),
        grid_spec=pltpu.PrefetchScalarGridSpec(
            num_scalar_prefetch=1,
            grid=(base,),
            in_specs=in_specs,
            out_specs=[whole(o.shape) for o in outs],
            scratch_shapes=[pltpu.VMEM((features, features), F32)],
        ),
        out_shape=outs,
        cost_estimate=cost(4 * rows * features * columns, 8 * rows * features + 4 * features * columns),
        compiler_params=params(),
        name="gradients",
    )((lax.axis_index("dp") % near).reshape(1), *operands)


def pairs(groups, distance):
    return [(i, i ^ distance) for i in range(groups)]


def far_halves(total, groups, bit):
    total = total.reshape(-1, 2, *total.shape[1:])
    side = (lax.axis_index("dp") // near_groups(groups)[0] >> bit) & 1
    kept = lax.dynamic_index_in_dim(total, side, 1, keepdims=False)
    return kept, lax.dynamic_index_in_dim(total, 1 - side, 1, keepdims=False).astype(BF16)


def far_step(halves, groups, bit, first=()):
    near, far = near_groups(groups)
    kept, sent = halves
    got = after(lax.ppermute(sent, "dp", pairs(groups, near << bit)), first)
    total = kept.astype(F32) + got.astype(F32)
    return far_halves(total, groups, bit + 1) if 2 << bit < far else total[0]


def far_direct(total, groups, first=()):
    near, far = near_groups(groups)
    run = lax.axis_index("dp") // near
    kept = lax.dynamic_index_in_dim(total, run, 0, keepdims=False)
    got = []
    for step in range(1, far):
        sent = lax.dynamic_index_in_dim(total, run ^ step, 0, keepdims=False).astype(BF16)
        got.append(lax.ppermute(sent, "dp", pairs(groups, step * near)))
    return sum_of(kept, after(got, first))


def near_sends(terms, groups):
    return [lax.ppermute(t, "dp", pairs(groups, n + 1)) for n, t in enumerate(terms)]


def sum_of(kept, got):
    kept = kept.astype(F32)
    for term in got:
        kept = kept + term.astype(F32)
    return kept


def input_kernel(first_ref, mine_ref, other_ref, *refs):
    weights, out_ref = refs[:-1], refs[-1]
    total = first_ref[...]
    for n, rows in enumerate((mine_ref, other_ref)):
        wide = jnp.concatenate([weight[...] for weight in weights[3 * n : 3 * n + 3]], axis=1)
        total = total + nt(rows[...], wide)
    out_ref[...] = total.astype(BF16)


def input_rows(first_grad, mine_rows, other_rows, weights):
    half, features = first_grad.shape
    wide = other_rows.shape[1]
    count = 256

    def tile(n):
        return pl.BlockSpec((count, n), lambda i: (i, 0))

    return pl.pallas_call(
        input_kernel,
        grid=(half // count,),
        in_specs=[tile(features), tile(wide), tile(wide)] + [whole(w.shape) for w in weights],
        out_specs=tile(features),
        out_shape=jax.ShapeDtypeStruct((half, features), BF16),
        cost_estimate=cost(4 * half * features * wide, 8 * half * features + 4 * features * wide),
        compiler_params=params(),
        name="input_rows",
    )(first_grad, mine_rows, other_rows, *weights)


def route_kernel(share, has_extra, core, slots_mine, slots_other, mine_ref, other_ref, *refs):
    out_ref = refs[-1]
    groups, run = out_ref.shape[0], mine_ref.shape[0] // out_ref.shape[0]
    half = mine_ref.shape[0]
    row = lax.broadcasted_iota(jnp.int32, (half, half), 0)
    column_mine = columns_of(slots_mine[...], core[0], 2 * run, half)
    column_other = columns_of(slots_other[...], core[0], 2 * run, half)
    put_mine = (column_mine == row).astype(F32).astype(BF16)
    put_other = (column_other == row).astype(F32).astype(BF16)
    rows = (nn(put_mine, mine_ref[...]) + nn(put_other, other_ref[...])).astype(BF16)
    out_ref[:, :run, :] = rows.reshape(groups, run, rows.shape[1])
    if has_extra:
        sums, up_sums, qv_sums, wide, wide_up = refs[:5]
        features = sums.shape[1]
        width = qv_sums.shape[1]
        wide[...] = jnp.zeros_like(wide)
        wide_up[...] = jnp.zeros_like(wide_up)
        wide[:, :features] = sums[...]
        wide_up[:4, :features] = up_sums[...]
        at = pl.ds(pl.multiple_of(core[0] * width, LANES), width)
        wide[6:8, at] = qv_sums[:2, :]
        for g in range(groups):
            block = wide[:, share * g : share * g + LANES]
            start = 4 * share * g
            blocks = [block]
            parts = []
            for r in range(4):
                line = (start + share * r) // features
                lane = (start + share * r) % features
                parts.append(wide_up[line : line + 1, lane : lane + LANES])
            blocks.append(jnp.concatenate(parts + [jnp.zeros((4, LANES), F32)], axis=0))
            for b, rest in enumerate(blocks):
                for piece in range(3):
                    term = rest.astype(BF16)
                    rest = rest - term.astype(F32)
                    q = 2 * piece + b
                    out_ref[g, run : run + 8, q * LANES : (q + 1) * LANES] = term


def route(core, slots, mine_rows, other_rows, groups, extra=None):
    half, features = mine_rows.shape
    run = half // groups
    share = features // groups
    extra = extra or ()
    args = [core, slots, slots, mine_rows, other_rows, *extra]
    in_specs = [
        pl.BlockSpec((1, half), lambda i, core: (0, core[0])),
        pl.BlockSpec((1, half), lambda i, core: (0, 1 - core[0])),
    ] + [whole(a.shape) for a in args[3:]]
    scratch = [pltpu.VMEM((8, features + LANES), F32)] * 2 if extra else []
    shape = (groups, run + (8 if extra else 0), features)

    def kernel(*refs):
        ins, (out_ref, *more) = refs[: len(args)], refs[len(args) :]
        route_kernel(share, len(extra) > 0, *ins, *more, out_ref)

    return pl.pallas_call(
        kernel,
        grid_spec=pltpu.PrefetchScalarGridSpec(
            num_scalar_prefetch=1,
            grid=(1,),
            in_specs=in_specs,
            out_specs=whole(shape),
            scratch_shapes=scratch,
        ),
        out_shape=jax.ShapeDtypeStruct(shape, BF16),
        cost_estimate=cost(4 * half * half * features, 6 * half * features),
        compiler_params=params(),
        name="route",
    )(*args)


def exchange(values):
    return lax.all_to_all(values, "dp", split_axis=0, concat_axis=0, tiled=True)


def weave_kernel(core, mine_ref, other_ref, out_ref, *outs):
    run = out_ref.shape[2]
    out_ref[:, core[0]] = mine_ref[:, :run, :]
    out_ref[:, 1 - core[0]] = other_ref[:, :run, :]
    if not outs:
        return
    pieces = []
    for q in range(6):
        at = slice(q * LANES, (q + 1) * LANES)
        both = [jnp.sum(r[:, run:, at].astype(F32), axis=0) for r in (mine_ref, other_ref)]
        pieces.append(both[0] + both[1])
    first, more = [pieces[4 + b] + pieces[2 + b] + pieces[b] for b in range(2)]
    each = outs[0].shape[1]
    share = 2 * each
    low = core[0] == 0

    def half_of(values):
        return jnp.where(low, values[:, :each], values[:, each:share])

    for out, row in zip(outs[:8], (6, 7, 0, 1, 2, 3, 4, 5)):
        out[...] = half_of(first[row : row + 1, :])
    pair = jnp.where(low, more[0:2, :share], more[2:4, :share])
    outs[8][:, :share] = pair[0:1, :]
    outs[8][:, share:] = pair[1:2, :]


def weave(core, part, rows_of_core, small=0):
    groups, _, features = part.shape
    outs = [jax.ShapeDtypeStruct((groups, 2, rows_of_core, features), BF16)]
    if small:
        outs += [jax.ShapeDtypeStruct((1, small), F32)] * 8
        outs.append(jax.ShapeDtypeStruct((1, 4 * small), F32))
    rows, *more = pl.pallas_call(
        weave_kernel,
        grid_spec=pltpu.PrefetchScalarGridSpec(
            num_scalar_prefetch=1,
            grid=(1,),
            in_specs=[whole(part.shape)] * 2,
            out_specs=[whole(o.shape) for o in outs],
        ),
        out_shape=outs,
        cost_estimate=cost(1, 1),
        compiler_params=params(),
        name="weave",
    )(core, part, swap(part))
    rows = rows.reshape(groups * 2 * rows_of_core, features)
    return (rows, *[m.reshape(-1) for m in more]) if small else rows


def local(
    tokens,
    token_slot,
    seq_lengths,
    query_weight,
    query_bias,
    key_weight,
    value_weight,
    value_bias,
    out_weight,
    out_bias,
    first_gain,
    first_shift,
    up_weight,
    up_bias,
    down_weight,
    down_bias,
    second_gain,
    second_shift,
    cotangent,
):
    groups = lax.axis_size("dp")
    row_count, features = tokens.shape
    run_rows = row_count // groups
    half_run = run_rows // 2
    half = row_count // 2
    mine = lax.axis_index("tensor")
    core = mine.reshape(1)
    near, far = near_groups(groups)

    def part_of(values):
        return lax.dynamic_slice_in_dim(
            values.reshape(groups, run_rows, features), mine * half_run, half_run, 1
        )

    token_part, cot_part = lax.optimization_barrier((part_of(tokens), part_of(cotangent)))
    token_rows = exchange(token_part).reshape(half, features)
    cot_raw = exchange(cot_part).reshape(half, features)

    qkv_weights = [query_weight, key_weight, value_weight]
    out_other, up_other, down_other = swap(out_weight), swap(up_weight), swap(down_weight)
    vectors = [out_bias, first_gain, first_shift, down_bias, second_gain, second_shift]
    vectors = [v.reshape(1, -1) for v in vectors + [up_bias, swap(up_bias)]]
    qkv_other = [swap(w) for w in qkv_weights]
    token_got = after(swap(token_rows), (out_other, up_other, down_other, qkv_other))

    inputs, query_rows, key_rows, value_rows = intake(
        core, token_slot, run_rows, token_rows, token_got, qkv_weights,
        (query_bias.reshape(1, -1), value_bias.reshape(1, -1)),
    )
    mixed_mine, mixed_theirs, logsum = attention_forward(seq_lengths, core, query_rows, key_rows, value_rows)
    cot_rows = after(cot_raw, mixed_mine)
    mixed_other = swap(mixed_theirs)
    (
        output_low, hidden_low, second_low, act_mine, act_other, inner_mine, inner_other, first_grad,
        first_low, mixed_grad_mine, mixed_grad_other, sums, up_sums,
    ) = row_pass(
        core, inputs, mixed_mine, mixed_other, token_slot, run_rows, cot_rows, swap(cot_rows), vectors,
        out_weight, out_other, up_weight, up_other, down_weight, down_other,
    )
    mixed_grad_got = swap(mixed_grad_other)

    width = query_weight.shape[1]
    ff_width = up_weight.shape[1]
    output_got = swap(output_low)
    second_low, hidden_low, first_low, act_other, inner_other = after(
        (second_low, hidden_low, first_low, act_other, inner_other), output_got
    )
    second_got, act_got = swap(second_low), swap(act_other)
    hidden_got, inner_got = swap(hidden_low), swap(inner_other)
    first_got = swap(first_low)
    returned = route(core, token_slot, output_low, output_got, groups)
    kept, sent = [], []
    left = gradients([((second_low, 0), (second_got, 0), act_mine, act_got)], groups, near == 4)
    right = [
        ((hidden_low, 0), (hidden_got, 0), inner_mine, inner_got),
        ((first_low, 0), (first_got, 0), mixed_mine, mixed_theirs),
    ]
    right = gradients(right, groups, 2 * (near == 4))
    if near == 4:
        kept, sent = [left[0], right[0]], [left[1], right[1]]
    else:
        kept, sent = [left[0][None], right[0][None]], []
    mixed_grad_mine, mixed_grad_got = after(
        (mixed_grad_mine, mixed_grad_got), (returned, kept, sent)
    )
    returned = exchange(returned)
    got = [lax.ppermute(v, "dp", pairs(groups, n + 1)) for n, v in enumerate(sent)]
    qkv_mine, qkv_theirs, qv_sums = attention_backward(
        seq_lengths, core, query_rows, key_rows, value_rows, (mixed_mine, mixed_theirs), logsum,
        mixed_grad_mine, mixed_grad_got,
    )
    other_grad = swap(qkv_theirs)
    qkv_terms = gradients([((inputs, 0), (inputs, 1), qkv_mine, qkv_theirs)], groups)
    got, returned = after((got, returned), qkv_terms)
    both = [k.astype(F32) + g.astype(F32) for k, g in zip(kept, got)]
    sent = [b[1].astype(BF16) for b in both]
    kept = [b[0] for b in both] if got else [k[0] for k in kept]
    first_grad = after(first_grad, (qkv_terms, sent, kept))
    qkv_got = near_sends(qkv_terms[1:], groups)
    got = [lax.ppermute(v, "dp", pairs(groups, 2 - n)) for n, v in enumerate(sent)]
    input_low = input_rows(
        first_grad, qkv_mine, other_grad, qkv_weights + qkv_other
    )
    given = route(core, token_slot, input_low, swap(input_low), groups, (sums, up_sums, qv_sums))
    got = after(got, given)
    if got:
        kept = [k + g.astype(F32) for k, g in zip(kept, got)]
    ffn_terms = far_halves(jnp.concatenate(kept, axis=2), groups, 0)
    payload, given = given, exchange(given)
    layer_out = weave(core, after(returned, payload), half_run)
    ffn_sum = far_step(ffn_terms, groups, 0, (given, layer_out))
    qkv_got = after(qkv_got, ffn_sum)
    for bit in range(1, far.bit_length() - 1):
        ffn_sum = far_step(ffn_sum, groups, bit, qkv_got)
    qkv_sum = far_direct(sum_of(qkv_terms[0], qkv_got), groups, ffn_sum)
    (
        input_gradient, query_bias_sum, value_bias_sum, out_bias_sum, first_gain_sum,
        first_shift_sum, down_bias_sum, second_gain_sum, second_shift_sum, up_bias_sum,
    ) = weave(core, given, half_run, features // groups // 2)
    return (
        layer_out,
        input_gradient,
        qkv_sum[:, :width],
        query_bias_sum,
        qkv_sum[:, width : 2 * width],
        qkv_sum[:, 2 * width :],
        value_bias_sum,
        ffn_sum[:, 2 * ff_width :].T,
        out_bias_sum,
        first_gain_sum,
        first_shift_sum,
        ffn_sum[:, ff_width : 2 * ff_width],
        up_bias_sum,
        ffn_sum[:, :ff_width].T,
        down_bias_sum,
        second_gain_sum,
        second_shift_sum,
    )


def solution(mesh):
    rows = P("dp", None)
    in_specs = (
        rows,
        rows,
        rows,
        P(None, "tensor"),
        P("tensor"),
        P(None, "tensor"),
        P(None, "tensor"),
        P("tensor"),
        P("tensor", None),
        P(),
        P(),
        P(),
        P(None, "tensor"),
        P("tensor"),
        P("tensor", None),
        P(),
        P(),
        P(),
        rows,
    )
    spread = P(("dp", "tensor"))
    out_specs = (
        rows,
        rows,
        P("dp", "tensor"),
        spread,
        P("dp", "tensor"),
        P("dp", "tensor"),
        spread,
        P("tensor", "dp"),
        spread,
        spread,
        spread,
        P("dp", "tensor"),
        spread,
        P("tensor", "dp"),
        spread,
        spread,
        spread,
    )
    return jax.shard_map(local, mesh=mesh, in_specs=in_specs, out_specs=out_specs, check_vma=False)
```

```python
import functools
import jax
import jax.numpy as jnp
from jax import lax
from jax.experimental import pallas as pl
from jax.experimental.pallas import tpu as pltpu
from jax.sharding import PartitionSpec as P

HD = 64
LANES = 128
SEG_MAX = 8
FORWARD_ROWS = 512
FORWARD_KEYS = 512
QB = 256
KB = 256
ROW_TILE = 64


EPSILON = 1e-12
MASKED = -1e30
F32 = jnp.float32
BF16 = jnp.bfloat16
SWAP = [(0, 1), (1, 0)]
VMEM_LIMIT = 60 << 20


def swap(values):
    return lax.ppermute(values, "tensor", SWAP)


def nt(a, b):
    return lax.dot_general(a, b, (((1,), (1,)), ((), ())), preferred_element_type=F32)


def nn(a, b):
    return jnp.dot(a, b, preferred_element_type=F32)


def segment_ends(lengths):
    ends, end = [], jnp.int32(0)
    for n in range(lengths.shape[1]):
        end = end + lengths[0, n]
        ends.append(end)
    return ends


def bounds(ends, rows, first, last):
    low, high = jnp.int32(0), jnp.int32(rows)
    for end in ends:
        low = jnp.where(end <= first, jnp.maximum(low, end), low)
        high = jnp.where(end > last, jnp.minimum(high, end), high)
    return low, high


def lane_bounds(ends, rows):
    lane = lax.broadcasted_iota(jnp.int32, (1, LANES), 1)
    start = jnp.full((1, LANES), 2 * rows, jnp.int32)
    stop = jnp.zeros((1, LANES), jnp.int32)
    begin = 0
    for n, end in enumerate(ends):
        start = jnp.where(lane == n, begin, start)
        stop = jnp.where(lane == n, end, stop)
        begin = end
    return start, stop


def key_marks(ends, rows, offset):
    start, stop = lane_bounds(ends, rows)
    pos = lax.broadcasted_iota(jnp.int32, (rows, LANES), 0) + offset
    pos = jnp.where(pos >= rows, pos - rows, pos)
    return ((pos >= start) & (pos < stop)).astype(F32).astype(BF16)


def query_marks(ends, rows, first, count):
    start, stop = lane_bounds(ends, rows)
    lane = lax.broadcasted_iota(jnp.int32, (1, LANES), 1)
    pos = lax.broadcasted_iota(jnp.int32, (count, LANES), 0) + first
    return jnp.where((lane < len(ends)) & ((pos < start) | (pos >= stop)), MASKED, 0.0)


def lane_mask(half):
    lane = lax.broadcasted_iota(jnp.int32, (1, LANES), 1)
    return ((lane // HD) == half).astype(F32).astype(BF16)


def of_pair(h):
    return slice(h // 2 * LANES, (h // 2 + 1) * LANES)


def forward_kernel(
    lengths, core, q_ref, k_ref, v_ref, o_mine, o_other, lse_ref, keys, values_t, mixed, peaks, totals
):
    rows, width = k_ref.shape
    heads = width // HD
    step = pl.program_id(0)
    ends = segment_ends(lengths)
    offset = core[0] * (rows // 2)

    @pl.when(step == 0)
    def _():
        marks = key_marks(ends, rows, offset)
        for p in range(heads // 2):
            keys[p, :, :LANES] = k_ref[:, of_pair(2 * p)]
            keys[p, :, LANES:] = marks
        for block in range(rows // FORWARD_KEYS):
            at = slice(block * FORWARD_KEYS, (block + 1) * FORWARD_KEYS)
            values_t[block] = v_ref[at, :].astype(F32).T.astype(BF16)

    first = lax.rem(step * FORWARD_ROWS + offset, rows)
    low, high = bounds(ends, rows, first, first + FORWARD_ROWS - 1)
    block_low, block_high = low // FORWARD_KEYS, (high + FORWARD_KEYS - 1) // FORWARD_KEYS
    marked = query_marks(ends, rows, first, FORWARD_ROWS).astype(BF16)
    queries = []
    for p in range(heads // 2):
        query = q_ref[:, of_pair(2 * p)] * BF16(HD**-0.5)
        both = [jnp.concatenate([query * lane_mask(n), marked], axis=1) for n in range(2)]
        queries.append(jnp.concatenate(both, axis=0))
    mixed[...] = jnp.zeros_like(mixed)
    peaks[...] = jnp.full_like(peaks, MASKED)
    totals[...] = jnp.zeros_like(totals)

    def block_step(i, carry):
        start = lax.rem(i * FORWARD_KEYS + rows - offset, rows)
        at = pl.ds(pl.multiple_of(start, FORWARD_KEYS), FORWARD_KEYS)
        block = start // FORWARD_KEYS
        made = [nt(keys[p, at, :], queries[p]) for p in range(heads // 2)]
        for p in range(heads // 2):
            scores = made[p]
            row = slice(p, p + 1)
            peak = jnp.maximum(peaks[row, :], jnp.max(scores, axis=0, keepdims=True))
            shrink = jnp.exp(peaks[row, :] - peak)
            weights = jnp.exp(scores - peak)
            peaks[row, :] = peak
            totals[row, :] = totals[row, :] * shrink + jnp.sum(weights, axis=0, keepdims=True)
            part = nn(values_t[block, of_pair(2 * p), :], weights.astype(BF16))
            for n in range(2):
                h = slice((2 * p + n) * HD, (2 * p + n + 1) * HD)
                q = slice(n * FORWARD_ROWS, (n + 1) * FORWARD_ROWS)
                mixed[h, :] = mixed[h, :] * shrink[:, q] + part[n * HD : (n + 1) * HD, q]
        return carry

    lax.fori_loop(block_low, block_high, block_step, 0)
    inverse = 1.0 / totals[...]
    lse = peaks[...] + jnp.log(totals[...])
    for h in range(heads):
        wide = slice(h * HD, (h + 1) * HD)
        p, q = h // 2, slice(h % 2 * FORWARD_ROWS, (h % 2 + 1) * FORWARD_ROWS)
        mixed[wide, :] = mixed[wide, :] * inverse[p : p + 1, q]
        lse_ref[h : h + 1, :] = lse[p : p + 1, q]
    made = mixed[...].T.astype(BF16)
    half = rows // 2
    for n in range(rows // FORWARD_ROWS):
        start = n * FORWARD_ROWS % half

        @pl.when(step == n)
        def _():
            ref = (o_mine, o_other)[n * FORWARD_ROWS // half]
            ref[start : start + FORWARD_ROWS, :] = made


def whole(shape):
    return pl.BlockSpec(shape, lambda *_: (0,) * len(shape))


def attention_forward(lengths, core, query_rows, key_rows, value_rows):
    rows, width = query_rows.shape
    heads = width // HD
    tile = pl.BlockSpec((FORWARD_ROWS, width), lambda i, *_: (i, 0))
    return pl.pallas_call(
        forward_kernel,
        grid_spec=pltpu.PrefetchScalarGridSpec(
            num_scalar_prefetch=2,
            grid=(rows // FORWARD_ROWS,),
            in_specs=[tile, whole((rows, width)), whole((rows, width))],
            out_specs=[whole((rows // 2, width))] * 2
            + [pl.BlockSpec((8, FORWARD_ROWS), lambda i, *_: (0, i))],
            scratch_shapes=[
                pltpu.VMEM((heads // 2, rows, 2 * LANES), BF16),
                pltpu.VMEM((rows // FORWARD_KEYS, width, FORWARD_KEYS), BF16),
                pltpu.VMEM((width, FORWARD_ROWS), F32),
                pltpu.VMEM((8, 2 * FORWARD_ROWS), F32),
                pltpu.VMEM((8, 2 * FORWARD_ROWS), F32),
            ],
        ),
        out_shape=[jax.ShapeDtypeStruct((rows // 2, width), BF16)] * 2
        + [jax.ShapeDtypeStruct((8, rows), F32)],
        cost_estimate=pl.CostEstimate(
            flops=8 * rows * rows * LANES * heads,
            bytes_accessed=8 * rows * width,
            transcendentals=rows * rows * heads // 2,
        ),
        compiler_params=params(),
        name="attend",
    )(lengths, core, query_rows, key_rows, value_rows)


def backward_kernel(
    lengths, core, q_ref, do_mine, do_other, o_mine, o_other, lse_ref, k_ref, v_ref,
    grad_mine, grad_other, sums_ref, keys, values, keys_t, dk_sum, dv_sum, dq_sum
):
    rows, width = k_ref.shape
    heads = width // HD
    step = pl.program_id(0)
    steps = rows // QB
    ends = segment_ends(lengths)
    offset = core[0] * (rows // 2)
    scale = HD**-0.5

    @pl.when(step == 0)
    def _():
        marks = key_marks(ends, rows, offset)
        for p in range(heads // 2):
            keys[p, :, :LANES] = k_ref[:, of_pair(2 * p)]
            keys[p, :, LANES:] = marks
            values[p] = v_ref[:, of_pair(2 * p)]
        for block in range(rows // KB):
            at = slice(block * KB, (block + 1) * KB)
            keys_t[block] = k_ref[at, :].astype(F32).T.astype(BF16)
        dk_sum[...] = jnp.zeros_like(dk_sum)
        dv_sum[...] = jnp.zeros_like(dv_sum)

    first = lax.rem(step * QB + offset, rows)
    low, high = bounds(ends, rows, first, first + QB - 1)
    block_low, block_high = low // KB, (high + KB - 1) // KB
    marked = query_marks(ends, rows, first, QB).astype(BF16)
    early = jnp.full((1, width), step, jnp.int32) < steps // 2
    use_mine = early.astype(F32).astype(BF16)
    use_other = (~early).astype(F32).astype(BF16)
    grad_rows = do_mine[...] * use_mine + do_other[...] * use_other
    mixed_rows = o_mine[...] * use_mine + o_other[...] * use_other
    lane = lax.broadcasted_iota(jnp.int32, (8, LANES), 1)
    row = lax.broadcasted_iota(jnp.int32, (8, LANES), 0)
    by_head = (lane // HD == row).astype(F32).astype(BF16)
    queries, grads, marked_queries, logsums, centres = [], [], [], [], []
    for p in range(heads // 2):
        pair = of_pair(2 * p)
        query = [q_ref[:, pair] * (lane_mask(n) * BF16(scale)) for n in range(2)]
        grad = grad_rows[:, pair]
        exact = grad.astype(F32) * mixed_rows[:, pair].astype(F32)
        high_term = exact.astype(BF16)
        low_term = (exact - high_term.astype(F32)).astype(BF16)
        centre = nt(by_head, high_term) + nt(by_head, low_term)
        centres.append(jnp.concatenate([centre[0:1, :], centre[1:2, :]], axis=1))
        logsums.append(
            jnp.concatenate([lse_ref[2 * p : 2 * p + 1, :], lse_ref[2 * p + 1 : 2 * p + 2, :]], axis=1)
        )
        queries.append(jnp.concatenate(query, axis=0))
        grads.append(jnp.concatenate([grad * lane_mask(n) for n in range(2)], axis=0))
        marked_queries.append(
            jnp.concatenate([queries[p], jnp.concatenate([marked, marked], axis=0)], axis=1)
        )
    dq_sum[...] = jnp.zeros_like(dq_sum)

    def block_step(i, carry):
        start = lax.rem(i * KB + rows - offset, rows)
        at = pl.ds(pl.multiple_of(start, KB), KB)
        block = start // KB
        scores = [nt(keys[p, at, :], marked_queries[p]) for p in range(heads // 2)]
        pulls = [nt(values[p, at, :], grads[p]) for p in range(heads // 2)]
        for p in range(heads // 2):
            weights = jnp.exp(scores[p] - logsums[p])
            pulled = pulls[p]
            dv_sum[at, of_pair(2 * p)] += nn(weights.astype(BF16), grads[p])
            slopes = (weights * (pulled - centres[p])).astype(BF16)
            dk_sum[at, of_pair(2 * p)] += nn(slopes, queries[p])
            part = nn(keys_t[block, of_pair(2 * p), :], slopes)
            for n in range(2):
                h = slice((2 * p + n) * HD, (2 * p + n + 1) * HD)
                dq_sum[h, :] += part[n * HD : (n + 1) * HD, n * QB : (n + 1) * QB]
        return carry

    lax.fori_loop(block_low, block_high, block_step, 0)
    made = (dq_sum[...] * scale).T.astype(BF16)
    half = rows // 2
    for n in range(steps):
        start = n * QB % half

        @pl.when(step == n)
        def _():
            (grad_mine, grad_other)[n * QB // half][start : start + QB, :width] = made

    total = jnp.sum(made.astype(F32), axis=0, keepdims=True)

    @pl.when(step == 0)
    def _():
        sums_ref[...] = jnp.zeros_like(sums_ref)

    sums_ref[0:1, :] += total

    @pl.when(step == steps - 1)
    def _():
        for n, ref in enumerate((grad_mine, grad_other)):
            at = slice(n * half, (n + 1) * half)
            ref[:, width : 2 * width] = dk_sum[at, :].astype(BF16)
            made = dv_sum[at, :].astype(BF16)
            ref[:, 2 * width :] = made
            sums_ref[1:2, :] += jnp.sum(made.astype(F32), axis=0, keepdims=True)


def attention_backward(
    lengths, core, query_rows, key_rows, value_rows, mixed, lse, grad_mine, grad_other
):
    rows, width = query_rows.shape
    heads = width // HD
    steps = rows // QB
    tile = pl.BlockSpec((QB, width), lambda i, *_: (i, 0))
    full = whole((rows, width))
    early = pl.BlockSpec((QB, width), lambda i, *_: (jnp.minimum(i, steps // 2 - 1), 0))
    late = pl.BlockSpec((QB, width), lambda i, *_: (jnp.maximum(i - steps // 2, 0), 0))
    outs = [jax.ShapeDtypeStruct((rows // 2, 3 * width), BF16)] * 2
    outs.append(jax.ShapeDtypeStruct((8, width), F32))
    return pl.pallas_call(
        backward_kernel,
        grid_spec=pltpu.PrefetchScalarGridSpec(
            num_scalar_prefetch=2,
            grid=(steps,),
            in_specs=[
                tile,
                early,
                late,
                early,
                late,
                pl.BlockSpec((8, QB), lambda i, *_: (0, i)),
                full,
                full,
            ],
            out_specs=[whole(o.shape) for o in outs],
            scratch_shapes=[
                pltpu.VMEM((heads // 2, rows, 2 * LANES), BF16),
                pltpu.VMEM((heads // 2, rows, LANES), BF16),
                pltpu.VMEM((rows // KB, width, KB), BF16),
                pltpu.VMEM((rows, width), F32),
                pltpu.VMEM((rows, width), F32),
                pltpu.VMEM((width, QB), F32),
            ],
        ),
        out_shape=outs,
        cost_estimate=pl.CostEstimate(
            flops=20 * rows * rows * LANES * heads,
            bytes_accessed=16 * rows * width,
            transcendentals=rows * rows * heads // 2,
        ),
        compiler_params=params(),
        name="attend_back",
    )(lengths, core, query_rows, grad_mine, grad_other, *mixed, lse, key_rows, value_rows)


def params():
    return pltpu.CompilerParams(vmem_limit_bytes=VMEM_LIMIT)


def cost(flops, moved, transcendentals=0):
    return pl.CostEstimate(flops=flops, bytes_accessed=moved, transcendentals=transcendentals)


def columns_of(slots, core, run_rows, half):
    half_run = run_rows // 2
    run, place = slots // run_rows, slots % run_rows
    held = (place // half_run + core) % 2
    return held * half + run * half_run + place % half_run


def one_hot(column, width, base):
    count = column.shape[1]
    down = jnp.broadcast_to(column, (8, count)).T[:, :1]
    lane = lax.broadcasted_iota(jnp.int32, (count, width), 1) + base
    return (down == lane).astype(F32).astype(BF16)


def intake_kernel(
    run_rows, core, slots, mine_ref, other_ref, q_weight, k_weight, v_weight, q_bias, v_bias,
    x_ref, q_ref, k_ref, v_ref
):
    half = mine_ref.shape[0]
    column = columns_of(slots[...], core[0], run_rows, half)
    rows = nn(one_hot(column, half, 0), mine_ref[...])
    rows = (rows + nn(one_hot(column, half, half), other_ref[...])).astype(BF16)
    x_ref[...] = rows
    q_ref[...] = (nn(rows, q_weight[...]) + q_bias[...]).astype(BF16)
    k_ref[...] = nn(rows, k_weight[...]).astype(BF16)
    v_ref[...] = (nn(rows, v_weight[...]) + v_bias[...]).astype(BF16)


def intake(core, slots, run_rows, mine_rows, other_rows, weights, biases):
    half, features = mine_rows.shape
    rows = 2 * half
    width = weights[0].shape[1]
    count = 512
    blocks = rows // count

    def tile(n):
        return pl.BlockSpec((count, n), lambda i, core: (i, 0))

    return pl.pallas_call(
        functools.partial(intake_kernel, run_rows),
        grid_spec=pltpu.PrefetchScalarGridSpec(
            num_scalar_prefetch=1,
            grid=(blocks,),
            in_specs=[
                pl.BlockSpec(
                    (1, count), lambda i, core: (0, (i + core[0] * (blocks // 2)) % blocks)
                ),
                whole((half, features)),
                whole((half, features)),
            ]
            + [whole((features, width))] * 3
            + [whole((1, width))] * 2,
            out_specs=[tile(features), tile(width), tile(width), tile(width)],
        ),
        out_shape=[jax.ShapeDtypeStruct((rows, features), BF16)]
        + [jax.ShapeDtypeStruct((rows, width), BF16)] * 3,
        cost_estimate=cost(2 * rows * features * (rows + 3 * width), 8 * rows * features),
        compiler_params=params(),
        name="intake",
    )(core, slots, mine_rows, other_rows, *weights, *biases)


def centred(values):
    centre = values - jnp.mean(values, axis=-1, keepdims=True)
    inverse = lax.rsqrt(jnp.mean(centre * centre, axis=-1, keepdims=True) + EPSILON)
    return centre * inverse, inverse


def norm_back(upstream, normed, inverse, gain):
    scaled = upstream * gain
    return inverse * (
        scaled
        - jnp.mean(scaled, axis=-1, keepdims=True)
        - normed * jnp.mean(scaled * normed, axis=-1, keepdims=True)
    )


def add_rows(ref, row, values):
    ref[row : row + 1, :] += jnp.sum(values, axis=0, keepdims=True)


def rows_kernel(
    run_rows, core, x_ref, mixed_mine, mixed_other, slots, cot_mine, cot_other,
    out_bias, first_gain, first_shift, down_bias, second_gain, second_shift, bias_mine, bias_other,
    out_mine, out_other, up_mine, up_other, down_mine, down_other,
    y_out, hb_out, second_out, act_out_mine, act_out_other, du_out_mine, du_out_other, first_out, low_out,
    back_out_mine, back_out_other, sums, up_sums,
    w_out, w_up, w_down, sems, out_sems, hidden, first_inv, total, slope, grad, pulled, biases,
    y_ref, hb_ref, second_ref, act, du, first_ref, low_ref, back
):
    half, features = x_ref.shape
    width = mixed_mine.shape[1]
    chunks, _, chunk = w_up.shape
    per_half = chunks // 2
    tiles = half // ROW_TILE
    copies = [
        pltpu.make_async_copy(out_mine, w_out.at[0], sems.at[0]),
        pltpu.make_async_copy(out_other, w_out.at[1], sems.at[1]),
    ]
    up_copies, down_copies = [], []
    for c in range(chunks):
        up, down = ((up_mine, down_mine), (up_other, down_other))[c // per_half]
        at = pl.ds(c % per_half * chunk, chunk)
        up_copies.append(pltpu.make_async_copy(up.at[:, at], w_up.at[c], sems.at[2 + c]))
        down_copies.append(
            pltpu.make_async_copy(down.at[at, :], w_down.at[c], sems.at[2 + chunks + c])
        )
    outgoing = []

    def send(source, target):
        copy = pltpu.make_async_copy(source, target, out_sems.at[len(outgoing)])
        copy.start()
        outgoing.append(copy)

    for copy in copies:
        copy.start()
    for up, down in zip(up_copies, down_copies):
        up.start()
        down.start()
    out_bias, first_gain, first_shift = out_bias[...], first_gain[...], first_shift[...]
    down_bias, second_gain, second_shift = down_bias[...], second_gain[...], second_shift[...]
    sums[...] = jnp.zeros_like(sums)
    up_sums[...] = jnp.zeros_like(up_sums)

    column = columns_of(slots[...], core[0], run_rows, half)
    grad[...] = nn(one_hot(column, half, 0), cot_mine[...])
    grad[...] += nn(one_hot(column, half, half), cot_other[...])

    def of_chunk(refs, c):
        return refs[c // per_half], pl.ds(c % per_half * chunk, chunk)

    for copy in copies:
        copy.wait()
    total[...] = nn(mixed_mine[...], w_out[0]) + nn(mixed_other[...], w_out[1])

    @pl.loop(0, tiles, unroll=2)
    def _(i):
        at = pl.ds(pl.multiple_of(i * ROW_TILE, ROW_TILE), ROW_TILE)
        normed, inverse = centred(x_ref[at, :].astype(F32) + total[at, :] + out_bias)
        rows = normed * first_gain + first_shift
        hidden[at, :] = rows
        hb_ref[at, :] = rows.astype(BF16)
        first_ref[at, :] = normed
        first_inv[at, :] = inverse

    send(hb_ref, hb_out)

    block = half // 2
    blocks = [slice(r * block, (r + 1) * block) for r in range(2)]
    for c in range(chunks):
        ref, wide = of_chunk((bias_mine, bias_other), c)
        biases[c : c + 1, :] = ref[:, wide]

    def inner_of(c):
        pltpu.make_async_copy(up_mine.at[:, pl.ds(0, chunk)], w_up.at[c], sems.at[2 + c]).wait()
        for at in blocks:
            slope[c, at, :] = nn(hb_ref[at, :], w_up[c]) + biases[pl.ds(c, 1), :]

    def activate(c):
        for at in blocks:
            inner = slope[c, at, :]
            share = 0.5 * (1.0 + lax.erf(inner * 0.7071067811865476))
            density = jnp.exp(-0.5 * inner * inner) * 0.3989422804014327
            act[c, at, :] = (inner * share).astype(BF16)
            slope[c, at, :] = share + inner * density
            total[at, :] += nn(act[c, at, :], w_down[c])

    def down_ready(c):
        source = down_mine.at[pl.ds(0, chunk), :]
        pltpu.make_async_copy(source, w_down.at[c], sems.at[2 + chunks + c]).wait()

    total[...] = jnp.zeros_like(total)
    inner_of(0)

    @pl.loop(0, chunks - 1)
    def _(c):
        down_ready(c)
        inner_of(c + 1)
        activate(c)

    down_ready(chunks - 1)
    activate(chunks - 1)
    for c in range(chunks):
        ref, wide = of_chunk((act_out_mine, act_out_other), c)
        send(act.at[c], ref.at[:, wide])

    @pl.loop(0, tiles, unroll=2)
    def _(i):
        at = pl.ds(pl.multiple_of(i * ROW_TILE, ROW_TILE), ROW_TILE)
        normed, inverse = centred(hidden[at, :] + total[at, :] + down_bias)
        y_ref[at, :] = (normed * second_gain + second_shift).astype(BF16)
        upstream = grad[at, :]
        add_rows(sums, 4, upstream * normed)
        add_rows(sums, 5, upstream)
        back = norm_back(upstream, normed, inverse, second_gain)
        add_rows(sums, 3, back)
        second_ref[at, :] = back.astype(BF16)
        grad[at, :] = back

    send(y_ref, y_out)
    send(second_ref, second_out)
    def pull(c):
        for at in blocks:
            pulled[c % 2, at, :] = nt(second_ref[at, :], w_down[c])

    def push(c):
        row = (c // per_half ^ core[0]) * per_half + c % per_half
        for at in blocks:
            low = (pulled[c % 2, at, :] * slope[c, at, :]).astype(BF16)
            du[c, at, :] = low
            up_sums[pl.ds(row, 1), :] += jnp.sum(low.astype(F32), axis=0, keepdims=True)
            grad[at, :] += nt(low, w_up[c])

    pull(0)

    @pl.loop(0, chunks - 1)
    def _(c):
        pull(c + 1)
        push(c)

    push(chunks - 1)
    for c in range(chunks):
        ref, wide = of_chunk((du_out_mine, du_out_other), c)
        send(du.at[c], ref.at[:, wide])

    @pl.loop(0, tiles, unroll=2)
    def _(i):
        at = pl.ds(pl.multiple_of(i * ROW_TILE, ROW_TILE), ROW_TILE)
        upstream, normed = grad[at, :], first_ref[at, :]
        add_rows(sums, 1, upstream * normed)
        add_rows(sums, 2, upstream)
        back = norm_back(upstream, normed, first_inv[at, :], first_gain)
        add_rows(sums, 0, back)
        first_ref[at, :] = back

    send(first_ref, first_out)
    low_ref[...] = first_ref[...].astype(BF16)
    send(low_ref, low_out)
    for n, out in enumerate((back_out_mine, back_out_other)):
        back[n] = nt(low_ref[...], w_out[n]).astype(BF16)
        send(back.at[n], out)
    for copy in outgoing:
        copy.wait()


def row_pass(
    core, inputs, mixed, mixed_other, slots, run_rows, cot_mine, cot_other, vectors,
    out_mine, out_other, up_mine, up_other, down_mine, down_other
):
    half, features = cot_mine.shape
    width = mixed.shape[1]
    chunk = features
    chunks = 2 * up_mine.shape[1] // chunk
    any_space = pl.BlockSpec(memory_space=pl.ANY)

    def low(*shape):
        return jax.ShapeDtypeStruct(shape, BF16)

    outs = [
        low(half, features),
        low(half, features),
        low(half, features),
        low(half, up_mine.shape[1]),
        low(half, up_mine.shape[1]),
        low(half, up_mine.shape[1]),
        low(half, up_mine.shape[1]),
        jax.ShapeDtypeStruct((half, features), F32),
        low(half, features),
        low(half, width),
        low(half, width),
        jax.ShapeDtypeStruct((8, features), F32),
        jax.ShapeDtypeStruct((chunks, chunk), F32),
    ]
    return pl.pallas_call(
        functools.partial(rows_kernel, run_rows),
        grid_spec=pltpu.PrefetchScalarGridSpec(
            num_scalar_prefetch=1,
            grid=(1,),
            in_specs=[
                whole((half, features)),
                whole((half, width)),
                whole((half, width)),
                pl.BlockSpec((1, half), lambda i, core: (0, core[0])),
                whole((half, features)),
                whole((half, features)),
            ]
            + [whole(v.shape) for v in vectors]
            + [any_space] * 6,
            out_specs=[any_space] * (len(outs) - 2) + [whole(o.shape) for o in outs[-2:]],
            scratch_shapes=[
                pltpu.VMEM((2, width, features), BF16),
                pltpu.VMEM((chunks, features, chunk), BF16),
                pltpu.VMEM((chunks, chunk, features), BF16),
                pltpu.SemaphoreType.DMA((2 + 2 * chunks,)),
                pltpu.SemaphoreType.DMA((7 + 2 * chunks,)),
                pltpu.VMEM((half, features), F32),
                pltpu.VMEM((half, 1), F32),
                pltpu.VMEM((half, features), F32),
                pltpu.VMEM((chunks, half, chunk), F32),
                pltpu.VMEM((half, features), F32),
                pltpu.VMEM((2, half, chunk), F32),
                pltpu.VMEM((chunks, chunk), F32),
                pltpu.VMEM((half, features), BF16),
                pltpu.VMEM((half, features), BF16),
                pltpu.VMEM((half, features), BF16),
                pltpu.VMEM((chunks, half, chunk), BF16),
                pltpu.VMEM((chunks, half, chunk), BF16),
                pltpu.VMEM((half, features), F32),
                pltpu.VMEM((half, features), BF16),
                pltpu.VMEM((2, half, width), BF16),
            ],
        ),
        out_shape=outs,
        cost_estimate=cost(
            8 * half * features * chunk * chunks + 10 * half * features * features,
            30 * half * features + 8 * features * chunk * chunks,
            half * chunk * chunks,
        ),
        compiler_params=params(),
        name="row_pass",
    )(
        core, inputs, mixed, mixed_other, slots, cot_mine, cot_other, *vectors,
        out_mine, out_other, up_mine, up_other, down_mine, down_other
    )


def after(values, others):
    return lax.optimization_barrier((values, others))[0]


def near_groups(groups):
    near = 4 if groups % 4 == 0 else 1
    return near, groups // near


def tn(left, right):
    return lax.dot_general(left, right, (((0,), (0,)), ((), ())), preferred_element_type=F32)


def by_place(terms, groups):
    near, far = near_groups(groups)
    place = lax.axis_index("dp") % near
    terms = terms.reshape(far, near, terms.shape[0] // groups, terms.shape[1])
    return [lax.dynamic_index_in_dim(terms, place ^ n, 1, keepdims=False) for n in range(near)]


def gradient_kernel(chunks, near, share, halving, me, *refs):
    operands, outs, acc = refs[: 4 * len(chunks)], refs[4 * len(chunks) : -1], refs[-1]
    step = pl.program_id(0)
    first, column = 0, 0
    for n, (chunk, count) in enumerate(chunks):
        left, left_more, right, right_more = operands[4 * n : 4 * n + 4]

        @pl.when((step >= first) & (step < first + count))
        def _():
            acc[:, :chunk] = tn(left[...], right[...])
            acc[:, :chunk] += tn(left_more[...], right_more[...])
            at = pl.ds(pl.multiple_of(column + (step - first) * chunk, LANES), chunk)

            def place(out, place):
                for f in range(out.shape[0]):
                    row = share * (f * near + (me[0] ^ place))
                    row = pl.ds(pl.multiple_of(row, 16), share)
                    out[f, :, at] = acc[row, :chunk].astype(out.dtype)

            if halving:
                for out, (a, b) in zip(outs, ((0, 3 - halving), (halving, 3))):
                    place(out.at[0], a)
                    place(out.at[1], b)
            else:
                for m, out in enumerate(outs):
                    place(out, m)

        first += count
        column += count * chunk


def gradients(pieces, groups, halving=0):
    near, far = near_groups(groups)
    features = pieces[0][0][0].shape[1]
    share = features // groups
    if near != 4 or share % 16 != 0:

        def rows_of(left, rows):
            return lax.slice_in_dim(left[0], left[1] * rows, (left[1] + 1) * rows, axis=0)

        terms = [
            tn(rows_of(p[0], p[2].shape[0]), p[2]) + tn(rows_of(p[1], p[3].shape[0]), p[3])
            for p in pieces
        ]
        made = [t.astype(BF16) for t in by_place(jnp.concatenate(terms, axis=1), groups)]
        if halving:
            made = [
                jnp.stack([made[0], made[3 - halving]]), jnp.stack([made[halving], made[3]])
            ]
        return made
    in_specs, operands, chunks, base, columns = [], [], [], 0, 0
    for left, left_more, right, right_more in pieces:
        rows = right.shape[0]
        chunk = min(features, right.shape[1])
        if right.shape[1] % chunk:
            chunk = right.shape[1] // 3
        count = right.shape[1] // chunk

        def at(j, me, base=base, count=count):
            return 0, jnp.clip(j - base, 0, count - 1)

        for array, block in (left, left_more):
            in_specs.append(
                pl.BlockSpec((rows, features), lambda j, me, block=block: (block, 0))
            )
            operands.append(array)
        in_specs += [pl.BlockSpec((rows, chunk), at)] * 2
        operands += [right, right_more]
        chunks.append((chunk, count))
        base += count
        columns += count * chunk
    if halving:
        outs = [jax.ShapeDtypeStruct((2, far, share, columns), BF16)] * 2
    else:
        outs = [jax.ShapeDtypeStruct((far, share, columns), BF16)] * near
    return pl.pallas_call(
        functools.partial(gradient_kernel, chunks, near, share, halving),
        grid_spec=pltpu.PrefetchScalarGridSpec(
            num_scalar_prefetch=1,
            grid=(base,),
            in_specs=in_specs,
            out_specs=[whole(o.shape) for o in outs],
            scratch_shapes=[pltpu.VMEM((features, features), F32)],
        ),
        out_shape=outs,
        cost_estimate=cost(4 * rows * features * columns, 8 * rows * features + 4 * features * columns),
        compiler_params=params(),
        name="gradients",
    )((lax.axis_index("dp") % near).reshape(1), *operands)


def pairs(groups, distance):
    return [(i, i ^ distance) for i in range(groups)]


def far_halves(total, groups, bit):
    total = total.reshape(-1, 2, *total.shape[1:])
    side = (lax.axis_index("dp") // near_groups(groups)[0] >> bit) & 1
    kept = lax.dynamic_index_in_dim(total, side, 1, keepdims=False)
    return kept, lax.dynamic_index_in_dim(total, 1 - side, 1, keepdims=False).astype(BF16)


def far_step(halves, groups, bit, first=()):
    near, far = near_groups(groups)
    kept, sent = halves
    got = after(lax.ppermute(sent, "dp", pairs(groups, near << bit)), first)
    total = kept.astype(F32) + got.astype(F32)
    return far_halves(total, groups, bit + 1) if 2 << bit < far else total[0]


def far_direct(total, groups, first=()):
    near, far = near_groups(groups)
    run = lax.axis_index("dp") // near
    kept = lax.dynamic_index_in_dim(total, run, 0, keepdims=False)
    got = []
    for step in range(1, far):
        sent = lax.dynamic_index_in_dim(total, run ^ step, 0, keepdims=False).astype(BF16)
        got.append(lax.ppermute(sent, "dp", pairs(groups, step * near)))
    return sum_of(kept, after(got, first))


def near_sends(terms, groups):
    return [lax.ppermute(t, "dp", pairs(groups, n + 1)) for n, t in enumerate(terms)]


def sum_of(kept, got):
    kept = kept.astype(F32)
    for term in got:
        kept = kept + term.astype(F32)
    return kept


def input_kernel(first_ref, mine_ref, other_ref, *refs):
    weights, out_ref = refs[:-1], refs[-1]
    total = first_ref[...]
    for n, rows in enumerate((mine_ref, other_ref)):
        wide = jnp.concatenate([weight[...] for weight in weights[3 * n : 3 * n + 3]], axis=1)
        total = total + nt(rows[...], wide)
    out_ref[...] = total.astype(BF16)


def input_rows(first_grad, mine_rows, other_rows, weights):
    half, features = first_grad.shape
    wide = other_rows.shape[1]
    count = 256

    def tile(n):
        return pl.BlockSpec((count, n), lambda i: (i, 0))

    return pl.pallas_call(
        input_kernel,
        grid=(half // count,),
        in_specs=[tile(features), tile(wide), tile(wide)] + [whole(w.shape) for w in weights],
        out_specs=tile(features),
        out_shape=jax.ShapeDtypeStruct((half, features), BF16),
        cost_estimate=cost(4 * half * features * wide, 8 * half * features + 4 * features * wide),
        compiler_params=params(),
        name="input_rows",
    )(first_grad, mine_rows, other_rows, *weights)


def route_kernel(share, has_extra, core, slots_mine, slots_other, mine_ref, other_ref, *refs):
    out_ref = refs[-1]
    groups, run = out_ref.shape[0], mine_ref.shape[0] // out_ref.shape[0]
    half = mine_ref.shape[0]
    row = lax.broadcasted_iota(jnp.int32, (half, half), 0)
    column_mine = columns_of(slots_mine[...], core[0], 2 * run, half)
    column_other = columns_of(slots_other[...], core[0], 2 * run, half)
    put_mine = (column_mine == row).astype(F32).astype(BF16)
    put_other = (column_other == row).astype(F32).astype(BF16)
    rows = (nn(put_mine, mine_ref[...]) + nn(put_other, other_ref[...])).astype(BF16)
    out_ref[:, :run, :] = rows.reshape(groups, run, rows.shape[1])
    if has_extra:
        sums, up_sums, qv_sums, wide, wide_up = refs[:5]
        features = sums.shape[1]
        width = qv_sums.shape[1]
        wide[...] = jnp.zeros_like(wide)
        wide_up[...] = jnp.zeros_like(wide_up)
        wide[:, :features] = sums[...]
        wide_up[:4, :features] = up_sums[...]
        at = pl.ds(pl.multiple_of(core[0] * width, LANES), width)
        wide[6:8, at] = qv_sums[:2, :]
        for g in range(groups):
            block = wide[:, share * g : share * g + LANES]
            start = 4 * share * g
            blocks = [block]
            parts = []
            for r in range(4):
                line = (start + share * r) // features
                lane = (start + share * r) % features
                parts.append(wide_up[line : line + 1, lane : lane + LANES])
            blocks.append(jnp.concatenate(parts + [jnp.zeros((4, LANES), F32)], axis=0))
            for b, rest in enumerate(blocks):
                for piece in range(3):
                    term = rest.astype(BF16)
                    rest = rest - term.astype(F32)
                    q = 2 * piece + b
                    out_ref[g, run : run + 8, q * LANES : (q + 1) * LANES] = term


def route(core, slots, mine_rows, other_rows, groups, extra=None):
    half, features = mine_rows.shape
    run = half // groups
    share = features // groups
    extra = extra or ()
    args = [core, slots, slots, mine_rows, other_rows, *extra]
    in_specs = [
        pl.BlockSpec((1, half), lambda i, core: (0, core[0])),
        pl.BlockSpec((1, half), lambda i, core: (0, 1 - core[0])),
    ] + [whole(a.shape) for a in args[3:]]
    scratch = [pltpu.VMEM((8, features + LANES), F32)] * 2 if extra else []
    shape = (groups, run + (8 if extra else 0), features)

    def kernel(*refs):
        ins, (out_ref, *more) = refs[: len(args)], refs[len(args) :]
        route_kernel(share, len(extra) > 0, *ins, *more, out_ref)

    return pl.pallas_call(
        kernel,
        grid_spec=pltpu.PrefetchScalarGridSpec(
            num_scalar_prefetch=1,
            grid=(1,),
            in_specs=in_specs,
            out_specs=whole(shape),
            scratch_shapes=scratch,
        ),
        out_shape=jax.ShapeDtypeStruct(shape, BF16),
        cost_estimate=cost(4 * half * half * features, 6 * half * features),
        compiler_params=params(),
        name="route",
    )(*args)


def exchange(values):
    return lax.all_to_all(values, "dp", split_axis=0, concat_axis=0, tiled=True)


def weave_kernel(core, mine_ref, other_ref, out_ref, *outs):
    run = out_ref.shape[2]
    out_ref[:, core[0]] = mine_ref[:, :run, :]
    out_ref[:, 1 - core[0]] = other_ref[:, :run, :]
    if not outs:
        return
    pieces = []
    for q in range(6):
        at = slice(q * LANES, (q + 1) * LANES)
        both = [jnp.sum(r[:, run:, at].astype(F32), axis=0) for r in (mine_ref, other_ref)]
        pieces.append(both[0] + both[1])
    first, more = [pieces[4 + b] + pieces[2 + b] + pieces[b] for b in range(2)]
    each = outs[0].shape[1]
    share = 2 * each
    low = core[0] == 0

    def half_of(values):
        return jnp.where(low, values[:, :each], values[:, each:share])

    for out, row in zip(outs[:8], (6, 7, 0, 1, 2, 3, 4, 5)):
        out[...] = half_of(first[row : row + 1, :])
    pair = jnp.where(low, more[0:2, :share], more[2:4, :share])
    outs[8][:, :share] = pair[0:1, :]
    outs[8][:, share:] = pair[1:2, :]


def weave(core, part, rows_of_core, small=0):
    groups, _, features = part.shape
    outs = [jax.ShapeDtypeStruct((groups, 2, rows_of_core, features), BF16)]
    if small:
        outs += [jax.ShapeDtypeStruct((1, small), F32)] * 8
        outs.append(jax.ShapeDtypeStruct((1, 4 * small), F32))
    rows, *more = pl.pallas_call(
        weave_kernel,
        grid_spec=pltpu.PrefetchScalarGridSpec(
            num_scalar_prefetch=1,
            grid=(1,),
            in_specs=[whole(part.shape)] * 2,
            out_specs=[whole(o.shape) for o in outs],
        ),
        out_shape=outs,
        cost_estimate=cost(1, 1),
        compiler_params=params(),
        name="weave",
    )(core, part, swap(part))
    rows = rows.reshape(groups * 2 * rows_of_core, features)
    return (rows, *[m.reshape(-1) for m in more]) if small else rows


def local(
    tokens,
    token_slot,
    seq_lengths,
    query_weight,
    query_bias,
    key_weight,
    value_weight,
    value_bias,
    out_weight,
    out_bias,
    first_gain,
    first_shift,
    up_weight,
    up_bias,
    down_weight,
    down_bias,
    second_gain,
    second_shift,
    cotangent,
):
    groups = lax.axis_size("dp")
    row_count, features = tokens.shape
    run_rows = row_count // groups
    half_run = run_rows // 2
    half = row_count // 2
    mine = lax.axis_index("tensor")
    core = mine.reshape(1)
    near, far = near_groups(groups)

    def part_of(values):
        return lax.dynamic_slice_in_dim(
            values.reshape(groups, run_rows, features), mine * half_run, half_run, 1
        )

    cot_part = part_of(cotangent)
    token_rows = after(exchange(part_of(tokens)), cot_part).reshape(half, features)
    cot_raw = exchange(cot_part).reshape(half, features)

    qkv_weights = [query_weight, key_weight, value_weight]
    out_other, up_other, down_other = swap(out_weight), swap(up_weight), swap(down_weight)
    vectors = [out_bias, first_gain, first_shift, down_bias, second_gain, second_shift]
    bias_other = swap(up_bias)
    vectors = [v.reshape(1, -1) for v in vectors + [up_bias, bias_other]]
    qkv_other = [swap(w) for w in qkv_weights]
    token_got = after(swap(token_rows), (out_other, up_other, down_other, qkv_other, bias_other))

    inputs, query_rows, key_rows, value_rows = intake(
        core, token_slot, run_rows, token_rows, token_got, qkv_weights,
        (query_bias.reshape(1, -1), value_bias.reshape(1, -1)),
    )
    mixed_mine, mixed_theirs, logsum = attention_forward(seq_lengths, core, query_rows, key_rows, value_rows)
    cot_rows = after(cot_raw, mixed_mine)
    mixed_other = swap(mixed_theirs)
    (
        output_low, hidden_low, second_low, act_mine, act_other, inner_mine, inner_other, first_grad,
        first_low, mixed_grad_mine, mixed_grad_other, sums, up_sums,
    ) = row_pass(
        core, inputs, mixed_mine, mixed_other, token_slot, run_rows, cot_rows, swap(cot_rows), vectors,
        out_weight, out_other, up_weight, up_other, down_weight, down_other,
    )
    mixed_grad_got = swap(mixed_grad_other)

    width = query_weight.shape[1]
    ff_width = up_weight.shape[1]
    output_got = swap(output_low)
    second_low, hidden_low, first_low, act_other, inner_other = after(
        (second_low, hidden_low, first_low, act_other, inner_other), output_got
    )
    second_got, act_got = swap(second_low), swap(act_other)
    hidden_got, inner_got = swap(hidden_low), swap(inner_other)
    first_got = swap(first_low)
    returned = route(core, token_slot, output_low, output_got, groups)
    kept, sent = [], []
    left = gradients([((second_low, 0), (second_got, 0), act_mine, act_got)], groups, near == 4)
    right = [
        ((hidden_low, 0), (hidden_got, 0), inner_mine, inner_got),
        ((first_low, 0), (first_got, 0), mixed_mine, mixed_theirs),
    ]
    right = gradients(right, groups, 2 * (near == 4))
    if near == 4:
        kept, sent = [left[0], right[0]], [left[1], right[1]]
    else:
        kept, sent = [left[0][None], right[0][None]], []
    mixed_grad_mine, mixed_grad_got = after(
        (mixed_grad_mine, mixed_grad_got), (returned, kept, sent)
    )
    returned = exchange(returned)
    got = [lax.ppermute(v, "dp", pairs(groups, n + 1)) for n, v in enumerate(sent)]
    qkv_mine, qkv_theirs, qv_sums = attention_backward(
        seq_lengths, core, query_rows, key_rows, value_rows, (mixed_mine, mixed_theirs), logsum,
        mixed_grad_mine, mixed_grad_got,
    )
    other_grad = swap(qkv_theirs)
    qkv_terms = gradients([((inputs, 0), (inputs, 1), qkv_mine, qkv_theirs)], groups)
    got, returned = after((got, returned), qkv_terms)
    both = [k.astype(F32) + g.astype(F32) for k, g in zip(kept, got)]
    sent = [b[1].astype(BF16) for b in both]
    kept = [b[0] for b in both] if got else [k[0] for k in kept]
    first_grad = after(first_grad, (qkv_terms, sent, kept))
    qkv_got = near_sends(qkv_terms[1:], groups)
    got = [lax.ppermute(v, "dp", pairs(groups, 2 - n)) for n, v in enumerate(sent)]
    input_low = input_rows(
        first_grad, qkv_mine, other_grad, qkv_weights + qkv_other
    )
    given = route(core, token_slot, input_low, swap(input_low), groups, (sums, up_sums, qv_sums))
    got = after(got, given)
    if got:
        kept = [k + g.astype(F32) for k, g in zip(kept, got)]
    ffn_terms = far_halves(jnp.concatenate(kept, axis=2), groups, 0)
    payload, given = given, exchange(given)
    layer_out = weave(core, after(returned, payload), half_run)
    ffn_sum = far_step(ffn_terms, groups, 0, (given, layer_out))
    qkv_got = after(qkv_got, ffn_sum)
    for bit in range(1, far.bit_length() - 1):
        ffn_sum = far_step(ffn_sum, groups, bit, qkv_got)
    qkv_sum = far_direct(sum_of(qkv_terms[0], qkv_got), groups, ffn_sum)
    (
        input_gradient, query_bias_sum, value_bias_sum, out_bias_sum, first_gain_sum,
        first_shift_sum, down_bias_sum, second_gain_sum, second_shift_sum, up_bias_sum,
    ) = weave(core, given, half_run, features // groups // 2)
    return (
        layer_out,
        input_gradient,
        qkv_sum[:, :width],
        query_bias_sum,
        qkv_sum[:, width : 2 * width],
        qkv_sum[:, 2 * width :],
        value_bias_sum,
        ffn_sum[:, 2 * ff_width :].T,
        out_bias_sum,
        first_gain_sum,
        first_shift_sum,
        ffn_sum[:, ff_width : 2 * ff_width],
        up_bias_sum,
        ffn_sum[:, :ff_width].T,
        down_bias_sum,
        second_gain_sum,
        second_shift_sum,
    )


def solution(mesh):
    rows = P("dp", None)
    in_specs = (
        rows,
        rows,
        rows,
        P(None, "tensor"),
        P("tensor"),
        P(None, "tensor"),
        P(None, "tensor"),
        P("tensor"),
        P("tensor", None),
        P(),
        P(),
        P(),
        P(None, "tensor"),
        P("tensor"),
        P("tensor", None),
        P(),
        P(),
        P(),
        rows,
    )
    spread = P(("dp", "tensor"))
    out_specs = (
        rows,
        rows,
        P("dp", "tensor"),
        spread,
        P("dp", "tensor"),
        P("dp", "tensor"),
        spread,
        P("tensor", "dp"),
        spread,
        spread,
        spread,
        P("dp", "tensor"),
        spread,
        P("tensor", "dp"),
        spread,
        spread,
        spread,
    )
    return jax.shard_map(local, mesh=mesh, in_specs=in_specs, out_specs=out_specs, check_vma=False)
```

```python
import functools
import jax
import jax.numpy as jnp
from jax import lax
from jax.experimental import pallas as pl
from jax.experimental.pallas import tpu as pltpu
from jax.sharding import PartitionSpec as P

HD = 64
LANES = 128
SEG_MAX = 8
FORWARD_ROWS = 512
FORWARD_KEYS = 512
QB = 256
KB = 256
ROW_TILE = 64


EPSILON = 1e-12
MASKED = -1e30
F32 = jnp.float32
BF16 = jnp.bfloat16
SWAP = [(0, 1), (1, 0)]
VMEM_LIMIT = 60 << 20


def swap(values):
    return lax.ppermute(values, "tensor", SWAP)


def nt(a, b):
    return lax.dot_general(a, b, (((1,), (1,)), ((), ())), preferred_element_type=F32)


def nn(a, b):
    return jnp.dot(a, b, preferred_element_type=F32)


def segment_ends(lengths):
    ends, end = [], jnp.int32(0)
    for n in range(lengths.shape[1]):
        end = end + lengths[0, n]
        ends.append(end)
    return ends


def bounds(ends, rows, first, last):
    low, high = jnp.int32(0), jnp.int32(rows)
    for end in ends:
        low = jnp.where(end <= first, jnp.maximum(low, end), low)
        high = jnp.where(end > last, jnp.minimum(high, end), high)
    return low, high


def lane_bounds(ends, rows):
    lane = lax.broadcasted_iota(jnp.int32, (1, LANES), 1)
    start = jnp.full((1, LANES), 2 * rows, jnp.int32)
    stop = jnp.zeros((1, LANES), jnp.int32)
    begin = 0
    for n, end in enumerate(ends):
        start = jnp.where(lane == n, begin, start)
        stop = jnp.where(lane == n, end, stop)
        begin = end
    return start, stop


def key_marks(ends, rows, offset):
    start, stop = lane_bounds(ends, rows)
    pos = lax.broadcasted_iota(jnp.int32, (rows, LANES), 0) + offset
    pos = jnp.where(pos >= rows, pos - rows, pos)
    return ((pos >= start) & (pos < stop)).astype(F32).astype(BF16)


def query_marks(ends, rows, first, count):
    start, stop = lane_bounds(ends, rows)
    lane = lax.broadcasted_iota(jnp.int32, (1, LANES), 1)
    pos = lax.broadcasted_iota(jnp.int32, (count, LANES), 0) + first
    return jnp.where((lane < len(ends)) & ((pos < start) | (pos >= stop)), MASKED, 0.0)


def lane_mask(half):
    lane = lax.broadcasted_iota(jnp.int32, (1, LANES), 1)
    return ((lane // HD) == half).astype(F32).astype(BF16)


def of_pair(h):
    return slice(h // 2 * LANES, (h // 2 + 1) * LANES)


def forward_kernel(
    lengths, core, q_ref, k_ref, v_ref, o_mine, o_other, lse_ref, keys, values_t, mixed, peaks, totals
):
    rows, width = k_ref.shape
    heads = width // HD
    step = pl.program_id(0)
    ends = segment_ends(lengths)
    offset = core[0] * (rows // 2)

    @pl.when(step == 0)
    def _():
        marks = key_marks(ends, rows, offset)
        for p in range(heads // 2):
            keys[p, :, :LANES] = k_ref[:, of_pair(2 * p)]
            keys[p, :, LANES:] = marks
        for block in range(rows // FORWARD_KEYS):
            at = slice(block * FORWARD_KEYS, (block + 1) * FORWARD_KEYS)
            values_t[block] = v_ref[at, :].astype(F32).T.astype(BF16)

    first = lax.rem(step * FORWARD_ROWS + offset, rows)
    low, high = bounds(ends, rows, first, first + FORWARD_ROWS - 1)
    block_low, block_high = low // FORWARD_KEYS, (high + FORWARD_KEYS - 1) // FORWARD_KEYS
    marked = query_marks(ends, rows, first, FORWARD_ROWS).astype(BF16)
    queries = []
    for p in range(heads // 2):
        query = q_ref[:, of_pair(2 * p)] * BF16(HD**-0.5)
        both = [jnp.concatenate([query * lane_mask(n), marked], axis=1) for n in range(2)]
        queries.append(jnp.concatenate(both, axis=0))
    mixed[...] = jnp.zeros_like(mixed)
    peaks[...] = jnp.full_like(peaks, MASKED)
    totals[...] = jnp.zeros_like(totals)

    def block_step(i, carry):
        start = lax.rem(i * FORWARD_KEYS + rows - offset, rows)
        at = pl.ds(pl.multiple_of(start, FORWARD_KEYS), FORWARD_KEYS)
        block = start // FORWARD_KEYS
        made = [nt(keys[p, at, :], queries[p]) for p in range(heads // 2)]
        for p in range(heads // 2):
            scores = made[p]
            row = slice(p, p + 1)
            peak = jnp.maximum(peaks[row, :], jnp.max(scores, axis=0, keepdims=True))
            shrink = jnp.exp(peaks[row, :] - peak)
            weights = jnp.exp(scores - peak)
            peaks[row, :] = peak
            totals[row, :] = totals[row, :] * shrink + jnp.sum(weights, axis=0, keepdims=True)
            part = nn(values_t[block, of_pair(2 * p), :], weights.astype(BF16))
            for n in range(2):
                h = slice((2 * p + n) * HD, (2 * p + n + 1) * HD)
                q = slice(n * FORWARD_ROWS, (n + 1) * FORWARD_ROWS)
                mixed[h, :] = mixed[h, :] * shrink[:, q] + part[n * HD : (n + 1) * HD, q]
        return carry

    lax.fori_loop(block_low, block_high, block_step, 0)
    inverse = 1.0 / totals[...]
    lse = peaks[...] + jnp.log(totals[...])
    for h in range(heads):
        wide = slice(h * HD, (h + 1) * HD)
        p, q = h // 2, slice(h % 2 * FORWARD_ROWS, (h % 2 + 1) * FORWARD_ROWS)
        mixed[wide, :] = mixed[wide, :] * inverse[p : p + 1, q]
        lse_ref[h : h + 1, :] = lse[p : p + 1, q]
    made = mixed[...].T.astype(BF16)
    half = rows // 2
    for n in range(rows // FORWARD_ROWS):
        start = n * FORWARD_ROWS % half

        @pl.when(step == n)
        def _():
            ref = (o_mine, o_other)[n * FORWARD_ROWS // half]
            ref[start : start + FORWARD_ROWS, :] = made


def whole(shape):
    return pl.BlockSpec(shape, lambda *_: (0,) * len(shape))


def attention_forward(lengths, core, query_rows, key_rows, value_rows):
    rows, width = query_rows.shape
    heads = width // HD
    tile = pl.BlockSpec((FORWARD_ROWS, width), lambda i, *_: (i, 0))
    return pl.pallas_call(
        forward_kernel,
        grid_spec=pltpu.PrefetchScalarGridSpec(
            num_scalar_prefetch=2,
            grid=(rows // FORWARD_ROWS,),
            in_specs=[tile, whole((rows, width)), whole((rows, width))],
            out_specs=[whole((rows // 2, width))] * 2
            + [pl.BlockSpec((8, FORWARD_ROWS), lambda i, *_: (0, i))],
            scratch_shapes=[
                pltpu.VMEM((heads // 2, rows, 2 * LANES), BF16),
                pltpu.VMEM((rows // FORWARD_KEYS, width, FORWARD_KEYS), BF16),
                pltpu.VMEM((width, FORWARD_ROWS), F32),
                pltpu.VMEM((8, 2 * FORWARD_ROWS), F32),
                pltpu.VMEM((8, 2 * FORWARD_ROWS), F32),
            ],
        ),
        out_shape=[jax.ShapeDtypeStruct((rows // 2, width), BF16)] * 2
        + [jax.ShapeDtypeStruct((8, rows), F32)],
        cost_estimate=pl.CostEstimate(
            flops=8 * rows * rows * LANES * heads,
            bytes_accessed=8 * rows * width,
            transcendentals=rows * rows * heads // 2,
        ),
        compiler_params=params(),
        name="attend",
    )(lengths, core, query_rows, key_rows, value_rows)


def backward_kernel(
    lengths, core, q_ref, do_mine, do_other, o_mine, o_other, lse_ref, k_ref, v_ref,
    grad_mine, grad_other, sums_ref, keys, values, keys_t, dk_sum, dv_sum, dq_sum
):
    rows, width = k_ref.shape
    heads = width // HD
    step = pl.program_id(0)
    steps = rows // QB
    ends = segment_ends(lengths)
    offset = core[0] * (rows // 2)
    scale = HD**-0.5

    @pl.when(step == 0)
    def _():
        marks = key_marks(ends, rows, offset)
        for p in range(heads // 2):
            keys[p, :, :LANES] = k_ref[:, of_pair(2 * p)]
            keys[p, :, LANES:] = marks
            values[p] = v_ref[:, of_pair(2 * p)]
        for block in range(rows // KB):
            at = slice(block * KB, (block + 1) * KB)
            keys_t[block] = k_ref[at, :].astype(F32).T.astype(BF16)
        dk_sum[...] = jnp.zeros_like(dk_sum)
        dv_sum[...] = jnp.zeros_like(dv_sum)

    first = lax.rem(step * QB + offset, rows)
    low, high = bounds(ends, rows, first, first + QB - 1)
    block_low, block_high = low // KB, (high + KB - 1) // KB
    marked = query_marks(ends, rows, first, QB).astype(BF16)
    early = jnp.full((1, width), step, jnp.int32) < steps // 2
    use_mine = early.astype(F32).astype(BF16)
    use_other = (~early).astype(F32).astype(BF16)
    grad_rows = do_mine[...] * use_mine + do_other[...] * use_other
    mixed_rows = o_mine[...] * use_mine + o_other[...] * use_other
    lane = lax.broadcasted_iota(jnp.int32, (8, LANES), 1)
    row = lax.broadcasted_iota(jnp.int32, (8, LANES), 0)
    by_head = (lane // HD == row).astype(F32).astype(BF16)
    queries, grads, marked_queries, logsums, centres = [], [], [], [], []
    for p in range(heads // 2):
        pair = of_pair(2 * p)
        query = [q_ref[:, pair] * (lane_mask(n) * BF16(scale)) for n in range(2)]
        grad = grad_rows[:, pair]
        exact = grad.astype(F32) * mixed_rows[:, pair].astype(F32)
        high_term = exact.astype(BF16)
        low_term = (exact - high_term.astype(F32)).astype(BF16)
        centre = nt(by_head, high_term) + nt(by_head, low_term)
        centres.append(jnp.concatenate([centre[0:1, :], centre[1:2, :]], axis=1))
        logsums.append(
            jnp.concatenate([lse_ref[2 * p : 2 * p + 1, :], lse_ref[2 * p + 1 : 2 * p + 2, :]], axis=1)
        )
        queries.append(jnp.concatenate(query, axis=0))
        grads.append(jnp.concatenate([grad * lane_mask(n) for n in range(2)], axis=0))
        marked_queries.append(
            jnp.concatenate([queries[p], jnp.concatenate([marked, marked], axis=0)], axis=1)
        )
    dq_sum[...] = jnp.zeros_like(dq_sum)

    def block_step(i, carry):
        start = lax.rem(i * KB + rows - offset, rows)
        at = pl.ds(pl.multiple_of(start, KB), KB)
        block = start // KB
        scores = [nt(keys[p, at, :], marked_queries[p]) for p in range(heads // 2)]
        pulls = [nt(values[p, at, :], grads[p]) for p in range(heads // 2)]
        for p in range(heads // 2):
            weights = jnp.exp(scores[p] - logsums[p])
            pulled = pulls[p]
            dv_sum[at, of_pair(2 * p)] += nn(weights.astype(BF16), grads[p])
            slopes = (weights * (pulled - centres[p])).astype(BF16)
            dk_sum[at, of_pair(2 * p)] += nn(slopes, queries[p])
            part = nn(keys_t[block, of_pair(2 * p), :], slopes)
            for n in range(2):
                h = slice((2 * p + n) * HD, (2 * p + n + 1) * HD)
                dq_sum[h, :] += part[n * HD : (n + 1) * HD, n * QB : (n + 1) * QB]
        return carry

    lax.fori_loop(block_low, block_high, block_step, 0)
    made = (dq_sum[...] * scale).T.astype(BF16)
    half = rows // 2
    for n in range(steps):
        start = n * QB % half

        @pl.when(step == n)
        def _():
            (grad_mine, grad_other)[n * QB // half][start : start + QB, :width] = made

    total = jnp.sum(made.astype(F32), axis=0, keepdims=True)

    @pl.when(step == 0)
    def _():
        sums_ref[...] = jnp.zeros_like(sums_ref)

    sums_ref[0:1, :] += total

    @pl.when(step == steps - 1)
    def _():
        for n, ref in enumerate((grad_mine, grad_other)):
            at = slice(n * half, (n + 1) * half)
            ref[:, width : 2 * width] = dk_sum[at, :].astype(BF16)
            made = dv_sum[at, :].astype(BF16)
            ref[:, 2 * width :] = made
            sums_ref[1:2, :] += jnp.sum(made.astype(F32), axis=0, keepdims=True)


def attention_backward(
    lengths, core, query_rows, key_rows, value_rows, mixed, lse, grad_mine, grad_other
):
    rows, width = query_rows.shape
    heads = width // HD
    steps = rows // QB
    tile = pl.BlockSpec((QB, width), lambda i, *_: (i, 0))
    full = whole((rows, width))
    early = pl.BlockSpec((QB, width), lambda i, *_: (jnp.minimum(i, steps // 2 - 1), 0))
    late = pl.BlockSpec((QB, width), lambda i, *_: (jnp.maximum(i - steps // 2, 0), 0))
    outs = [jax.ShapeDtypeStruct((rows // 2, 3 * width), BF16)] * 2
    outs.append(jax.ShapeDtypeStruct((8, width), F32))
    return pl.pallas_call(
        backward_kernel,
        grid_spec=pltpu.PrefetchScalarGridSpec(
            num_scalar_prefetch=2,
            grid=(steps,),
            in_specs=[
                tile,
                early,
                late,
                early,
                late,
                pl.BlockSpec((8, QB), lambda i, *_: (0, i)),
                full,
                full,
            ],
            out_specs=[whole(o.shape) for o in outs],
            scratch_shapes=[
                pltpu.VMEM((heads // 2, rows, 2 * LANES), BF16),
                pltpu.VMEM((heads // 2, rows, LANES), BF16),
                pltpu.VMEM((rows // KB, width, KB), BF16),
                pltpu.VMEM((rows, width), F32),
                pltpu.VMEM((rows, width), F32),
                pltpu.VMEM((width, QB), F32),
            ],
        ),
        out_shape=outs,
        cost_estimate=pl.CostEstimate(
            flops=20 * rows * rows * LANES * heads,
            bytes_accessed=16 * rows * width,
            transcendentals=rows * rows * heads // 2,
        ),
        compiler_params=params(),
        name="attend_back",
    )(lengths, core, query_rows, grad_mine, grad_other, *mixed, lse, key_rows, value_rows)


def params():
    return pltpu.CompilerParams(vmem_limit_bytes=VMEM_LIMIT)


def cost(flops, moved, transcendentals=0):
    return pl.CostEstimate(flops=flops, bytes_accessed=moved, transcendentals=transcendentals)


def columns_of(slots, core, run_rows, half):
    half_run = run_rows // 2
    run, place = slots // run_rows, slots % run_rows
    held = (place // half_run + core) % 2
    return held * half + run * half_run + place % half_run


def one_hot(column, width, base):
    count = column.shape[1]
    down = jnp.broadcast_to(column, (8, count)).T[:, :1]
    lane = lax.broadcasted_iota(jnp.int32, (count, width), 1) + base
    return (down == lane).astype(F32).astype(BF16)


def intake_kernel(
    run_rows, core, slots, mine_ref, other_ref, q_weight, k_weight, v_weight, q_bias, v_bias,
    x_ref, q_ref, k_ref, v_ref
):
    half = mine_ref.shape[0]
    column = columns_of(slots[...], core[0], run_rows, half)
    rows = nn(one_hot(column, half, 0), mine_ref[...])
    rows = (rows + nn(one_hot(column, half, half), other_ref[...])).astype(BF16)
    x_ref[...] = rows
    q_ref[...] = (nn(rows, q_weight[...]) + q_bias[...]).astype(BF16)
    k_ref[...] = nn(rows, k_weight[...]).astype(BF16)
    v_ref[...] = (nn(rows, v_weight[...]) + v_bias[...]).astype(BF16)


def intake(core, slots, run_rows, mine_rows, other_rows, weights, biases):
    half, features = mine_rows.shape
    rows = 2 * half
    width = weights[0].shape[1]
    count = 512
    blocks = rows // count

    def tile(n):
        return pl.BlockSpec((count, n), lambda i, core: (i, 0))

    return pl.pallas_call(
        functools.partial(intake_kernel, run_rows),
        grid_spec=pltpu.PrefetchScalarGridSpec(
            num_scalar_prefetch=1,
            grid=(blocks,),
            in_specs=[
                pl.BlockSpec(
                    (1, count), lambda i, core: (0, (i + core[0] * (blocks // 2)) % blocks)
                ),
                whole((half, features)),
                whole((half, features)),
            ]
            + [whole((features, width))] * 3
            + [whole((1, width))] * 2,
            out_specs=[tile(features), tile(width), tile(width), tile(width)],
        ),
        out_shape=[jax.ShapeDtypeStruct((rows, features), BF16)]
        + [jax.ShapeDtypeStruct((rows, width), BF16)] * 3,
        cost_estimate=cost(2 * rows * features * (rows + 3 * width), 8 * rows * features),
        compiler_params=params(),
        name="intake",
    )(core, slots, mine_rows, other_rows, *weights, *biases)


def centred(values):
    centre = values - jnp.mean(values, axis=-1, keepdims=True)
    inverse = lax.rsqrt(jnp.mean(centre * centre, axis=-1, keepdims=True) + EPSILON)
    return centre * inverse, inverse


def norm_back(upstream, normed, inverse, gain):
    scaled = upstream * gain
    return inverse * (
        scaled
        - jnp.mean(scaled, axis=-1, keepdims=True)
        - normed * jnp.mean(scaled * normed, axis=-1, keepdims=True)
    )


def add_rows(ref, row, values):
    ref[row : row + 1, :] += jnp.sum(values, axis=0, keepdims=True)


def rows_kernel(
    run_rows, core, x_ref, mixed_mine, mixed_other, slots, cot_mine, cot_other,
    out_bias, first_gain, first_shift, down_bias, second_gain, second_shift, bias_mine, bias_other,
    out_mine, out_other, up_mine, up_other, down_mine, down_other,
    y_out, hb_out, second_out, act_out_mine, act_out_other, du_out_mine, du_out_other, first_out, low_out,
    back_out_mine, back_out_other, sums, up_sums,
    w_out, w_up, w_down, sems, out_sems, hidden, first_inv, total, slope, grad, pulled, biases,
    y_ref, hb_ref, second_ref, act, du, first_ref, low_ref, back
):
    half, features = x_ref.shape
    width = mixed_mine.shape[1]
    chunks, _, chunk = w_up.shape
    per_half = chunks // 2
    tiles = half // ROW_TILE
    copies = [
        pltpu.make_async_copy(out_mine, w_out.at[0], sems.at[0]),
        pltpu.make_async_copy(out_other, w_out.at[1], sems.at[1]),
    ]
    up_copies, down_copies = [], []
    for c in range(chunks):
        up, down = ((up_mine, down_mine), (up_other, down_other))[c // per_half]
        at = pl.ds(c % per_half * chunk, chunk)
        up_copies.append(pltpu.make_async_copy(up.at[:, at], w_up.at[c], sems.at[2 + c]))
        down_copies.append(
            pltpu.make_async_copy(down.at[at, :], w_down.at[c], sems.at[2 + chunks + c])
        )
    outgoing = []

    def send(source, target):
        copy = pltpu.make_async_copy(source, target, out_sems.at[len(outgoing)])
        copy.start()
        outgoing.append(copy)

    for copy in copies:
        copy.start()
    for up, down in zip(up_copies, down_copies):
        up.start()
        down.start()
    out_bias, first_gain, first_shift = out_bias[...], first_gain[...], first_shift[...]
    down_bias, second_gain, second_shift = down_bias[...], second_gain[...], second_shift[...]
    sums[...] = jnp.zeros_like(sums)
    up_sums[...] = jnp.zeros_like(up_sums)

    column = columns_of(slots[...], core[0], run_rows, half)
    grad[...] = nn(one_hot(column, half, 0), cot_mine[...])
    grad[...] += nn(one_hot(column, half, half), cot_other[...])

    def of_chunk(refs, c):
        return refs[c // per_half], pl.ds(c % per_half * chunk, chunk)

    for copy in copies:
        copy.wait()
    total[...] = nn(mixed_mine[...], w_out[0]) + nn(mixed_other[...], w_out[1])

    @pl.loop(0, tiles, unroll=2)
    def _(i):
        at = pl.ds(pl.multiple_of(i * ROW_TILE, ROW_TILE), ROW_TILE)
        normed, inverse = centred(x_ref[at, :].astype(F32) + total[at, :] + out_bias)
        rows = normed * first_gain + first_shift
        hidden[at, :] = rows
        hb_ref[at, :] = rows.astype(BF16)
        first_ref[at, :] = normed
        first_inv[at, :] = inverse

    send(hb_ref, hb_out)

    block = half // 2
    blocks = [slice(r * block, (r + 1) * block) for r in range(2)]
    for c in range(chunks):
        ref, wide = of_chunk((bias_mine, bias_other), c)
        biases[c : c + 1, :] = ref[:, wide]

    def inner_of(c):
        pltpu.make_async_copy(up_mine.at[:, pl.ds(0, chunk)], w_up.at[c], sems.at[2 + c]).wait()
        for at in blocks:
            slope[c, at, :] = nn(hb_ref[at, :], w_up[c]) + biases[pl.ds(c, 1), :]

    def activate(c):
        for at in blocks:
            inner = slope[c, at, :]
            share = 0.5 * (1.0 + lax.erf(inner * 0.7071067811865476))
            density = jnp.exp(-0.5 * inner * inner) * 0.3989422804014327
            act[c, at, :] = (inner * share).astype(BF16)
            slope[c, at, :] = share + inner * density
            total[at, :] += nn(act[c, at, :], w_down[c])

    def down_ready(c):
        source = down_mine.at[pl.ds(0, chunk), :]
        pltpu.make_async_copy(source, w_down.at[c], sems.at[2 + chunks + c]).wait()

    total[...] = jnp.zeros_like(total)
    inner_of(0)

    @pl.loop(0, chunks - 1)
    def _(c):
        down_ready(c)
        inner_of(c + 1)
        activate(c)

    down_ready(chunks - 1)
    activate(chunks - 1)
    for c in range(chunks):
        ref, wide = of_chunk((act_out_mine, act_out_other), c)
        send(act.at[c], ref.at[:, wide])

    @pl.loop(0, tiles, unroll=2)
    def _(i):
        at = pl.ds(pl.multiple_of(i * ROW_TILE, ROW_TILE), ROW_TILE)
        normed, inverse = centred(hidden[at, :] + total[at, :] + down_bias)
        y_ref[at, :] = (normed * second_gain + second_shift).astype(BF16)
        upstream = grad[at, :]
        add_rows(sums, 4, upstream * normed)
        add_rows(sums, 5, upstream)
        back = norm_back(upstream, normed, inverse, second_gain)
        add_rows(sums, 3, back)
        second_ref[at, :] = back.astype(BF16)
        grad[at, :] = back

    send(y_ref, y_out)
    send(second_ref, second_out)
    def pull(c):
        for at in blocks:
            pulled[c % 2, at, :] = nt(second_ref[at, :], w_down[c])

    def push(c):
        row = (c // per_half ^ core[0]) * per_half + c % per_half
        for at in blocks:
            low = (pulled[c % 2, at, :] * slope[c, at, :]).astype(BF16)
            du[c, at, :] = low
            up_sums[pl.ds(row, 1), :] += jnp.sum(low.astype(F32), axis=0, keepdims=True)
            grad[at, :] += nt(low, w_up[c])

    pull(0)

    @pl.loop(0, chunks - 1)
    def _(c):
        pull(c + 1)
        push(c)

    push(chunks - 1)
    for c in range(chunks):
        ref, wide = of_chunk((du_out_mine, du_out_other), c)
        send(du.at[c], ref.at[:, wide])

    @pl.loop(0, tiles, unroll=2)
    def _(i):
        at = pl.ds(pl.multiple_of(i * ROW_TILE, ROW_TILE), ROW_TILE)
        upstream, normed = grad[at, :], first_ref[at, :]
        add_rows(sums, 1, upstream * normed)
        add_rows(sums, 2, upstream)
        back = norm_back(upstream, normed, first_inv[at, :], first_gain)
        add_rows(sums, 0, back)
        first_ref[at, :] = back

    send(first_ref, first_out)
    low_ref[...] = first_ref[...].astype(BF16)
    send(low_ref, low_out)
    for n, out in enumerate((back_out_mine, back_out_other)):
        back[n] = nt(low_ref[...], w_out[n]).astype(BF16)
        send(back.at[n], out)
    for copy in outgoing:
        copy.wait()


def row_pass(
    core, inputs, mixed, mixed_other, slots, run_rows, cot_mine, cot_other, vectors,
    out_mine, out_other, up_mine, up_other, down_mine, down_other
):
    half, features = cot_mine.shape
    width = mixed.shape[1]
    chunk = features
    chunks = 2 * up_mine.shape[1] // chunk
    any_space = pl.BlockSpec(memory_space=pl.ANY)

    def low(*shape):
        return jax.ShapeDtypeStruct(shape, BF16)

    outs = [
        low(half, features),
        low(half, features),
        low(half, features),
        low(half, up_mine.shape[1]),
        low(half, up_mine.shape[1]),
        low(half, up_mine.shape[1]),
        low(half, up_mine.shape[1]),
        jax.ShapeDtypeStruct((half, features), F32),
        low(half, features),
        low(half, width),
        low(half, width),
        jax.ShapeDtypeStruct((8, features), F32),
        jax.ShapeDtypeStruct((chunks, chunk), F32),
    ]
    return pl.pallas_call(
        functools.partial(rows_kernel, run_rows),
        grid_spec=pltpu.PrefetchScalarGridSpec(
            num_scalar_prefetch=1,
            grid=(1,),
            in_specs=[
                whole((half, features)),
                whole((half, width)),
                whole((half, width)),
                pl.BlockSpec((1, half), lambda i, core: (0, core[0])),
                whole((half, features)),
                whole((half, features)),
            ]
            + [whole(v.shape) for v in vectors]
            + [any_space] * 6,
            out_specs=[any_space] * (len(outs) - 2) + [whole(o.shape) for o in outs[-2:]],
            scratch_shapes=[
                pltpu.VMEM((2, width, features), BF16),
                pltpu.VMEM((chunks, features, chunk), BF16),
                pltpu.VMEM((chunks, chunk, features), BF16),
                pltpu.SemaphoreType.DMA((2 + 2 * chunks,)),
                pltpu.SemaphoreType.DMA((7 + 2 * chunks,)),
                pltpu.VMEM((half, features), F32),
                pltpu.VMEM((half, 1), F32),
                pltpu.VMEM((half, features), F32),
                pltpu.VMEM((chunks, half, chunk), F32),
                pltpu.VMEM((half, features), F32),
                pltpu.VMEM((2, half, chunk), F32),
                pltpu.VMEM((chunks, chunk), F32),
                pltpu.VMEM((half, features), BF16),
                pltpu.VMEM((half, features), BF16),
                pltpu.VMEM((half, features), BF16),
                pltpu.VMEM((chunks, half, chunk), BF16),
                pltpu.VMEM((chunks, half, chunk), BF16),
                pltpu.VMEM((half, features), F32),
                pltpu.VMEM((half, features), BF16),
                pltpu.VMEM((2, half, width), BF16),
            ],
        ),
        out_shape=outs,
        cost_estimate=cost(
            8 * half * features * chunk * chunks + 10 * half * features * features,
            30 * half * features + 8 * features * chunk * chunks,
            half * chunk * chunks,
        ),
        compiler_params=params(),
        name="row_pass",
    )(
        core, inputs, mixed, mixed_other, slots, cot_mine, cot_other, *vectors,
        out_mine, out_other, up_mine, up_other, down_mine, down_other
    )


def after(values, others):
    return lax.optimization_barrier((values, others))[0]


def near_groups(groups):
    near = 4 if groups % 4 == 0 else 1
    return near, groups // near


def tn(left, right):
    return lax.dot_general(left, right, (((0,), (0,)), ((), ())), preferred_element_type=F32)


def by_place(terms, groups):
    near, far = near_groups(groups)
    place = lax.axis_index("dp") % near
    terms = terms.reshape(far, near, terms.shape[0] // groups, terms.shape[1])
    return [lax.dynamic_index_in_dim(terms, place ^ n, 1, keepdims=False) for n in range(near)]


def gradient_kernel(chunks, near, share, halving, me, *refs):
    operands, outs, acc = refs[: 4 * len(chunks)], refs[4 * len(chunks) : -1], refs[-1]
    step = pl.program_id(0)
    first, column = 0, 0
    for n, (chunk, count) in enumerate(chunks):
        left, left_more, right, right_more = operands[4 * n : 4 * n + 4]

        @pl.when((step >= first) & (step < first + count))
        def _():
            acc[:, :chunk] = tn(left[...], right[...])
            acc[:, :chunk] += tn(left_more[...], right_more[...])
            at = pl.ds(pl.multiple_of(column + (step - first) * chunk, LANES), chunk)

            def place(out, place):
                for f in range(out.shape[0]):
                    row = share * (f * near + (me[0] ^ place))
                    row = pl.ds(pl.multiple_of(row, 16), share)
                    out[f, :, at] = acc[row, :chunk].astype(out.dtype)

            if halving:
                for out, (a, b) in zip(outs, ((0, 3 - halving), (halving, 3))):
                    place(out.at[0], a)
                    place(out.at[1], b)
            else:
                for m, out in enumerate(outs):
                    place(out, m)

        first += count
        column += count * chunk


def gradients(pieces, groups, halving=0):
    near, far = near_groups(groups)
    features = pieces[0][0][0].shape[1]
    share = features // groups
    if near != 4 or share % 16 != 0:

        def rows_of(left, rows):
            return lax.slice_in_dim(left[0], left[1] * rows, (left[1] + 1) * rows, axis=0)

        terms = [
            tn(rows_of(p[0], p[2].shape[0]), p[2]) + tn(rows_of(p[1], p[3].shape[0]), p[3])
            for p in pieces
        ]
        made = [t.astype(BF16) for t in by_place(jnp.concatenate(terms, axis=1), groups)]
        if halving:
            made = [
                jnp.stack([made[0], made[3 - halving]]), jnp.stack([made[halving], made[3]])
            ]
        return made
    in_specs, operands, chunks, base, columns = [], [], [], 0, 0
    for left, left_more, right, right_more in pieces:
        rows = right.shape[0]
        chunk = min(features, right.shape[1])
        if right.shape[1] % chunk:
            chunk = right.shape[1] // 3
        count = right.shape[1] // chunk

        def at(j, me, base=base, count=count):
            return 0, jnp.clip(j - base, 0, count - 1)

        for array, block in (left, left_more):
            in_specs.append(
                pl.BlockSpec((rows, features), lambda j, me, block=block: (block, 0))
            )
            operands.append(array)
        in_specs += [pl.BlockSpec((rows, chunk), at)] * 2
        operands += [right, right_more]
        chunks.append((chunk, count))
        base += count
        columns += count * chunk
    if halving:
        outs = [jax.ShapeDtypeStruct((2, far, share, columns), BF16)] * 2
    else:
        outs = [jax.ShapeDtypeStruct((far, share, columns), BF16)] * near
    return pl.pallas_call(
        functools.partial(gradient_kernel, chunks, near, share, halving),
        grid_spec=pltpu.PrefetchScalarGridSpec(
            num_scalar_prefetch=1,
            grid=(base,),
            in_specs=in_specs,
            out_specs=[whole(o.shape) for o in outs],
            scratch_shapes=[pltpu.VMEM((features, features), F32)],
        ),
        out_shape=outs,
        cost_estimate=cost(4 * rows * features * columns, 8 * rows * features + 4 * features * columns),
        compiler_params=params(),
        name="gradients",
    )((lax.axis_index("dp") % near).reshape(1), *operands)


def pairs(groups, distance):
    return [(i, i ^ distance) for i in range(groups)]


def far_halves(total, groups, bit):
    total = total.reshape(-1, 2, *total.shape[1:])
    side = (lax.axis_index("dp") // near_groups(groups)[0] >> bit) & 1
    kept = lax.dynamic_index_in_dim(total, side, 1, keepdims=False)
    return kept, lax.dynamic_index_in_dim(total, 1 - side, 1, keepdims=False).astype(BF16)


def far_step(halves, groups, bit, first=()):
    near, far = near_groups(groups)
    kept, sent = halves
    got = after(lax.ppermute(sent, "dp", pairs(groups, near << bit)), first)
    total = kept.astype(F32) + got.astype(F32)
    return far_halves(total, groups, bit + 1) if 2 << bit < far else total[0]


def far_direct(total, groups, first=()):
    near, far = near_groups(groups)
    run = lax.axis_index("dp") // near
    kept = lax.dynamic_index_in_dim(total, run, 0, keepdims=False)
    got = []
    for step in range(1, far):
        sent = lax.dynamic_index_in_dim(total, run ^ step, 0, keepdims=False).astype(BF16)
        got.append(lax.ppermute(sent, "dp", pairs(groups, step * near)))
    return sum_of(kept, after(got, first))


def near_sends(terms, groups):
    return [lax.ppermute(t, "dp", pairs(groups, n + 1)) for n, t in enumerate(terms)]


def sum_of(kept, got):
    kept = kept.astype(F32)
    for term in got:
        kept = kept + term.astype(F32)
    return kept


def input_kernel(first_ref, mine_ref, other_ref, *refs):
    weights, out_ref = refs[:-1], refs[-1]
    total = first_ref[...]
    width = weights[0].shape[1]
    for n, weight in enumerate(weights):
        rows = (mine_ref, other_ref)[n // 3]
        total = total + nt(rows[:, n % 3 * width : (n % 3 + 1) * width], weight[...])
    out_ref[...] = total.astype(BF16)


def input_rows(first_grad, mine_rows, other_rows, weights):
    half, features = first_grad.shape
    wide = other_rows.shape[1]
    count = 512

    def tile(n):
        return pl.BlockSpec((count, n), lambda i: (i, 0))

    return pl.pallas_call(
        input_kernel,
        grid=(half // count,),
        in_specs=[tile(features), tile(wide), tile(wide)] + [whole(w.shape) for w in weights],
        out_specs=tile(features),
        out_shape=jax.ShapeDtypeStruct((half, features), BF16),
        cost_estimate=cost(4 * half * features * wide, 8 * half * features + 4 * features * wide),
        compiler_params=params(),
        name="input_rows",
    )(first_grad, mine_rows, other_rows, *weights)


def route_kernel(share, has_extra, core, slots_mine, slots_other, mine_ref, other_ref, *refs):
    out_ref = refs[-1]
    groups, run = out_ref.shape[0], mine_ref.shape[0] // out_ref.shape[0]
    half = mine_ref.shape[0]
    row = lax.broadcasted_iota(jnp.int32, (half, half), 0)
    column_mine = columns_of(slots_mine[...], core[0], 2 * run, half)
    column_other = columns_of(slots_other[...], core[0], 2 * run, half)
    put_mine = (column_mine == row).astype(F32).astype(BF16)
    put_other = (column_other == row).astype(F32).astype(BF16)
    rows = (nn(put_mine, mine_ref[...]) + nn(put_other, other_ref[...])).astype(BF16)
    out_ref[:, :run, :] = rows.reshape(groups, run, rows.shape[1])
    if has_extra:
        sums, up_sums, qv_sums, wide, wide_up = refs[:5]
        features = sums.shape[1]
        width = qv_sums.shape[1]
        wide[...] = jnp.zeros_like(wide)
        wide_up[...] = jnp.zeros_like(wide_up)
        wide[:, :features] = sums[...]
        wide_up[:4, :features] = up_sums[...]
        at = pl.ds(pl.multiple_of(core[0] * width, LANES), width)
        wide[6:8, at] = qv_sums[:2, :]
        for g in range(groups):
            block = wide[:, share * g : share * g + LANES]
            start = 4 * share * g
            blocks = [block]
            parts = []
            for r in range(4):
                line = (start + share * r) // features
                lane = (start + share * r) % features
                parts.append(wide_up[line : line + 1, lane : lane + LANES])
            blocks.append(jnp.concatenate(parts + [jnp.zeros((4, LANES), F32)], axis=0))
            for b, rest in enumerate(blocks):
                for piece in range(3):
                    term = rest.astype(BF16)
                    rest = rest - term.astype(F32)
                    q = 2 * piece + b
                    out_ref[g, run : run + 8, q * LANES : (q + 1) * LANES] = term


def route(core, slots, mine_rows, other_rows, groups, extra=None):
    half, features = mine_rows.shape
    run = half // groups
    share = features // groups
    extra = extra or ()
    args = [core, slots, slots, mine_rows, other_rows, *extra]
    in_specs = [
        pl.BlockSpec((1, half), lambda i, core: (0, core[0])),
        pl.BlockSpec((1, half), lambda i, core: (0, 1 - core[0])),
    ] + [whole(a.shape) for a in args[3:]]
    scratch = [pltpu.VMEM((8, features + LANES), F32)] * 2 if extra else []
    shape = (groups, run + (8 if extra else 0), features)

    def kernel(*refs):
        ins, (out_ref, *more) = refs[: len(args)], refs[len(args) :]
        route_kernel(share, len(extra) > 0, *ins, *more, out_ref)

    return pl.pallas_call(
        kernel,
        grid_spec=pltpu.PrefetchScalarGridSpec(
            num_scalar_prefetch=1,
            grid=(1,),
            in_specs=in_specs,
            out_specs=whole(shape),
            scratch_shapes=scratch,
        ),
        out_shape=jax.ShapeDtypeStruct(shape, BF16),
        cost_estimate=cost(4 * half * half * features, 6 * half * features),
        compiler_params=params(),
        name="route",
    )(*args)


def exchange(values):
    return lax.all_to_all(values, "dp", split_axis=0, concat_axis=0, tiled=True)


def weave_kernel(core, mine_ref, other_ref, out_ref, *outs):
    run = out_ref.shape[2]
    out_ref[:, core[0]] = mine_ref[:, :run, :]
    out_ref[:, 1 - core[0]] = other_ref[:, :run, :]
    if not outs:
        return
    pieces = []
    for q in range(6):
        at = slice(q * LANES, (q + 1) * LANES)
        both = [jnp.sum(r[:, run:, at].astype(F32), axis=0) for r in (mine_ref, other_ref)]
        pieces.append(both[0] + both[1])
    first, more = [pieces[4 + b] + pieces[2 + b] + pieces[b] for b in range(2)]
    each = outs[0].shape[1]
    share = 2 * each
    low = core[0] == 0

    def half_of(values):
        return jnp.where(low, values[:, :each], values[:, each:share])

    for out, row in zip(outs[:8], (6, 7, 0, 1, 2, 3, 4, 5)):
        out[...] = half_of(first[row : row + 1, :])
    pair = jnp.where(low, more[0:2, :share], more[2:4, :share])
    outs[8][:, :share] = pair[0:1, :]
    outs[8][:, share:] = pair[1:2, :]


def weave(core, part, rows_of_core, small=0):
    groups, _, features = part.shape
    outs = [jax.ShapeDtypeStruct((groups, 2, rows_of_core, features), BF16)]
    if small:
        outs += [jax.ShapeDtypeStruct((1, small), F32)] * 8
        outs.append(jax.ShapeDtypeStruct((1, 4 * small), F32))
    rows, *more = pl.pallas_call(
        weave_kernel,
        grid_spec=pltpu.PrefetchScalarGridSpec(
            num_scalar_prefetch=1,
            grid=(1,),
            in_specs=[whole(part.shape)] * 2,
            out_specs=[whole(o.shape) for o in outs],
        ),
        out_shape=outs,
        cost_estimate=cost(1, 1),
        compiler_params=params(),
        name="weave",
    )(core, part, swap(part))
    rows = rows.reshape(groups * 2 * rows_of_core, features)
    return (rows, *[m.reshape(-1) for m in more]) if small else rows


def local(
    tokens,
    token_slot,
    seq_lengths,
    query_weight,
    query_bias,
    key_weight,
    value_weight,
    value_bias,
    out_weight,
    out_bias,
    first_gain,
    first_shift,
    up_weight,
    up_bias,
    down_weight,
    down_bias,
    second_gain,
    second_shift,
    cotangent,
):
    groups = lax.axis_size("dp")
    row_count, features = tokens.shape
    run_rows = row_count // groups
    half_run = run_rows // 2
    half = row_count // 2
    mine = lax.axis_index("tensor")
    core = mine.reshape(1)
    near, far = near_groups(groups)

    def part_of(values):
        return lax.dynamic_slice_in_dim(
            values.reshape(groups, run_rows, features), mine * half_run, half_run, 1
        )

    cot_part = part_of(cotangent)
    token_rows = after(exchange(part_of(tokens)), cot_part).reshape(half, features)
    cot_raw = exchange(cot_part).reshape(half, features)

    qkv_weights = [query_weight, key_weight, value_weight]
    out_other, up_other, down_other = swap(out_weight), swap(up_weight), swap(down_weight)
    vectors = [out_bias, first_gain, first_shift, down_bias, second_gain, second_shift]
    bias_other = swap(up_bias)
    vectors = [v.reshape(1, -1) for v in vectors + [up_bias, bias_other]]
    qkv_other = [swap(w) for w in qkv_weights]
    biases = [query_bias.reshape(1, -1), value_bias.reshape(1, -1)]
    early = (out_other, up_other, down_other, qkv_other)
    token_rows, vectors, biases, early = lax.optimization_barrier(
        (token_rows, vectors, biases, early)
    )
    out_other, up_other, down_other, qkv_other = early
    token_got = swap(token_rows)

    inputs, query_rows, key_rows, value_rows = intake(
        core, token_slot, run_rows, token_rows, token_got, qkv_weights,
        biases,
    )
    mixed_mine, mixed_theirs, logsum = attention_forward(seq_lengths, core, query_rows, key_rows, value_rows)
    cot_rows = after(cot_raw, mixed_mine)
    mixed_other = swap(mixed_theirs)
    (
        output_low, hidden_low, second_low, act_mine, act_other, inner_mine, inner_other, first_grad,
        first_low, mixed_grad_mine, mixed_grad_other, sums, up_sums,
    ) = row_pass(
        core, inputs, mixed_mine, mixed_other, token_slot, run_rows, cot_rows, swap(cot_rows), vectors,
        out_weight, out_other, up_weight, up_other, down_weight, down_other,
    )
    mixed_grad_got = swap(mixed_grad_other)

    width = query_weight.shape[1]
    ff_width = up_weight.shape[1]
    output_got = swap(output_low)
    second_low, hidden_low, first_low, act_other, inner_other = after(
        (second_low, hidden_low, first_low, act_other, inner_other), output_got
    )
    second_got, act_got = swap(second_low), swap(act_other)
    hidden_got, inner_got = swap(hidden_low), swap(inner_other)
    first_got = swap(first_low)
    returned = route(core, token_slot, output_low, output_got, groups)
    kept, sent = [], []
    left = gradients([((second_low, 0), (second_got, 0), act_mine, act_got)], groups, near == 4)
    right = [
        ((hidden_low, 0), (hidden_got, 0), inner_mine, inner_got),
        ((first_low, 0), (first_got, 0), mixed_mine, mixed_theirs),
    ]
    right = gradients(right, groups, 2 * (near == 4))
    if near == 4:
        kept, sent = [left[0], right[0]], [left[1], right[1]]
    else:
        kept, sent = [left[0][None], right[0][None]], []
    mixed_grad_mine, mixed_grad_got = after(
        (mixed_grad_mine, mixed_grad_got), (returned, kept, sent)
    )
    returned = exchange(returned)
    got = [lax.ppermute(v, "dp", pairs(groups, n + 1)) for n, v in enumerate(sent)]
    qkv_mine, qkv_theirs, qv_sums = attention_backward(
        seq_lengths, core, query_rows, key_rows, value_rows, (mixed_mine, mixed_theirs), logsum,
        mixed_grad_mine, mixed_grad_got,
    )
    other_grad = swap(qkv_theirs)
    qkv_terms = gradients([((inputs, 0), (inputs, 1), qkv_mine, qkv_theirs)], groups)
    got, returned = after((got, returned), qkv_terms)
    both = [k.astype(F32) + g.astype(F32) for k, g in zip(kept, got)]
    sent = [b[1].astype(BF16) for b in both]
    kept = [b[0] for b in both] if got else [k[0] for k in kept]
    first_grad = after(first_grad, (qkv_terms, sent, kept))
    qkv_got = near_sends(qkv_terms[1:], groups)
    got = [lax.ppermute(v, "dp", pairs(groups, 2 - n)) for n, v in enumerate(sent)]
    input_low = input_rows(
        first_grad, qkv_mine, other_grad, qkv_weights + qkv_other
    )
    given = route(core, token_slot, input_low, swap(input_low), groups, (sums, up_sums, qv_sums))
    got = after(got, given)
    if got:
        kept = [k + g.astype(F32) for k, g in zip(kept, got)]
    ffn_terms = far_halves(jnp.concatenate(kept, axis=2), groups, 0)
    payload, given = given, exchange(given)
    layer_out = weave(core, after(returned, payload), half_run)
    ffn_sum = far_step(ffn_terms, groups, 0, (given, layer_out))
    qkv_got = after(qkv_got, ffn_sum)
    for bit in range(1, far.bit_length() - 1):
        ffn_sum = far_step(ffn_sum, groups, bit, qkv_got)
    qkv_sum = far_direct(sum_of(qkv_terms[0], qkv_got), groups, ffn_sum)
    (
        input_gradient, query_bias_sum, value_bias_sum, out_bias_sum, first_gain_sum,
        first_shift_sum, down_bias_sum, second_gain_sum, second_shift_sum, up_bias_sum,
    ) = weave(core, given, half_run, features // groups // 2)
    return (
        layer_out,
        input_gradient,
        qkv_sum[:, :width],
        query_bias_sum,
        qkv_sum[:, width : 2 * width],
        qkv_sum[:, 2 * width :],
        value_bias_sum,
        ffn_sum[:, 2 * ff_width :].T,
        out_bias_sum,
        first_gain_sum,
        first_shift_sum,
        ffn_sum[:, ff_width : 2 * ff_width],
        up_bias_sum,
        ffn_sum[:, :ff_width].T,
        down_bias_sum,
        second_gain_sum,
        second_shift_sum,
    )


def solution(mesh):
    rows = P("dp", None)
    in_specs = (
        rows,
        rows,
        rows,
        P(None, "tensor"),
        P("tensor"),
        P(None, "tensor"),
        P(None, "tensor"),
        P("tensor"),
        P("tensor", None),
        P(),
        P(),
        P(),
        P(None, "tensor"),
        P("tensor"),
        P("tensor", None),
        P(),
        P(),
        P(),
        rows,
    )
    spread = P(("dp", "tensor"))
    out_specs = (
        rows,
        rows,
        P("dp", "tensor"),
        spread,
        P("dp", "tensor"),
        P("dp", "tensor"),
        spread,
        P("tensor", "dp"),
        spread,
        spread,
        spread,
        P("dp", "tensor"),
        spread,
        P("tensor", "dp"),
        spread,
        spread,
        spread,
    )
    return jax.shard_map(local, mesh=mesh, in_specs=in_specs, out_specs=out_specs, check_vma=False)
```

```python
import functools
import jax
import jax.numpy as jnp
from jax import lax
from jax.experimental import pallas as pl
from jax.experimental.pallas import tpu as pltpu
from jax.sharding import PartitionSpec as P

HD = 64
LANES = 128
SEG_MAX = 8
FORWARD_ROWS = 512
FORWARD_KEYS = 512
QB = 256
KB = 256
ROW_TILE = 64


EPSILON = 1e-12
MASKED = -1e30
F32 = jnp.float32
BF16 = jnp.bfloat16
SWAP = [(0, 1), (1, 0)]
VMEM_LIMIT = 60 << 20


def swap(values):
    return lax.ppermute(values, "tensor", SWAP)


def nt(a, b):
    return lax.dot_general(a, b, (((1,), (1,)), ((), ())), preferred_element_type=F32)


def nn(a, b):
    return jnp.dot(a, b, preferred_element_type=F32)


def segment_ends(lengths):
    ends, end = [], jnp.int32(0)
    for n in range(lengths.shape[1]):
        end = end + lengths[0, n]
        ends.append(end)
    return ends


def bounds(ends, rows, first, last):
    low, high = jnp.int32(0), jnp.int32(rows)
    for end in ends:
        low = jnp.where(end <= first, jnp.maximum(low, end), low)
        high = jnp.where(end > last, jnp.minimum(high, end), high)
    return low, high


def lane_bounds(ends, rows):
    lane = lax.broadcasted_iota(jnp.int32, (1, LANES), 1)
    start = jnp.full((1, LANES), 2 * rows, jnp.int32)
    stop = jnp.zeros((1, LANES), jnp.int32)
    begin = 0
    for n, end in enumerate(ends):
        start = jnp.where(lane == n, begin, start)
        stop = jnp.where(lane == n, end, stop)
        begin = end
    return start, stop


def key_marks(ends, rows, offset):
    start, stop = lane_bounds(ends, rows)
    pos = lax.broadcasted_iota(jnp.int32, (rows, LANES), 0) + offset
    pos = jnp.where(pos >= rows, pos - rows, pos)
    return ((pos >= start) & (pos < stop)).astype(F32).astype(BF16)


def query_marks(ends, rows, first, count):
    start, stop = lane_bounds(ends, rows)
    lane = lax.broadcasted_iota(jnp.int32, (1, LANES), 1)
    pos = lax.broadcasted_iota(jnp.int32, (count, LANES), 0) + first
    return jnp.where((lane < len(ends)) & ((pos < start) | (pos >= stop)), MASKED, 0.0)


def lane_mask(half):
    lane = lax.broadcasted_iota(jnp.int32, (1, LANES), 1)
    return ((lane // HD) == half).astype(F32).astype(BF16)


def of_pair(h):
    return slice(h // 2 * LANES, (h // 2 + 1) * LANES)


def forward_kernel(
    lengths, core, q_ref, k_ref, v_ref, o_mine, o_other, lse_ref, keys, values_t, mixed, peaks, totals
):
    rows, width = k_ref.shape
    heads = width // HD
    step = pl.program_id(0)
    ends = segment_ends(lengths)
    offset = core[0] * (rows // 2)

    @pl.when(step == 0)
    def _():
        marks = key_marks(ends, rows, offset)
        for p in range(heads // 2):
            keys[p, :, :LANES] = k_ref[:, of_pair(2 * p)]
            keys[p, :, LANES:] = marks
        for block in range(rows // FORWARD_KEYS):
            at = slice(block * FORWARD_KEYS, (block + 1) * FORWARD_KEYS)
            values_t[block] = v_ref[at, :].astype(F32).T.astype(BF16)

    first = lax.rem(step * FORWARD_ROWS + offset, rows)
    low, high = bounds(ends, rows, first, first + FORWARD_ROWS - 1)
    block_low, block_high = low // FORWARD_KEYS, (high + FORWARD_KEYS - 1) // FORWARD_KEYS
    marked = query_marks(ends, rows, first, FORWARD_ROWS).astype(BF16)
    queries = []
    for p in range(heads // 2):
        query = q_ref[:, of_pair(2 * p)] * BF16(HD**-0.5)
        both = [jnp.concatenate([query * lane_mask(n), marked], axis=1) for n in range(2)]
        queries.append(jnp.concatenate(both, axis=0))
    mixed[...] = jnp.zeros_like(mixed)
    peaks[...] = jnp.full_like(peaks, MASKED)
    totals[...] = jnp.zeros_like(totals)

    def block_step(i, carry):
        start = lax.rem(i * FORWARD_KEYS + rows - offset, rows)
        at = pl.ds(pl.multiple_of(start, FORWARD_KEYS), FORWARD_KEYS)
        block = start // FORWARD_KEYS
        made = [nt(keys[p, at, :], queries[p]) for p in range(heads // 2)]
        for p in range(heads // 2):
            scores = made[p]
            row = slice(p, p + 1)
            peak = jnp.maximum(peaks[row, :], jnp.max(scores, axis=0, keepdims=True))
            shrink = jnp.exp(peaks[row, :] - peak)
            weights = jnp.exp(scores - peak)
            peaks[row, :] = peak
            totals[row, :] = totals[row, :] * shrink + jnp.sum(weights, axis=0, keepdims=True)
            part = nn(values_t[block, of_pair(2 * p), :], weights.astype(BF16))
            for n in range(2):
                h = slice((2 * p + n) * HD, (2 * p + n + 1) * HD)
                q = slice(n * FORWARD_ROWS, (n + 1) * FORWARD_ROWS)
                mixed[h, :] = mixed[h, :] * shrink[:, q] + part[n * HD : (n + 1) * HD, q]
        return carry

    lax.fori_loop(block_low, block_high, block_step, 0)
    inverse = 1.0 / totals[...]
    lse = peaks[...] + jnp.log(totals[...])
    for h in range(heads):
        wide = slice(h * HD, (h + 1) * HD)
        p, q = h // 2, slice(h % 2 * FORWARD_ROWS, (h % 2 + 1) * FORWARD_ROWS)
        mixed[wide, :] = mixed[wide, :] * inverse[p : p + 1, q]
        lse_ref[h : h + 1, :] = lse[p : p + 1, q]
    made = mixed[...].T.astype(BF16)
    half = rows // 2
    for n in range(rows // FORWARD_ROWS):
        start = n * FORWARD_ROWS % half

        @pl.when(step == n)
        def _():
            ref = (o_mine, o_other)[n * FORWARD_ROWS // half]
            ref[start : start + FORWARD_ROWS, :] = made


def whole(shape):
    return pl.BlockSpec(shape, lambda *_: (0,) * len(shape))


def attention_forward(lengths, core, query_rows, key_rows, value_rows):
    rows, width = query_rows.shape
    heads = width // HD
    tile = pl.BlockSpec((FORWARD_ROWS, width), lambda i, *_: (i, 0))
    return pl.pallas_call(
        forward_kernel,
        grid_spec=pltpu.PrefetchScalarGridSpec(
            num_scalar_prefetch=2,
            grid=(rows // FORWARD_ROWS,),
            in_specs=[tile, whole((rows, width)), whole((rows, width))],
            out_specs=[whole((rows // 2, width))] * 2
            + [pl.BlockSpec((8, FORWARD_ROWS), lambda i, *_: (0, i))],
            scratch_shapes=[
                pltpu.VMEM((heads // 2, rows, 2 * LANES), BF16),
                pltpu.VMEM((rows // FORWARD_KEYS, width, FORWARD_KEYS), BF16),
                pltpu.VMEM((width, FORWARD_ROWS), F32),
                pltpu.VMEM((8, 2 * FORWARD_ROWS), F32),
                pltpu.VMEM((8, 2 * FORWARD_ROWS), F32),
            ],
        ),
        out_shape=[jax.ShapeDtypeStruct((rows // 2, width), BF16)] * 2
        + [jax.ShapeDtypeStruct((8, rows), F32)],
        cost_estimate=pl.CostEstimate(
            flops=8 * rows * rows * LANES * heads,
            bytes_accessed=8 * rows * width,
            transcendentals=rows * rows * heads // 2,
        ),
        compiler_params=params(),
        name="attend",
    )(lengths, core, query_rows, key_rows, value_rows)


def backward_kernel(
    lengths, core, q_ref, do_mine, do_other, o_mine, o_other, lse_ref, k_ref, v_ref,
    grad_mine, grad_other, sums_ref, keys, values, keys_t, dk_sum, dv_sum, dq_sum
):
    rows, width = k_ref.shape
    heads = width // HD
    step = pl.program_id(0)
    steps = rows // QB
    ends = segment_ends(lengths)
    offset = core[0] * (rows // 2)
    scale = HD**-0.5

    @pl.when(step == 0)
    def _():
        marks = key_marks(ends, rows, offset)
        for p in range(heads // 2):
            keys[p, :, :LANES] = k_ref[:, of_pair(2 * p)]
            keys[p, :, LANES:] = marks
            values[p] = v_ref[:, of_pair(2 * p)]
        for block in range(rows // KB):
            at = slice(block * KB, (block + 1) * KB)
            keys_t[block] = k_ref[at, :].astype(F32).T.astype(BF16)
        dk_sum[...] = jnp.zeros_like(dk_sum)
        dv_sum[...] = jnp.zeros_like(dv_sum)

    first = lax.rem(step * QB + offset, rows)
    low, high = bounds(ends, rows, first, first + QB - 1)
    block_low, block_high = low // KB, (high + KB - 1) // KB
    marked = query_marks(ends, rows, first, QB).astype(BF16)
    early = jnp.full((1, width), step, jnp.int32) < steps // 2
    use_mine = early.astype(F32).astype(BF16)
    use_other = (~early).astype(F32).astype(BF16)
    grad_rows = do_mine[...] * use_mine + do_other[...] * use_other
    mixed_rows = o_mine[...] * use_mine + o_other[...] * use_other
    lane = lax.broadcasted_iota(jnp.int32, (8, LANES), 1)
    row = lax.broadcasted_iota(jnp.int32, (8, LANES), 0)
    by_head = (lane // HD == row).astype(F32).astype(BF16)
    queries, grads, marked_queries, logsums, centres = [], [], [], [], []
    for p in range(heads // 2):
        pair = of_pair(2 * p)
        query = [q_ref[:, pair] * (lane_mask(n) * BF16(scale)) for n in range(2)]
        grad = grad_rows[:, pair]
        exact = grad.astype(F32) * mixed_rows[:, pair].astype(F32)
        high_term = exact.astype(BF16)
        low_term = (exact - high_term.astype(F32)).astype(BF16)
        centre = nt(by_head, high_term) + nt(by_head, low_term)
        centres.append(jnp.concatenate([centre[0:1, :], centre[1:2, :]], axis=1))
        logsums.append(
            jnp.concatenate([lse_ref[2 * p : 2 * p + 1, :], lse_ref[2 * p + 1 : 2 * p + 2, :]], axis=1)
        )
        queries.append(jnp.concatenate(query, axis=0))
        grads.append(jnp.concatenate([grad * lane_mask(n) for n in range(2)], axis=0))
        marked_queries.append(
            jnp.concatenate([queries[p], jnp.concatenate([marked, marked], axis=0)], axis=1)
        )
    dq_sum[...] = jnp.zeros_like(dq_sum)

    def block_step(i, carry):
        start = lax.rem(i * KB + rows - offset, rows)
        at = pl.ds(pl.multiple_of(start, KB), KB)
        block = start // KB
        scores = [nt(keys[p, at, :], marked_queries[p]) for p in range(heads // 2)]
        pulls = [nt(values[p, at, :], grads[p]) for p in range(heads // 2)]
        for p in range(heads // 2):
            weights = jnp.exp(scores[p] - logsums[p])
            pulled = pulls[p]
            dv_sum[at, of_pair(2 * p)] += nn(weights.astype(BF16), grads[p])
            slopes = (weights * (pulled - centres[p])).astype(BF16)
            dk_sum[at, of_pair(2 * p)] += nn(slopes, queries[p])
            part = nn(keys_t[block, of_pair(2 * p), :], slopes)
            for n in range(2):
                h = slice((2 * p + n) * HD, (2 * p + n + 1) * HD)
                dq_sum[h, :] += part[n * HD : (n + 1) * HD, n * QB : (n + 1) * QB]
        return carry

    lax.fori_loop(block_low, block_high, block_step, 0)
    made = (dq_sum[...] * scale).T.astype(BF16)
    half = rows // 2
    for n in range(steps):
        start = n * QB % half

        @pl.when(step == n)
        def _():
            (grad_mine, grad_other)[n * QB // half][start : start + QB, :width] = made

    total = jnp.sum(made.astype(F32), axis=0, keepdims=True)

    @pl.when(step == 0)
    def _():
        sums_ref[...] = jnp.zeros_like(sums_ref)

    sums_ref[0:1, :] += total

    @pl.when(step == steps - 1)
    def _():
        for n, ref in enumerate((grad_mine, grad_other)):
            at = slice(n * half, (n + 1) * half)
            ref[:, width : 2 * width] = dk_sum[at, :].astype(BF16)
            made = dv_sum[at, :].astype(BF16)
            ref[:, 2 * width :] = made
            sums_ref[1:2, :] += jnp.sum(made.astype(F32), axis=0, keepdims=True)


def attention_backward(
    lengths, core, query_rows, key_rows, value_rows, mixed, lse, grad_mine, grad_other
):
    rows, width = query_rows.shape
    heads = width // HD
    steps = rows // QB
    tile = pl.BlockSpec((QB, width), lambda i, *_: (i, 0))
    full = whole((rows, width))
    early = pl.BlockSpec((QB, width), lambda i, *_: (jnp.minimum(i, steps // 2 - 1), 0))
    late = pl.BlockSpec((QB, width), lambda i, *_: (jnp.maximum(i - steps // 2, 0), 0))
    outs = [jax.ShapeDtypeStruct((rows // 2, 3 * width), BF16)] * 2
    outs.append(jax.ShapeDtypeStruct((8, width), F32))
    return pl.pallas_call(
        backward_kernel,
        grid_spec=pltpu.PrefetchScalarGridSpec(
            num_scalar_prefetch=2,
            grid=(steps,),
            in_specs=[
                tile,
                early,
                late,
                early,
                late,
                pl.BlockSpec((8, QB), lambda i, *_: (0, i)),
                full,
                full,
            ],
            out_specs=[whole(o.shape) for o in outs],
            scratch_shapes=[
                pltpu.VMEM((heads // 2, rows, 2 * LANES), BF16),
                pltpu.VMEM((heads // 2, rows, LANES), BF16),
                pltpu.VMEM((rows // KB, width, KB), BF16),
                pltpu.VMEM((rows, width), F32),
                pltpu.VMEM((rows, width), F32),
                pltpu.VMEM((width, QB), F32),
            ],
        ),
        out_shape=outs,
        cost_estimate=pl.CostEstimate(
            flops=20 * rows * rows * LANES * heads,
            bytes_accessed=16 * rows * width,
            transcendentals=rows * rows * heads // 2,
        ),
        compiler_params=params(),
        name="attend_back",
    )(lengths, core, query_rows, grad_mine, grad_other, *mixed, lse, key_rows, value_rows)


def params():
    return pltpu.CompilerParams(vmem_limit_bytes=VMEM_LIMIT)


def cost(flops, moved, transcendentals=0):
    return pl.CostEstimate(flops=flops, bytes_accessed=moved, transcendentals=transcendentals)


def columns_of(slots, core, run_rows, half):
    half_run = run_rows // 2
    run, place = slots // run_rows, slots % run_rows
    held = (place // half_run + core) % 2
    return held * half + run * half_run + place % half_run


def one_hot(column, width, base):
    count = column.shape[1]
    down = jnp.broadcast_to(column, (8, count)).T[:, :1]
    lane = lax.broadcasted_iota(jnp.int32, (count, width), 1) + base
    return (down == lane).astype(F32).astype(BF16)


def intake_kernel(
    run_rows, core, slots, mine_ref, other_ref, q_weight, k_weight, v_weight, q_bias, v_bias,
    x_ref, q_ref, k_ref, v_ref
):
    half = mine_ref.shape[0]
    column = columns_of(slots[...], core[0], run_rows, half)
    rows = nn(one_hot(column, half, 0), mine_ref[...])
    rows = (rows + nn(one_hot(column, half, half), other_ref[...])).astype(BF16)
    x_ref[...] = rows
    q_ref[...] = (nn(rows, q_weight[...]) + q_bias[...]).astype(BF16)
    k_ref[...] = nn(rows, k_weight[...]).astype(BF16)
    v_ref[...] = (nn(rows, v_weight[...]) + v_bias[...]).astype(BF16)


def intake(core, slots, run_rows, mine_rows, other_rows, weights, biases):
    half, features = mine_rows.shape
    rows = 2 * half
    width = weights[0].shape[1]
    count = 512
    blocks = rows // count

    def tile(n):
        return pl.BlockSpec((count, n), lambda i, core: (i, 0))

    return pl.pallas_call(
        functools.partial(intake_kernel, run_rows),
        grid_spec=pltpu.PrefetchScalarGridSpec(
            num_scalar_prefetch=1,
            grid=(blocks,),
            in_specs=[
                pl.BlockSpec(
                    (1, count), lambda i, core: (0, (i + core[0] * (blocks // 2)) % blocks)
                ),
                whole((half, features)),
                whole((half, features)),
            ]
            + [whole((features, width))] * 3
            + [whole((1, width))] * 2,
            out_specs=[tile(features), tile(width), tile(width), tile(width)],
        ),
        out_shape=[jax.ShapeDtypeStruct((rows, features), BF16)]
        + [jax.ShapeDtypeStruct((rows, width), BF16)] * 3,
        cost_estimate=cost(2 * rows * features * (rows + 3 * width), 8 * rows * features),
        compiler_params=params(),
        name="intake",
    )(core, slots, mine_rows, other_rows, *weights, *biases)


def centred(values):
    centre = values - jnp.mean(values, axis=-1, keepdims=True)
    inverse = lax.rsqrt(jnp.mean(centre * centre, axis=-1, keepdims=True) + EPSILON)
    return centre * inverse, inverse


def norm_back(upstream, normed, inverse, gain):
    scaled = upstream * gain
    return inverse * (
        scaled
        - jnp.mean(scaled, axis=-1, keepdims=True)
        - normed * jnp.mean(scaled * normed, axis=-1, keepdims=True)
    )


def add_rows(ref, row, values):
    ref[row : row + 1, :] += jnp.sum(values, axis=0, keepdims=True)


def rows_kernel(
    run_rows, core, x_ref, mixed_mine, mixed_other, slots, cot_mine, cot_other,
    out_bias, first_gain, first_shift, down_bias, second_gain, second_shift, bias_mine, bias_other,
    out_mine, out_other, up_mine, up_other, down_mine, down_other,
    y_out, hb_out, second_out, act_out_mine, act_out_other, du_out_mine, du_out_other, first_out, low_out,
    back_out_mine, back_out_other, sums, up_sums,
    w_out, w_up, w_down, sems, out_sems, hidden, first_inv, total, slope, grad, pulled, biases,
    y_ref, hb_ref, second_ref, act, du, first_ref, low_ref, back
):
    half, features = x_ref.shape
    width = mixed_mine.shape[1]
    chunks, _, chunk = w_up.shape
    per_half = chunks // 2
    tiles = half // ROW_TILE
    copies = [
        pltpu.make_async_copy(out_mine, w_out.at[0], sems.at[0]),
        pltpu.make_async_copy(out_other, w_out.at[1], sems.at[1]),
    ]
    up_copies, down_copies = [], []
    for c in range(chunks):
        up, down = ((up_mine, down_mine), (up_other, down_other))[c // per_half]
        at = pl.ds(c % per_half * chunk, chunk)
        up_copies.append(pltpu.make_async_copy(up.at[:, at], w_up.at[c], sems.at[2 + c]))
        down_copies.append(
            pltpu.make_async_copy(down.at[at, :], w_down.at[c], sems.at[2 + chunks + c])
        )
    outgoing = []

    def send(source, target):
        copy = pltpu.make_async_copy(source, target, out_sems.at[len(outgoing)])
        copy.start()
        outgoing.append(copy)

    for copy in copies:
        copy.start()
    for up, down in zip(up_copies, down_copies):
        up.start()
        down.start()
    out_bias, first_gain, first_shift = out_bias[...], first_gain[...], first_shift[...]
    down_bias, second_gain, second_shift = down_bias[...], second_gain[...], second_shift[...]
    sums[...] = jnp.zeros_like(sums)
    up_sums[...] = jnp.zeros_like(up_sums)

    column = columns_of(slots[...], core[0], run_rows, half)
    grad[...] = nn(one_hot(column, half, 0), cot_mine[...])
    grad[...] += nn(one_hot(column, half, half), cot_other[...])

    def of_chunk(refs, c):
        return refs[c // per_half], pl.ds(c % per_half * chunk, chunk)

    for copy in copies:
        copy.wait()
    total[...] = nn(mixed_mine[...], w_out[0]) + nn(mixed_other[...], w_out[1])

    @pl.loop(0, tiles, unroll=2)
    def _(i):
        at = pl.ds(pl.multiple_of(i * ROW_TILE, ROW_TILE), ROW_TILE)
        normed, inverse = centred(x_ref[at, :].astype(F32) + total[at, :] + out_bias)
        rows = normed * first_gain + first_shift
        hidden[at, :] = rows
        hb_ref[at, :] = rows.astype(BF16)
        first_ref[at, :] = normed
        first_inv[at, :] = inverse

    send(hb_ref, hb_out)

    block = half // 2
    blocks = [slice(r * block, (r + 1) * block) for r in range(2)]
    for c in range(chunks):
        ref, wide = of_chunk((bias_mine, bias_other), c)
        biases[c : c + 1, :] = ref[:, wide]

    def inner_of(c):
        pltpu.make_async_copy(up_mine.at[:, pl.ds(0, chunk)], w_up.at[c], sems.at[2 + c]).wait()
        for at in blocks:
            slope[c, at, :] = nn(hb_ref[at, :], w_up[c]) + biases[pl.ds(c, 1), :]

    def activate(c):
        for at in blocks:
            inner = slope[c, at, :]
            share = 0.5 * (1.0 + lax.erf(inner * 0.7071067811865476))
            density = jnp.exp(-0.5 * inner * inner) * 0.3989422804014327
            act[c, at, :] = (inner * share).astype(BF16)
            slope[c, at, :] = share + inner * density
            total[at, :] += nn(act[c, at, :], w_down[c])

    def down_ready(c):
        source = down_mine.at[pl.ds(0, chunk), :]
        pltpu.make_async_copy(source, w_down.at[c], sems.at[2 + chunks + c]).wait()

    total[...] = jnp.zeros_like(total)
    inner_of(0)

    @pl.loop(0, chunks - 1)
    def _(c):
        down_ready(c)
        inner_of(c + 1)
        activate(c)

    down_ready(chunks - 1)
    activate(chunks - 1)
    for c in range(chunks):
        ref, wide = of_chunk((act_out_mine, act_out_other), c)
        send(act.at[c], ref.at[:, wide])

    @pl.loop(0, tiles, unroll=2)
    def _(i):
        at = pl.ds(pl.multiple_of(i * ROW_TILE, ROW_TILE), ROW_TILE)
        normed, inverse = centred(hidden[at, :] + total[at, :] + down_bias)
        y_ref[at, :] = (normed * second_gain + second_shift).astype(BF16)
        upstream = grad[at, :]
        add_rows(sums, 4, upstream * normed)
        add_rows(sums, 5, upstream)
        back = norm_back(upstream, normed, inverse, second_gain)
        add_rows(sums, 3, back)
        second_ref[at, :] = back.astype(BF16)
        grad[at, :] = back

    send(y_ref, y_out)
    send(second_ref, second_out)
    def pull(c):
        for at in blocks:
            pulled[c % 2, at, :] = nt(second_ref[at, :], w_down[c])

    def push(c):
        row = (c // per_half ^ core[0]) * per_half + c % per_half
        for at in blocks:
            low = (pulled[c % 2, at, :] * slope[c, at, :]).astype(BF16)
            du[c, at, :] = low
            up_sums[pl.ds(row, 1), :] += jnp.sum(low.astype(F32), axis=0, keepdims=True)
            grad[at, :] += nt(low, w_up[c])

    pull(0)

    @pl.loop(0, chunks - 1)
    def _(c):
        pull(c + 1)
        push(c)

    push(chunks - 1)
    for c in range(chunks):
        ref, wide = of_chunk((du_out_mine, du_out_other), c)
        send(du.at[c], ref.at[:, wide])

    @pl.loop(0, tiles, unroll=2)
    def _(i):
        at = pl.ds(pl.multiple_of(i * ROW_TILE, ROW_TILE), ROW_TILE)
        upstream, normed = grad[at, :], first_ref[at, :]
        add_rows(sums, 1, upstream * normed)
        add_rows(sums, 2, upstream)
        back = norm_back(upstream, normed, first_inv[at, :], first_gain)
        add_rows(sums, 0, back)
        first_ref[at, :] = back

    send(first_ref, first_out)
    low_ref[...] = first_ref[...].astype(BF16)
    send(low_ref, low_out)
    for n, out in enumerate((back_out_mine, back_out_other)):
        back[n] = nt(low_ref[...], w_out[n]).astype(BF16)
        send(back.at[n], out)
    for copy in outgoing:
        copy.wait()


def row_pass(
    core, inputs, mixed, mixed_other, slots, run_rows, cot_mine, cot_other, vectors,
    out_mine, out_other, up_mine, up_other, down_mine, down_other
):
    half, features = cot_mine.shape
    width = mixed.shape[1]
    chunk = features
    chunks = 2 * up_mine.shape[1] // chunk
    any_space = pl.BlockSpec(memory_space=pl.ANY)

    def low(*shape):
        return jax.ShapeDtypeStruct(shape, BF16)

    outs = [
        low(half, features),
        low(half, features),
        low(half, features),
        low(half, up_mine.shape[1]),
        low(half, up_mine.shape[1]),
        low(half, up_mine.shape[1]),
        low(half, up_mine.shape[1]),
        jax.ShapeDtypeStruct((half, features), F32),
        low(half, features),
        low(half, width),
        low(half, width),
        jax.ShapeDtypeStruct((8, features), F32),
        jax.ShapeDtypeStruct((chunks, chunk), F32),
    ]
    return pl.pallas_call(
        functools.partial(rows_kernel, run_rows),
        grid_spec=pltpu.PrefetchScalarGridSpec(
            num_scalar_prefetch=1,
            grid=(1,),
            in_specs=[
                whole((half, features)),
                whole((half, width)),
                whole((half, width)),
                pl.BlockSpec((1, half), lambda i, core: (0, core[0])),
                whole((half, features)),
                whole((half, features)),
            ]
            + [whole(v.shape) for v in vectors]
            + [any_space] * 6,
            out_specs=[any_space] * (len(outs) - 2) + [whole(o.shape) for o in outs[-2:]],
            scratch_shapes=[
                pltpu.VMEM((2, width, features), BF16),
                pltpu.VMEM((chunks, features, chunk), BF16),
                pltpu.VMEM((chunks, chunk, features), BF16),
                pltpu.SemaphoreType.DMA((2 + 2 * chunks,)),
                pltpu.SemaphoreType.DMA((7 + 2 * chunks,)),
                pltpu.VMEM((half, features), F32),
                pltpu.VMEM((half, 1), F32),
                pltpu.VMEM((half, features), F32),
                pltpu.VMEM((chunks, half, chunk), F32),
                pltpu.VMEM((half, features), F32),
                pltpu.VMEM((2, half, chunk), F32),
                pltpu.VMEM((chunks, chunk), F32),
                pltpu.VMEM((half, features), BF16),
                pltpu.VMEM((half, features), BF16),
                pltpu.VMEM((half, features), BF16),
                pltpu.VMEM((chunks, half, chunk), BF16),
                pltpu.VMEM((chunks, half, chunk), BF16),
                pltpu.VMEM((half, features), F32),
                pltpu.VMEM((half, features), BF16),
                pltpu.VMEM((2, half, width), BF16),
            ],
        ),
        out_shape=outs,
        cost_estimate=cost(
            8 * half * features * chunk * chunks + 10 * half * features * features,
            30 * half * features + 8 * features * chunk * chunks,
            half * chunk * chunks,
        ),
        compiler_params=params(),
        name="row_pass",
    )(
        core, inputs, mixed, mixed_other, slots, cot_mine, cot_other, *vectors,
        out_mine, out_other, up_mine, up_other, down_mine, down_other
    )


def after(values, others):
    return lax.optimization_barrier((values, others))[0]


def near_groups(groups):
    near = 4 if groups % 4 == 0 else 1
    return near, groups // near


def tn(left, right):
    return lax.dot_general(left, right, (((0,), (0,)), ((), ())), preferred_element_type=F32)


def by_place(terms, groups):
    near, far = near_groups(groups)
    place = lax.axis_index("dp") % near
    terms = terms.reshape(far, near, terms.shape[0] // groups, terms.shape[1])
    return [lax.dynamic_index_in_dim(terms, place ^ n, 1, keepdims=False) for n in range(near)]


def gradient_kernel(chunks, near, share, halving, me, *refs):
    operands, outs, acc = refs[: 4 * len(chunks)], refs[4 * len(chunks) : -1], refs[-1]
    step = pl.program_id(0)
    first, column = 0, 0
    for n, (chunk, count) in enumerate(chunks):
        left, left_more, right, right_more = operands[4 * n : 4 * n + 4]

        @pl.when((step >= first) & (step < first + count))
        def _():
            acc[:, :chunk] = tn(left[...], right[...])
            acc[:, :chunk] += tn(left_more[...], right_more[...])
            at = pl.ds(pl.multiple_of(column + (step - first) * chunk, LANES), chunk)

            def place(out, place):
                for f in range(out.shape[0]):
                    row = share * (f * near + (me[0] ^ place))
                    row = pl.ds(pl.multiple_of(row, 16), share)
                    out[f, :, at] = acc[row, :chunk].astype(out.dtype)

            if halving:
                for out, (a, b) in zip(outs, ((0, 3 - halving), (halving, 3))):
                    place(out.at[0], a)
                    place(out.at[1], b)
            else:
                for m, out in enumerate(outs):
                    place(out, m)

        first += count
        column += count * chunk


def gradients(pieces, groups, halving=0):
    near, far = near_groups(groups)
    features = pieces[0][0][0].shape[1]
    share = features // groups
    if near != 4 or share % 16 != 0:

        def rows_of(left, rows):
            return lax.slice_in_dim(left[0], left[1] * rows, (left[1] + 1) * rows, axis=0)

        terms = [
            tn(rows_of(p[0], p[2].shape[0]), p[2]) + tn(rows_of(p[1], p[3].shape[0]), p[3])
            for p in pieces
        ]
        made = [t.astype(BF16) for t in by_place(jnp.concatenate(terms, axis=1), groups)]
        if halving:
            made = [
                jnp.stack([made[0], made[3 - halving]]), jnp.stack([made[halving], made[3]])
            ]
        return made
    in_specs, operands, chunks, base, columns = [], [], [], 0, 0
    for left, left_more, right, right_more in pieces:
        rows = right.shape[0]
        chunk = min(features, right.shape[1])
        if right.shape[1] % chunk:
            chunk = right.shape[1] // 3
        count = right.shape[1] // chunk

        def at(j, me, base=base, count=count):
            return 0, jnp.clip(j - base, 0, count - 1)

        for array, block in (left, left_more):
            in_specs.append(
                pl.BlockSpec((rows, features), lambda j, me, block=block: (block, 0))
            )
            operands.append(array)
        in_specs += [pl.BlockSpec((rows, chunk), at)] * 2
        operands += [right, right_more]
        chunks.append((chunk, count))
        base += count
        columns += count * chunk
    if halving:
        outs = [jax.ShapeDtypeStruct((2, far, share, columns), BF16)] * 2
    else:
        outs = [jax.ShapeDtypeStruct((far, share, columns), BF16)] * near
    return pl.pallas_call(
        functools.partial(gradient_kernel, chunks, near, share, halving),
        grid_spec=pltpu.PrefetchScalarGridSpec(
            num_scalar_prefetch=1,
            grid=(base,),
            in_specs=in_specs,
            out_specs=[whole(o.shape) for o in outs],
            scratch_shapes=[pltpu.VMEM((features, features), F32)],
        ),
        out_shape=outs,
        cost_estimate=cost(4 * rows * features * columns, 8 * rows * features + 4 * features * columns),
        compiler_params=params(),
        name="gradients",
    )((lax.axis_index("dp") % near).reshape(1), *operands)


def pairs(groups, distance):
    return [(i, i ^ distance) for i in range(groups)]


def far_halves(total, groups, bit):
    total = total.reshape(-1, 2, *total.shape[1:])
    side = (lax.axis_index("dp") // near_groups(groups)[0] >> bit) & 1
    kept = lax.dynamic_index_in_dim(total, side, 1, keepdims=False)
    return kept, lax.dynamic_index_in_dim(total, 1 - side, 1, keepdims=False).astype(BF16)


def far_step(halves, groups, bit, first=()):
    near, far = near_groups(groups)
    kept, sent = halves
    got = after(lax.ppermute(sent, "dp", pairs(groups, near << bit)), first)
    total = kept.astype(F32) + got.astype(F32)
    return far_halves(total, groups, bit + 1) if 2 << bit < far else total[0]


def far_direct(total, groups, first=()):
    near, far = near_groups(groups)
    run = lax.axis_index("dp") // near
    kept = lax.dynamic_index_in_dim(total, run, 0, keepdims=False)
    got = []
    for step in range(1, far):
        sent = lax.dynamic_index_in_dim(total, run ^ step, 0, keepdims=False).astype(BF16)
        got.append(lax.ppermute(sent, "dp", pairs(groups, step * near)))
    return sum_of(kept, after(got, first))


def near_sends(terms, groups):
    return [lax.ppermute(t, "dp", pairs(groups, n + 1)) for n, t in enumerate(terms)]


def sum_of(kept, got):
    kept = kept.astype(F32)
    for term in got:
        kept = kept + term.astype(F32)
    return kept


def input_kernel(first_ref, mine_ref, other_ref, *refs):
    weights, out_ref = refs[:-1], refs[-1]
    total = first_ref[...]
    width = weights[0].shape[1]
    for n, weight in enumerate(weights):
        rows = (mine_ref, other_ref)[n // 3]
        total = total + nt(rows[:, n % 3 * width : (n % 3 + 1) * width], weight[...])
    out_ref[...] = total.astype(BF16)


def input_rows(first_grad, mine_rows, other_rows, weights):
    half, features = first_grad.shape
    wide = other_rows.shape[1]
    count = 512

    def tile(n):
        return pl.BlockSpec((count, n), lambda i: (i, 0))

    return pl.pallas_call(
        input_kernel,
        grid=(half // count,),
        in_specs=[tile(features), tile(wide), tile(wide)] + [whole(w.shape) for w in weights],
        out_specs=tile(features),
        out_shape=jax.ShapeDtypeStruct((half, features), BF16),
        cost_estimate=cost(4 * half * features * wide, 8 * half * features + 4 * features * wide),
        compiler_params=params(),
        name="input_rows",
    )(first_grad, mine_rows, other_rows, *weights)


def route_kernel(share, has_extra, core, slots_mine, slots_other, mine_ref, other_ref, *refs):
    out_ref = refs[-1]
    groups, run = out_ref.shape[0], mine_ref.shape[0] // out_ref.shape[0]
    half = mine_ref.shape[0]
    row = lax.broadcasted_iota(jnp.int32, (half, half), 0)
    column_mine = columns_of(slots_mine[...], core[0], 2 * run, half)
    column_other = columns_of(slots_other[...], core[0], 2 * run, half)
    put_mine = (column_mine == row).astype(F32).astype(BF16)
    put_other = (column_other == row).astype(F32).astype(BF16)
    rows = (nn(put_mine, mine_ref[...]) + nn(put_other, other_ref[...])).astype(BF16)
    out_ref[:, :run, :] = rows.reshape(groups, run, rows.shape[1])
    if has_extra:
        sums, up_sums, qv_sums, wide, wide_up = refs[:5]
        features = sums.shape[1]
        width = qv_sums.shape[1]
        wide[...] = jnp.zeros_like(wide)
        wide_up[...] = jnp.zeros_like(wide_up)
        wide[:, :features] = sums[...]
        wide_up[:4, :features] = up_sums[...]
        at = pl.ds(pl.multiple_of(core[0] * width, LANES), width)
        wide[6:8, at] = qv_sums[:2, :]
        for g in range(groups):
            block = wide[:, share * g : share * g + LANES]
            start = 4 * share * g
            blocks = [block]
            parts = []
            for r in range(4):
                line = (start + share * r) // features
                lane = (start + share * r) % features
                parts.append(wide_up[line : line + 1, lane : lane + LANES])
            blocks.append(jnp.concatenate(parts + [jnp.zeros((4, LANES), F32)], axis=0))
            for b, rest in enumerate(blocks):
                for piece in range(3):
                    term = rest.astype(BF16)
                    rest = rest - term.astype(F32)
                    q = 2 * piece + b
                    out_ref[g, run : run + 8, q * LANES : (q + 1) * LANES] = term


def route(core, slots, mine_rows, other_rows, groups, extra=None):
    half, features = mine_rows.shape
    run = half // groups
    share = features // groups
    extra = extra or ()
    args = [core, slots, slots, mine_rows, other_rows, *extra]
    in_specs = [
        pl.BlockSpec((1, half), lambda i, core: (0, core[0])),
        pl.BlockSpec((1, half), lambda i, core: (0, 1 - core[0])),
    ] + [whole(a.shape) for a in args[3:]]
    scratch = [pltpu.VMEM((8, features + LANES), F32)] * 2 if extra else []
    shape = (groups, run + (8 if extra else 0), features)

    def kernel(*refs):
        ins, (out_ref, *more) = refs[: len(args)], refs[len(args) :]
        route_kernel(share, len(extra) > 0, *ins, *more, out_ref)

    return pl.pallas_call(
        kernel,
        grid_spec=pltpu.PrefetchScalarGridSpec(
            num_scalar_prefetch=1,
            grid=(1,),
            in_specs=in_specs,
            out_specs=whole(shape),
            scratch_shapes=scratch,
        ),
        out_shape=jax.ShapeDtypeStruct(shape, BF16),
        cost_estimate=cost(4 * half * half * features, 6 * half * features),
        compiler_params=params(),
        name="route",
    )(*args)


def exchange(values):
    return lax.all_to_all(values, "dp", split_axis=0, concat_axis=0, tiled=True)


def weave_kernel(core, mine_ref, other_ref, out_ref, *outs):
    run = out_ref.shape[2]
    out_ref[:, core[0]] = mine_ref[:, :run, :]
    out_ref[:, 1 - core[0]] = other_ref[:, :run, :]
    if not outs:
        return
    pieces = []
    for q in range(6):
        at = slice(q * LANES, (q + 1) * LANES)
        both = [jnp.sum(r[:, run:, at].astype(F32), axis=0) for r in (mine_ref, other_ref)]
        pieces.append(both[0] + both[1])
    first, more = [pieces[4 + b] + pieces[2 + b] + pieces[b] for b in range(2)]
    each = outs[0].shape[1]
    share = 2 * each
    low = core[0] == 0

    def half_of(values):
        return jnp.where(low, values[:, :each], values[:, each:share])

    for out, row in zip(outs[:8], (6, 7, 0, 1, 2, 3, 4, 5)):
        out[...] = half_of(first[row : row + 1, :])
    pair = jnp.where(low, more[0:2, :share], more[2:4, :share])
    outs[8][:, :share] = pair[0:1, :]
    outs[8][:, share:] = pair[1:2, :]


def weave(core, part, rows_of_core, small=0):
    groups, _, features = part.shape
    outs = [jax.ShapeDtypeStruct((groups, 2, rows_of_core, features), BF16)]
    if small:
        outs += [jax.ShapeDtypeStruct((1, small), F32)] * 8
        outs.append(jax.ShapeDtypeStruct((1, 4 * small), F32))
    rows, *more = pl.pallas_call(
        weave_kernel,
        grid_spec=pltpu.PrefetchScalarGridSpec(
            num_scalar_prefetch=1,
            grid=(1,),
            in_specs=[whole(part.shape)] * 2,
            out_specs=[whole(o.shape) for o in outs],
        ),
        out_shape=outs,
        cost_estimate=cost(1, 1),
        compiler_params=params(),
        name="weave",
    )(core, part, swap(part))
    rows = rows.reshape(groups * 2 * rows_of_core, features)
    return (rows, *[m.reshape(-1) for m in more]) if small else rows


def local(
    tokens,
    token_slot,
    seq_lengths,
    query_weight,
    query_bias,
    key_weight,
    value_weight,
    value_bias,
    out_weight,
    out_bias,
    first_gain,
    first_shift,
    up_weight,
    up_bias,
    down_weight,
    down_bias,
    second_gain,
    second_shift,
    cotangent,
):
    groups = lax.axis_size("dp")
    row_count, features = tokens.shape
    run_rows = row_count // groups
    half_run = run_rows // 2
    half = row_count // 2
    mine = lax.axis_index("tensor")
    core = mine.reshape(1)
    near, far = near_groups(groups)

    def part_of(values):
        return lax.dynamic_slice_in_dim(
            values.reshape(groups, run_rows, features), mine * half_run, half_run, 1
        )

    cot_part = part_of(cotangent)
    token_rows = after(exchange(part_of(tokens)), cot_part).reshape(half, features)
    cot_raw = exchange(cot_part).reshape(half, features)

    qkv_weights = [query_weight, key_weight, value_weight]
    out_other, up_other, down_other = swap(out_weight), swap(up_weight), swap(down_weight)
    vectors = [out_bias, first_gain, first_shift, down_bias, second_gain, second_shift]
    bias_other = swap(up_bias)
    vectors = [v.reshape(1, -1) for v in vectors + [up_bias, bias_other]]
    qkv_other = [swap(w) for w in qkv_weights]
    biases = [query_bias.reshape(1, -1), value_bias.reshape(1, -1)]
    early = (out_other, up_other, down_other, qkv_other)
    token_rows, vectors, biases, early = lax.optimization_barrier(
        (token_rows, vectors, biases, early)
    )
    out_other, up_other, down_other, qkv_other = early
    token_got = swap(token_rows)

    inputs, query_rows, key_rows, value_rows = intake(
        core, token_slot, run_rows, token_rows, token_got, qkv_weights,
        biases,
    )
    mixed_mine, mixed_theirs, logsum = attention_forward(seq_lengths, core, query_rows, key_rows, value_rows)
    cot_rows = after(cot_raw, mixed_mine)
    mixed_other = swap(mixed_theirs)
    (
        output_low, hidden_low, second_low, act_mine, act_other, inner_mine, inner_other, first_grad,
        first_low, mixed_grad_mine, mixed_grad_other, sums, up_sums,
    ) = row_pass(
        core, inputs, mixed_mine, mixed_other, token_slot, run_rows, cot_rows, swap(cot_rows), vectors,
        out_weight, out_other, up_weight, up_other, down_weight, down_other,
    )
    mixed_grad_got = swap(mixed_grad_other)

    width = query_weight.shape[1]
    ff_width = up_weight.shape[1]
    output_got = swap(output_low)
    second_low, hidden_low, first_low, act_other, inner_other = after(
        (second_low, hidden_low, first_low, act_other, inner_other), output_got
    )
    second_got, act_got = swap(second_low), swap(act_other)
    hidden_got, inner_got = swap(hidden_low), swap(inner_other)
    first_got = swap(first_low)
    returned = route(core, token_slot, output_low, output_got, groups)
    kept, sent = [], []
    left = gradients([((second_low, 0), (second_got, 0), act_mine, act_got)], groups, near == 4)
    right = [
        ((hidden_low, 0), (hidden_got, 0), inner_mine, inner_got),
        ((first_low, 0), (first_got, 0), mixed_mine, mixed_theirs),
    ]
    right = gradients(right, groups, 2 * (near == 4))
    if near == 4:
        kept, sent = [left[0], right[0]], [left[1], right[1]]
    else:
        kept, sent = [left[0][None], right[0][None]], []
    mixed_grad_mine, mixed_grad_got = after(
        (mixed_grad_mine, mixed_grad_got), (returned, kept, sent)
    )
    returned = exchange(returned)
    got = [lax.ppermute(v, "dp", pairs(groups, n + 1)) for n, v in enumerate(sent)]
    qkv_mine, qkv_theirs, qv_sums = attention_backward(
        seq_lengths, core, query_rows, key_rows, value_rows, (mixed_mine, mixed_theirs), logsum,
        mixed_grad_mine, mixed_grad_got,
    )
    other_grad = swap(qkv_theirs)
    qkv_terms = gradients([((inputs, 0), (inputs, 1), qkv_mine, qkv_theirs)], groups)
    got, returned = after((got, returned), qkv_terms)
    sent = [(k[1].astype(F32) + g[1].astype(F32)).astype(BF16) for k, g in zip(kept, got)]
    first_grad = after(first_grad, (qkv_terms, sent))
    kept, first_got = [k[0].astype(F32) for k in kept], got
    qkv_got = near_sends(qkv_terms[1:], groups)
    got = [lax.ppermute(v, "dp", pairs(groups, 2 - n)) for n, v in enumerate(sent)]
    input_low = input_rows(
        first_grad, qkv_mine, other_grad, qkv_weights + qkv_other
    )
    given = route(core, token_slot, input_low, swap(input_low), groups, (sums, up_sums, qv_sums))
    got = after(got, given)
    if got:
        kept = [k + f[0].astype(F32) + g.astype(F32) for k, f, g in zip(kept, first_got, got)]
    ffn_terms = far_halves(jnp.concatenate(kept, axis=2), groups, 0)
    payload, given = given, exchange(given)
    layer_out = weave(core, after(returned, payload), half_run)
    ffn_sum = far_step(ffn_terms, groups, 0, (given, layer_out))
    qkv_got = after(qkv_got, ffn_sum)
    for bit in range(1, far.bit_length() - 1):
        ffn_sum = far_step(ffn_sum, groups, bit, qkv_got)
    qkv_sum = far_direct(sum_of(qkv_terms[0], qkv_got), groups, ffn_sum)
    (
        input_gradient, query_bias_sum, value_bias_sum, out_bias_sum, first_gain_sum,
        first_shift_sum, down_bias_sum, second_gain_sum, second_shift_sum, up_bias_sum,
    ) = weave(core, given, half_run, features // groups // 2)
    return (
        layer_out,
        input_gradient,
        qkv_sum[:, :width],
        query_bias_sum,
        qkv_sum[:, width : 2 * width],
        qkv_sum[:, 2 * width :],
        value_bias_sum,
        ffn_sum[:, 2 * ff_width :].T,
        out_bias_sum,
        first_gain_sum,
        first_shift_sum,
        ffn_sum[:, ff_width : 2 * ff_width],
        up_bias_sum,
        ffn_sum[:, :ff_width].T,
        down_bias_sum,
        second_gain_sum,
        second_shift_sum,
    )


def solution(mesh):
    rows = P("dp", None)
    in_specs = (
        rows,
        rows,
        rows,
        P(None, "tensor"),
        P("tensor"),
        P(None, "tensor"),
        P(None, "tensor"),
        P("tensor"),
        P("tensor", None),
        P(),
        P(),
        P(),
        P(None, "tensor"),
        P("tensor"),
        P("tensor", None),
        P(),
        P(),
        P(),
        rows,
    )
    spread = P(("dp", "tensor"))
    out_specs = (
        rows,
        rows,
        P("dp", "tensor"),
        spread,
        P("dp", "tensor"),
        P("dp", "tensor"),
        spread,
        P("tensor", "dp"),
        spread,
        spread,
        spread,
        P("dp", "tensor"),
        spread,
        P("tensor", "dp"),
        spread,
        spread,
        spread,
    )
    return jax.shard_map(local, mesh=mesh, in_specs=in_specs, out_specs=out_specs, check_vma=False)
```

```python
import functools
import jax
import jax.numpy as jnp
from jax import lax
from jax.experimental import pallas as pl
from jax.experimental.pallas import tpu as pltpu
from jax.sharding import PartitionSpec as P

HD = 64
LANES = 128
SEG_MAX = 8
FORWARD_ROWS = 512
FORWARD_KEYS = 512
QB = 256
KB = 256
ROW_TILE = 64


EPSILON = 1e-12
MASKED = -1e30
F32 = jnp.float32
BF16 = jnp.bfloat16
SWAP = [(0, 1), (1, 0)]
VMEM_LIMIT = 60 << 20


def swap(values):
    return lax.ppermute(values, "tensor", SWAP)


def nt(a, b):
    return lax.dot_general(a, b, (((1,), (1,)), ((), ())), preferred_element_type=F32)


def nn(a, b):
    return jnp.dot(a, b, preferred_element_type=F32)


def segment_ends(lengths):
    ends, end = [], jnp.int32(0)
    for n in range(lengths.shape[1]):
        end = end + lengths[0, n]
        ends.append(end)
    return ends


def bounds(ends, rows, first, last):
    low, high = jnp.int32(0), jnp.int32(rows)
    for end in ends:
        low = jnp.where(end <= first, jnp.maximum(low, end), low)
        high = jnp.where(end > last, jnp.minimum(high, end), high)
    return low, high


def lane_bounds(ends, rows):
    lane = lax.broadcasted_iota(jnp.int32, (1, LANES), 1)
    start = jnp.full((1, LANES), 2 * rows, jnp.int32)
    stop = jnp.zeros((1, LANES), jnp.int32)
    begin = 0
    for n, end in enumerate(ends):
        start = jnp.where(lane == n, begin, start)
        stop = jnp.where(lane == n, end, stop)
        begin = end
    return start, stop


def key_marks(ends, rows, offset):
    start, stop = lane_bounds(ends, rows)
    pos = lax.broadcasted_iota(jnp.int32, (rows, LANES), 0) + offset
    pos = jnp.where(pos >= rows, pos - rows, pos)
    return ((pos >= start) & (pos < stop)).astype(F32).astype(BF16)


def query_marks(ends, rows, first, count):
    start, stop = lane_bounds(ends, rows)
    lane = lax.broadcasted_iota(jnp.int32, (1, LANES), 1)
    pos = lax.broadcasted_iota(jnp.int32, (count, LANES), 0) + first
    return jnp.where((lane < len(ends)) & ((pos < start) | (pos >= stop)), MASKED, 0.0)


def lane_mask(half):
    lane = lax.broadcasted_iota(jnp.int32, (1, LANES), 1)
    return ((lane // HD) == half).astype(F32).astype(BF16)


def of_pair(h):
    return slice(h // 2 * LANES, (h // 2 + 1) * LANES)


def forward_kernel(
    lengths, core, q_ref, k_ref, v_ref, o_mine, o_other, lse_ref, keys, values_t, mixed, peaks, totals
):
    rows, width = k_ref.shape
    heads = width // HD
    step = pl.program_id(0)
    ends = segment_ends(lengths)
    offset = core[0] * (rows // 2)

    @pl.when(step == 0)
    def _():
        marks = key_marks(ends, rows, offset)
        for p in range(heads // 2):
            keys[p, :, :LANES] = k_ref[:, of_pair(2 * p)]
            keys[p, :, LANES:] = marks
        for block in range(rows // FORWARD_KEYS):
            at = slice(block * FORWARD_KEYS, (block + 1) * FORWARD_KEYS)
            values_t[block] = v_ref[at, :].astype(F32).T.astype(BF16)

    first = lax.rem(step * FORWARD_ROWS + offset, rows)
    low, high = bounds(ends, rows, first, first + FORWARD_ROWS - 1)
    block_low, block_high = low // FORWARD_KEYS, (high + FORWARD_KEYS - 1) // FORWARD_KEYS
    marked = query_marks(ends, rows, first, FORWARD_ROWS).astype(BF16)
    queries = []
    for p in range(heads // 2):
        query = q_ref[:, of_pair(2 * p)] * BF16(HD**-0.5)
        both = [jnp.concatenate([query * lane_mask(n), marked], axis=1) for n in range(2)]
        queries.append(jnp.concatenate(both, axis=0))
    mixed[...] = jnp.zeros_like(mixed)
    peaks[...] = jnp.full_like(peaks, MASKED)
    totals[...] = jnp.zeros_like(totals)

    def block_step(i, carry):
        start = lax.rem(i * FORWARD_KEYS + rows - offset, rows)
        at = pl.ds(pl.multiple_of(start, FORWARD_KEYS), FORWARD_KEYS)
        block = start // FORWARD_KEYS
        made = [nt(keys[p, at, :], queries[p]) for p in range(heads // 2)]
        for p in range(heads // 2):
            scores = made[p]
            row = slice(p, p + 1)
            peak = jnp.maximum(peaks[row, :], jnp.max(scores, axis=0, keepdims=True))
            shrink = jnp.exp(peaks[row, :] - peak)
            weights = jnp.exp(scores - peak)
            peaks[row, :] = peak
            totals[row, :] = totals[row, :] * shrink + jnp.sum(weights, axis=0, keepdims=True)
            part = nn(values_t[block, of_pair(2 * p), :], weights.astype(BF16))
            for n in range(2):
                h = slice((2 * p + n) * HD, (2 * p + n + 1) * HD)
                q = slice(n * FORWARD_ROWS, (n + 1) * FORWARD_ROWS)
                mixed[h, :] = mixed[h, :] * shrink[:, q] + part[n * HD : (n + 1) * HD, q]
        return carry

    lax.fori_loop(block_low, block_high, block_step, 0)
    inverse = 1.0 / totals[...]
    lse = peaks[...] + jnp.log(totals[...])
    for h in range(heads):
        wide = slice(h * HD, (h + 1) * HD)
        p, q = h // 2, slice(h % 2 * FORWARD_ROWS, (h % 2 + 1) * FORWARD_ROWS)
        mixed[wide, :] = mixed[wide, :] * inverse[p : p + 1, q]
        lse_ref[h : h + 1, :] = lse[p : p + 1, q]
    made = mixed[...].T.astype(BF16)
    half = rows // 2
    for n in range(rows // FORWARD_ROWS):
        start = n * FORWARD_ROWS % half

        @pl.when(step == n)
        def _():
            ref = (o_mine, o_other)[n * FORWARD_ROWS // half]
            ref[start : start + FORWARD_ROWS, :] = made


def whole(shape):
    return pl.BlockSpec(shape, lambda *_: (0,) * len(shape))


def attention_forward(lengths, core, query_rows, key_rows, value_rows):
    rows, width = query_rows.shape
    heads = width // HD
    tile = pl.BlockSpec((FORWARD_ROWS, width), lambda i, *_: (i, 0))
    return pl.pallas_call(
        forward_kernel,
        grid_spec=pltpu.PrefetchScalarGridSpec(
            num_scalar_prefetch=2,
            grid=(rows // FORWARD_ROWS,),
            in_specs=[tile, whole((rows, width)), whole((rows, width))],
            out_specs=[whole((rows // 2, width))] * 2
            + [pl.BlockSpec((8, FORWARD_ROWS), lambda i, *_: (0, i))],
            scratch_shapes=[
                pltpu.VMEM((heads // 2, rows, 2 * LANES), BF16),
                pltpu.VMEM((rows // FORWARD_KEYS, width, FORWARD_KEYS), BF16),
                pltpu.VMEM((width, FORWARD_ROWS), F32),
                pltpu.VMEM((8, 2 * FORWARD_ROWS), F32),
                pltpu.VMEM((8, 2 * FORWARD_ROWS), F32),
            ],
        ),
        out_shape=[jax.ShapeDtypeStruct((rows // 2, width), BF16)] * 2
        + [jax.ShapeDtypeStruct((8, rows), F32)],
        cost_estimate=pl.CostEstimate(
            flops=8 * rows * rows * LANES * heads,
            bytes_accessed=8 * rows * width,
            transcendentals=rows * rows * heads // 2,
        ),
        compiler_params=params(),
        name="attend",
    )(lengths, core, query_rows, key_rows, value_rows)


def backward_kernel(
    lengths, core, q_ref, do_mine, do_other, o_mine, o_other, lse_ref, k_ref, v_ref,
    grad_mine, grad_other, sums_ref, keys, values, keys_t, dk_sum, dv_sum, dq_sum
):
    rows, width = k_ref.shape
    heads = width // HD
    step = pl.program_id(0)
    steps = rows // QB
    ends = segment_ends(lengths)
    offset = core[0] * (rows // 2)
    scale = HD**-0.5

    @pl.when(step == 0)
    def _():
        marks = key_marks(ends, rows, offset)
        for p in range(heads // 2):
            keys[p, :, :LANES] = k_ref[:, of_pair(2 * p)]
            keys[p, :, LANES:] = marks
            values[p] = v_ref[:, of_pair(2 * p)]
        for block in range(rows // KB):
            at = slice(block * KB, (block + 1) * KB)
            keys_t[block] = k_ref[at, :].astype(F32).T.astype(BF16)
        dk_sum[...] = jnp.zeros_like(dk_sum)
        dv_sum[...] = jnp.zeros_like(dv_sum)

    first = lax.rem(step * QB + offset, rows)
    low, high = bounds(ends, rows, first, first + QB - 1)
    block_low, block_high = low // KB, (high + KB - 1) // KB
    marked = query_marks(ends, rows, first, QB).astype(BF16)
    early = jnp.full((1, width), step, jnp.int32) < steps // 2
    use_mine = early.astype(F32).astype(BF16)
    use_other = (~early).astype(F32).astype(BF16)
    grad_rows = do_mine[...] * use_mine + do_other[...] * use_other
    mixed_rows = o_mine[...] * use_mine + o_other[...] * use_other
    lane = lax.broadcasted_iota(jnp.int32, (8, LANES), 1)
    row = lax.broadcasted_iota(jnp.int32, (8, LANES), 0)
    by_head = (lane // HD == row).astype(F32).astype(BF16)
    queries, grads, marked_queries, logsums, centres = [], [], [], [], []
    for p in range(heads // 2):
        pair = of_pair(2 * p)
        query = [q_ref[:, pair] * (lane_mask(n) * BF16(scale)) for n in range(2)]
        grad = grad_rows[:, pair]
        exact = grad.astype(F32) * mixed_rows[:, pair].astype(F32)
        high_term = exact.astype(BF16)
        low_term = (exact - high_term.astype(F32)).astype(BF16)
        centre = nt(by_head, high_term) + nt(by_head, low_term)
        centres.append(jnp.concatenate([centre[0:1, :], centre[1:2, :]], axis=1))
        logsums.append(
            jnp.concatenate([lse_ref[2 * p : 2 * p + 1, :], lse_ref[2 * p + 1 : 2 * p + 2, :]], axis=1)
        )
        queries.append(jnp.concatenate(query, axis=0))
        grads.append(jnp.concatenate([grad * lane_mask(n) for n in range(2)], axis=0))
        marked_queries.append(
            jnp.concatenate([queries[p], jnp.concatenate([marked, marked], axis=0)], axis=1)
        )
    dq_sum[...] = jnp.zeros_like(dq_sum)

    def block_step(i, carry):
        start = lax.rem(i * KB + rows - offset, rows)
        at = pl.ds(pl.multiple_of(start, KB), KB)
        block = start // KB
        scores = [nt(keys[p, at, :], marked_queries[p]) for p in range(heads // 2)]
        pulls = [nt(values[p, at, :], grads[p]) for p in range(heads // 2)]
        for p in range(heads // 2):
            weights = jnp.exp(scores[p] - logsums[p])
            pulled = pulls[p]
            dv_sum[at, of_pair(2 * p)] += nn(weights.astype(BF16), grads[p])
            slopes = (weights * (pulled - centres[p])).astype(BF16)
            dk_sum[at, of_pair(2 * p)] += nn(slopes, queries[p])
            part = nn(keys_t[block, of_pair(2 * p), :], slopes)
            for n in range(2):
                h = slice((2 * p + n) * HD, (2 * p + n + 1) * HD)
                dq_sum[h, :] += part[n * HD : (n + 1) * HD, n * QB : (n + 1) * QB]
        return carry

    lax.fori_loop(block_low, block_high, block_step, 0)
    made = (dq_sum[...] * scale).T.astype(BF16)
    half = rows // 2
    for n in range(steps):
        start = n * QB % half

        @pl.when(step == n)
        def _():
            (grad_mine, grad_other)[n * QB // half][start : start + QB, :width] = made

    total = jnp.sum(made.astype(F32), axis=0, keepdims=True)

    @pl.when(step == 0)
    def _():
        sums_ref[...] = jnp.zeros_like(sums_ref)

    sums_ref[0:1, :] += total

    @pl.when(step == steps - 1)
    def _():
        for n, ref in enumerate((grad_mine, grad_other)):
            at = slice(n * half, (n + 1) * half)
            ref[:, width : 2 * width] = dk_sum[at, :].astype(BF16)
            made = dv_sum[at, :].astype(BF16)
            ref[:, 2 * width :] = made
            sums_ref[1:2, :] += jnp.sum(made.astype(F32), axis=0, keepdims=True)


def attention_backward(
    lengths, core, query_rows, key_rows, value_rows, mixed, lse, grad_mine, grad_other
):
    rows, width = query_rows.shape
    heads = width // HD
    steps = rows // QB
    tile = pl.BlockSpec((QB, width), lambda i, *_: (i, 0))
    full = whole((rows, width))
    early = pl.BlockSpec((QB, width), lambda i, *_: (jnp.minimum(i, steps // 2 - 1), 0))
    late = pl.BlockSpec((QB, width), lambda i, *_: (jnp.maximum(i - steps // 2, 0), 0))
    outs = [jax.ShapeDtypeStruct((rows // 2, 3 * width), BF16)] * 2
    outs.append(jax.ShapeDtypeStruct((8, width), F32))
    return pl.pallas_call(
        backward_kernel,
        grid_spec=pltpu.PrefetchScalarGridSpec(
            num_scalar_prefetch=2,
            grid=(steps,),
            in_specs=[
                tile,
                early,
                late,
                early,
                late,
                pl.BlockSpec((8, QB), lambda i, *_: (0, i)),
                full,
                full,
            ],
            out_specs=[whole(o.shape) for o in outs],
            scratch_shapes=[
                pltpu.VMEM((heads // 2, rows, 2 * LANES), BF16),
                pltpu.VMEM((heads // 2, rows, LANES), BF16),
                pltpu.VMEM((rows // KB, width, KB), BF16),
                pltpu.VMEM((rows, width), F32),
                pltpu.VMEM((rows, width), F32),
                pltpu.VMEM((width, QB), F32),
            ],
        ),
        out_shape=outs,
        cost_estimate=pl.CostEstimate(
            flops=20 * rows * rows * LANES * heads,
            bytes_accessed=16 * rows * width,
            transcendentals=rows * rows * heads // 2,
        ),
        compiler_params=params(),
        name="attend_back",
    )(lengths, core, query_rows, grad_mine, grad_other, *mixed, lse, key_rows, value_rows)


def params():
    return pltpu.CompilerParams(vmem_limit_bytes=VMEM_LIMIT)


def cost(flops, moved, transcendentals=0):
    return pl.CostEstimate(flops=flops, bytes_accessed=moved, transcendentals=transcendentals)


def columns_of(slots, core, run_rows, half):
    half_run = run_rows // 2
    run, place = slots // run_rows, slots % run_rows
    held = (place // half_run + core) % 2
    return held * half + run * half_run + place % half_run


def one_hot(column, width, base):
    count = column.shape[1]
    down = jnp.broadcast_to(column, (8, count)).T[:, :1]
    lane = lax.broadcasted_iota(jnp.int32, (count, width), 1) + base
    return (down == lane).astype(F32).astype(BF16)


def intake_kernel(
    run_rows, core, slots, mine_ref, other_ref, q_weight, k_weight, v_weight, q_bias, v_bias,
    x_ref, q_ref, k_ref, v_ref
):
    half = mine_ref.shape[0]
    column = columns_of(slots[...], core[0], run_rows, half)
    rows = nn(one_hot(column, half, 0), mine_ref[...])
    rows = (rows + nn(one_hot(column, half, half), other_ref[...])).astype(BF16)
    x_ref[...] = rows
    q_ref[...] = (nn(rows, q_weight[...]) + q_bias[...]).astype(BF16)
    k_ref[...] = nn(rows, k_weight[...]).astype(BF16)
    v_ref[...] = (nn(rows, v_weight[...]) + v_bias[...]).astype(BF16)


def intake(core, slots, run_rows, mine_rows, other_rows, weights, biases):
    half, features = mine_rows.shape
    rows = 2 * half
    width = weights[0].shape[1]
    count = 512
    blocks = rows // count

    def tile(n):
        return pl.BlockSpec((count, n), lambda i, core: (i, 0))

    return pl.pallas_call(
        functools.partial(intake_kernel, run_rows),
        grid_spec=pltpu.PrefetchScalarGridSpec(
            num_scalar_prefetch=1,
            grid=(blocks,),
            in_specs=[
                pl.BlockSpec(
                    (1, count), lambda i, core: (0, (i + core[0] * (blocks // 2)) % blocks)
                ),
                whole((half, features)),
                whole((half, features)),
            ]
            + [whole((features, width))] * 3
            + [whole((1, width))] * 2,
            out_specs=[tile(features), tile(width), tile(width), tile(width)],
        ),
        out_shape=[jax.ShapeDtypeStruct((rows, features), BF16)]
        + [jax.ShapeDtypeStruct((rows, width), BF16)] * 3,
        cost_estimate=cost(2 * rows * features * (rows + 3 * width), 8 * rows * features),
        compiler_params=params(),
        name="intake",
    )(core, slots, mine_rows, other_rows, *weights, *biases)


def centred(values):
    centre = values - jnp.mean(values, axis=-1, keepdims=True)
    inverse = lax.rsqrt(jnp.mean(centre * centre, axis=-1, keepdims=True) + EPSILON)
    return centre * inverse, inverse


def norm_back(upstream, normed, inverse, gain):
    scaled = upstream * gain
    return inverse * (
        scaled
        - jnp.mean(scaled, axis=-1, keepdims=True)
        - normed * jnp.mean(scaled * normed, axis=-1, keepdims=True)
    )


def add_rows(ref, row, values):
    ref[row : row + 1, :] += jnp.sum(values, axis=0, keepdims=True)


def rows_kernel(
    run_rows, core, x_ref, mixed_mine, mixed_other, slots, cot_mine, cot_other,
    out_bias, first_gain, first_shift, down_bias, second_gain, second_shift, bias_mine, bias_other,
    out_mine, out_other, up_mine, up_other, down_mine, down_other,
    y_out, hb_out, second_out, act_out_mine, act_out_other, du_out_mine, du_out_other, first_out, low_out,
    back_out_mine, back_out_other, sums, up_sums,
    w_out, w_up, w_down, sems, out_sems, hidden, first_inv, total, slope, grad, pulled, biases,
    y_ref, hb_ref, second_ref, act, du, first_ref, low_ref, back
):
    half, features = x_ref.shape
    width = mixed_mine.shape[1]
    chunks, _, chunk = w_up.shape
    per_half = chunks // 2
    tiles = half // ROW_TILE
    copies = [
        pltpu.make_async_copy(out_mine, w_out.at[0], sems.at[0]),
        pltpu.make_async_copy(out_other, w_out.at[1], sems.at[1]),
    ]
    up_copies, down_copies = [], []
    for c in range(chunks):
        up, down = ((up_mine, down_mine), (up_other, down_other))[c // per_half]
        at = pl.ds(c % per_half * chunk, chunk)
        up_copies.append(pltpu.make_async_copy(up.at[:, at], w_up.at[c], sems.at[2 + c]))
        down_copies.append(
            pltpu.make_async_copy(down.at[at, :], w_down.at[c], sems.at[2 + chunks + c])
        )
    outgoing = []

    def send(source, target):
        copy = pltpu.make_async_copy(source, target, out_sems.at[len(outgoing)])
        copy.start()
        outgoing.append(copy)

    for copy in copies:
        copy.start()
    for up, down in zip(up_copies, down_copies):
        up.start()
        down.start()
    out_bias, first_gain, first_shift = out_bias[...], first_gain[...], first_shift[...]
    down_bias, second_gain, second_shift = down_bias[...], second_gain[...], second_shift[...]
    sums[...] = jnp.zeros_like(sums)
    up_sums[...] = jnp.zeros_like(up_sums)

    column = columns_of(slots[...], core[0], run_rows, half)
    grad[...] = nn(one_hot(column, half, 0), cot_mine[...])
    grad[...] += nn(one_hot(column, half, half), cot_other[...])

    def of_chunk(refs, c):
        return refs[c // per_half], pl.ds(c % per_half * chunk, chunk)

    for copy in copies:
        copy.wait()
    total[...] = nn(mixed_mine[...], w_out[0]) + nn(mixed_other[...], w_out[1])

    @pl.loop(0, tiles, unroll=2)
    def _(i):
        at = pl.ds(pl.multiple_of(i * ROW_TILE, ROW_TILE), ROW_TILE)
        normed, inverse = centred(x_ref[at, :].astype(F32) + total[at, :] + out_bias)
        rows = normed * first_gain + first_shift
        hidden[at, :] = rows
        hb_ref[at, :] = rows.astype(BF16)
        first_ref[at, :] = normed
        first_inv[at, :] = inverse

    send(hb_ref, hb_out)

    block = half // 2
    blocks = [slice(r * block, (r + 1) * block) for r in range(2)]
    for c in range(chunks):
        ref, wide = of_chunk((bias_mine, bias_other), c)
        biases[c : c + 1, :] = ref[:, wide]

    def inner_of(c):
        pltpu.make_async_copy(up_mine.at[:, pl.ds(0, chunk)], w_up.at[c], sems.at[2 + c]).wait()
        for at in blocks:
            slope[c, at, :] = nn(hb_ref[at, :], w_up[c]) + biases[pl.ds(c, 1), :]

    def activate(c):
        for at in blocks:
            inner = slope[c, at, :]
            share = 0.5 * (1.0 + lax.erf(inner * 0.7071067811865476))
            density = jnp.exp(-0.5 * inner * inner) * 0.3989422804014327
            act[c, at, :] = (inner * share).astype(BF16)
            slope[c, at, :] = share + inner * density
            total[at, :] += nn(act[c, at, :], w_down[c])

    def down_ready(c):
        source = down_mine.at[pl.ds(0, chunk), :]
        pltpu.make_async_copy(source, w_down.at[c], sems.at[2 + chunks + c]).wait()

    total[...] = jnp.zeros_like(total)
    inner_of(0)

    @pl.loop(0, chunks - 1)
    def _(c):
        down_ready(c)
        inner_of(c + 1)
        activate(c)

    down_ready(chunks - 1)
    activate(chunks - 1)
    for c in range(chunks):
        ref, wide = of_chunk((act_out_mine, act_out_other), c)
        send(act.at[c], ref.at[:, wide])

    @pl.loop(0, tiles, unroll=2)
    def _(i):
        at = pl.ds(pl.multiple_of(i * ROW_TILE, ROW_TILE), ROW_TILE)
        normed, inverse = centred(hidden[at, :] + total[at, :] + down_bias)
        y_ref[at, :] = (normed * second_gain + second_shift).astype(BF16)
        upstream = grad[at, :]
        add_rows(sums, 4, upstream * normed)
        add_rows(sums, 5, upstream)
        back = norm_back(upstream, normed, inverse, second_gain)
        add_rows(sums, 3, back)
        second_ref[at, :] = back.astype(BF16)
        grad[at, :] = back

    send(y_ref, y_out)
    send(second_ref, second_out)
    def pull(c):
        for at in blocks:
            pulled[c % 2, at, :] = nt(second_ref[at, :], w_down[c])

    def push(c):
        row = (c // per_half ^ core[0]) * per_half + c % per_half
        for at in blocks:
            low = (pulled[c % 2, at, :] * slope[c, at, :]).astype(BF16)
            du[c, at, :] = low
            up_sums[pl.ds(row, 1), :] += jnp.sum(low.astype(F32), axis=0, keepdims=True)
            grad[at, :] += nt(low, w_up[c])

    pull(0)

    @pl.loop(0, chunks - 1)
    def _(c):
        pull(c + 1)
        push(c)

    push(chunks - 1)
    for c in range(chunks):
        ref, wide = of_chunk((du_out_mine, du_out_other), c)
        send(du.at[c], ref.at[:, wide])

    @pl.loop(0, tiles, unroll=2)
    def _(i):
        at = pl.ds(pl.multiple_of(i * ROW_TILE, ROW_TILE), ROW_TILE)
        upstream, normed = grad[at, :], first_ref[at, :]
        add_rows(sums, 1, upstream * normed)
        add_rows(sums, 2, upstream)
        back = norm_back(upstream, normed, first_inv[at, :], first_gain)
        add_rows(sums, 0, back)
        first_ref[at, :] = back

    send(first_ref, first_out)
    low_ref[...] = first_ref[...].astype(BF16)
    send(low_ref, low_out)
    for n, out in enumerate((back_out_mine, back_out_other)):
        back[n] = nt(low_ref[...], w_out[n]).astype(BF16)
        send(back.at[n], out)
    for copy in outgoing:
        copy.wait()


def row_pass(
    core, inputs, mixed, mixed_other, slots, run_rows, cot_mine, cot_other, vectors,
    out_mine, out_other, up_mine, up_other, down_mine, down_other
):
    half, features = cot_mine.shape
    width = mixed.shape[1]
    chunk = features
    chunks = 2 * up_mine.shape[1] // chunk
    any_space = pl.BlockSpec(memory_space=pl.ANY)

    def low(*shape):
        return jax.ShapeDtypeStruct(shape, BF16)

    outs = [
        low(half, features),
        low(half, features),
        low(half, features),
        low(half, up_mine.shape[1]),
        low(half, up_mine.shape[1]),
        low(half, up_mine.shape[1]),
        low(half, up_mine.shape[1]),
        jax.ShapeDtypeStruct((half, features), F32),
        low(half, features),
        low(half, width),
        low(half, width),
        jax.ShapeDtypeStruct((8, features), F32),
        jax.ShapeDtypeStruct((chunks, chunk), F32),
    ]
    return pl.pallas_call(
        functools.partial(rows_kernel, run_rows),
        grid_spec=pltpu.PrefetchScalarGridSpec(
            num_scalar_prefetch=1,
            grid=(1,),
            in_specs=[
                whole((half, features)),
                whole((half, width)),
                whole((half, width)),
                pl.BlockSpec((1, half), lambda i, core: (0, core[0])),
                whole((half, features)),
                whole((half, features)),
            ]
            + [whole(v.shape) for v in vectors]
            + [any_space] * 6,
            out_specs=[any_space] * (len(outs) - 2) + [whole(o.shape) for o in outs[-2:]],
            scratch_shapes=[
                pltpu.VMEM((2, width, features), BF16),
                pltpu.VMEM((chunks, features, chunk), BF16),
                pltpu.VMEM((chunks, chunk, features), BF16),
                pltpu.SemaphoreType.DMA((2 + 2 * chunks,)),
                pltpu.SemaphoreType.DMA((7 + 2 * chunks,)),
                pltpu.VMEM((half, features), F32),
                pltpu.VMEM((half, 1), F32),
                pltpu.VMEM((half, features), F32),
                pltpu.VMEM((chunks, half, chunk), F32),
                pltpu.VMEM((half, features), F32),
                pltpu.VMEM((2, half, chunk), F32),
                pltpu.VMEM((chunks, chunk), F32),
                pltpu.VMEM((half, features), BF16),
                pltpu.VMEM((half, features), BF16),
                pltpu.VMEM((half, features), BF16),
                pltpu.VMEM((chunks, half, chunk), BF16),
                pltpu.VMEM((chunks, half, chunk), BF16),
                pltpu.VMEM((half, features), F32),
                pltpu.VMEM((half, features), BF16),
                pltpu.VMEM((2, half, width), BF16),
            ],
        ),
        out_shape=outs,
        cost_estimate=cost(
            8 * half * features * chunk * chunks + 10 * half * features * features,
            30 * half * features + 8 * features * chunk * chunks,
            half * chunk * chunks,
        ),
        compiler_params=params(),
        name="row_pass",
    )(
        core, inputs, mixed, mixed_other, slots, cot_mine, cot_other, *vectors,
        out_mine, out_other, up_mine, up_other, down_mine, down_other
    )


def after(values, others):
    return lax.optimization_barrier((values, others))[0]


def near_groups(groups):
    near = 4 if groups % 4 == 0 else 1
    return near, groups // near


def tn(left, right):
    return lax.dot_general(left, right, (((0,), (0,)), ((), ())), preferred_element_type=F32)


def by_place(terms, groups):
    near, far = near_groups(groups)
    place = lax.axis_index("dp") % near
    terms = terms.reshape(far, near, terms.shape[0] // groups, terms.shape[1])
    return [lax.dynamic_index_in_dim(terms, place ^ n, 1, keepdims=False) for n in range(near)]


def gradient_kernel(chunks, near, share, halving, me, *refs):
    operands, outs, acc = refs[: 4 * len(chunks)], refs[4 * len(chunks) : -1], refs[-1]
    step = pl.program_id(0)
    first, column = 0, 0
    for n, (chunk, count) in enumerate(chunks):
        left, left_more, right, right_more = operands[4 * n : 4 * n + 4]

        @pl.when((step >= first) & (step < first + count))
        def _():
            acc[:, :chunk] = tn(left[...], right[...])
            acc[:, :chunk] += tn(left_more[...], right_more[...])
            at = pl.ds(pl.multiple_of(column + (step - first) * chunk, LANES), chunk)

            def place(out, place):
                for f in range(out.shape[0]):
                    row = share * (f * near + (me[0] ^ place))
                    row = pl.ds(pl.multiple_of(row, 16), share)
                    out[f, :, at] = acc[row, :chunk].astype(out.dtype)

            if halving:
                for out, (a, b) in zip(outs, ((0, 3 - halving), (halving, 3))):
                    place(out.at[0], a)
                    place(out.at[1], b)
            else:
                for m, out in enumerate(outs):
                    place(out, m)

        first += count
        column += count * chunk


def gradients(pieces, groups, halving=0):
    near, far = near_groups(groups)
    features = pieces[0][0][0].shape[1]
    share = features // groups
    if near != 4 or share % 16 != 0:

        def rows_of(left, rows):
            return lax.slice_in_dim(left[0], left[1] * rows, (left[1] + 1) * rows, axis=0)

        terms = [
            tn(rows_of(p[0], p[2].shape[0]), p[2]) + tn(rows_of(p[1], p[3].shape[0]), p[3])
            for p in pieces
        ]
        made = [t.astype(BF16) for t in by_place(jnp.concatenate(terms, axis=1), groups)]
        if halving:
            made = [
                jnp.stack([made[0], made[3 - halving]]), jnp.stack([made[halving], made[3]])
            ]
        return made
    in_specs, operands, chunks, base, columns = [], [], [], 0, 0
    for left, left_more, right, right_more in pieces:
        rows = right.shape[0]
        chunk = min(features, right.shape[1])
        if right.shape[1] % chunk:
            chunk = right.shape[1] // 3
        count = right.shape[1] // chunk

        def at(j, me, base=base, count=count):
            return 0, jnp.clip(j - base, 0, count - 1)

        for array, block in (left, left_more):
            in_specs.append(
                pl.BlockSpec((rows, features), lambda j, me, block=block: (block, 0))
            )
            operands.append(array)
        in_specs += [pl.BlockSpec((rows, chunk), at)] * 2
        operands += [right, right_more]
        chunks.append((chunk, count))
        base += count
        columns += count * chunk
    if halving:
        outs = [jax.ShapeDtypeStruct((2, far, share, columns), BF16)] * 2
    else:
        outs = [jax.ShapeDtypeStruct((far, share, columns), BF16)] * near
    return pl.pallas_call(
        functools.partial(gradient_kernel, chunks, near, share, halving),
        grid_spec=pltpu.PrefetchScalarGridSpec(
            num_scalar_prefetch=1,
            grid=(base,),
            in_specs=in_specs,
            out_specs=[whole(o.shape) for o in outs],
            scratch_shapes=[pltpu.VMEM((features, features), F32)],
        ),
        out_shape=outs,
        cost_estimate=cost(4 * rows * features * columns, 8 * rows * features + 4 * features * columns),
        compiler_params=params(),
        name="gradients",
    )((lax.axis_index("dp") % near).reshape(1), *operands)


def pairs(groups, distance):
    return [(i, i ^ distance) for i in range(groups)]


def far_halves(total, groups, bit):
    total = total.reshape(-1, 2, *total.shape[1:])
    side = (lax.axis_index("dp") // near_groups(groups)[0] >> bit) & 1
    kept = lax.dynamic_index_in_dim(total, side, 1, keepdims=False)
    return kept, lax.dynamic_index_in_dim(total, 1 - side, 1, keepdims=False).astype(BF16)


def far_halves_of(terms, groups, bit):
    side = (lax.axis_index("dp") // near_groups(groups)[0] >> bit) & 1
    halves = []
    for which in (side, 1 - side):
        total = 0.0
        for n, term in enumerate(terms):
            term = term.reshape(-1, 2, *term.shape[1:])
            term = lax.dynamic_index_in_dim(term, which, 1, keepdims=False).astype(F32)
            total = total + term if n else term
        halves.append(total)
    return halves[0], halves[1].astype(BF16)


def far_step(halves, groups, bit, first=()):
    near, far = near_groups(groups)
    kept, sent = halves
    got = after(lax.ppermute(sent, "dp", pairs(groups, near << bit)), first)
    total = kept.astype(F32) + got.astype(F32)
    return far_halves(total, groups, bit + 1) if 2 << bit < far else total[0]


def far_direct(total, groups, first=()):
    near, far = near_groups(groups)
    run = lax.axis_index("dp") // near
    kept = lax.dynamic_index_in_dim(total, run, 0, keepdims=False)
    got = []
    for step in range(1, far):
        sent = lax.dynamic_index_in_dim(total, run ^ step, 0, keepdims=False).astype(BF16)
        got.append(lax.ppermute(sent, "dp", pairs(groups, step * near)))
    return sum_of(kept, after(got, first))


def near_sends(terms, groups):
    return [lax.ppermute(t, "dp", pairs(groups, n + 1)) for n, t in enumerate(terms)]


def sum_of(kept, got):
    kept = kept.astype(F32)
    for term in got:
        kept = kept + term.astype(F32)
    return kept


def input_kernel(first_ref, mine_ref, other_ref, *refs):
    weights, out_ref = refs[:-1], refs[-1]
    total = first_ref[...]
    width = weights[0].shape[1]
    for n, weight in enumerate(weights):
        rows = (mine_ref, other_ref)[n // 3]
        total = total + nt(rows[:, n % 3 * width : (n % 3 + 1) * width], weight[...])
    out_ref[...] = total.astype(BF16)


def input_rows(first_grad, mine_rows, other_rows, weights):
    half, features = first_grad.shape
    wide = other_rows.shape[1]
    count = 512

    def tile(n):
        return pl.BlockSpec((count, n), lambda i: (i, 0))

    return pl.pallas_call(
        input_kernel,
        grid=(half // count,),
        in_specs=[tile(features), tile(wide), tile(wide)] + [whole(w.shape) for w in weights],
        out_specs=tile(features),
        out_shape=jax.ShapeDtypeStruct((half, features), BF16),
        cost_estimate=cost(4 * half * features * wide, 8 * half * features + 4 * features * wide),
        compiler_params=params(),
        name="input_rows",
    )(first_grad, mine_rows, other_rows, *weights)


def route_kernel(share, has_extra, core, slots_mine, slots_other, mine_ref, other_ref, *refs):
    out_ref = refs[-1]
    groups, run = out_ref.shape[0], mine_ref.shape[0] // out_ref.shape[0]
    half = mine_ref.shape[0]
    row = lax.broadcasted_iota(jnp.int32, (half, half), 0)
    column_mine = columns_of(slots_mine[...], core[0], 2 * run, half)
    column_other = columns_of(slots_other[...], core[0], 2 * run, half)
    put_mine = (column_mine == row).astype(F32).astype(BF16)
    put_other = (column_other == row).astype(F32).astype(BF16)
    rows = (nn(put_mine, mine_ref[...]) + nn(put_other, other_ref[...])).astype(BF16)
    out_ref[:, :run, :] = rows.reshape(groups, run, rows.shape[1])
    if has_extra:
        sums, up_sums, qv_sums, wide, wide_up = refs[:5]
        features = sums.shape[1]
        width = qv_sums.shape[1]
        wide[...] = jnp.zeros_like(wide)
        wide_up[...] = jnp.zeros_like(wide_up)
        wide[:, :features] = sums[...]
        wide_up[:4, :features] = up_sums[...]
        at = pl.ds(pl.multiple_of(core[0] * width, LANES), width)
        wide[6:8, at] = qv_sums[:2, :]
        for g in range(groups):
            block = wide[:, share * g : share * g + LANES]
            start = 4 * share * g
            blocks = [block]
            parts = []
            for r in range(4):
                line = (start + share * r) // features
                lane = (start + share * r) % features
                parts.append(wide_up[line : line + 1, lane : lane + LANES])
            blocks.append(jnp.concatenate(parts + [jnp.zeros((4, LANES), F32)], axis=0))
            for b, rest in enumerate(blocks):
                for piece in range(3):
                    term = rest.astype(BF16)
                    rest = rest - term.astype(F32)
                    q = 2 * piece + b
                    out_ref[g, run : run + 8, q * LANES : (q + 1) * LANES] = term


def route(core, slots, mine_rows, other_rows, groups, extra=None):
    half, features = mine_rows.shape
    run = half // groups
    share = features // groups
    extra = extra or ()
    args = [core, slots, slots, mine_rows, other_rows, *extra]
    in_specs = [
        pl.BlockSpec((1, half), lambda i, core: (0, core[0])),
        pl.BlockSpec((1, half), lambda i, core: (0, 1 - core[0])),
    ] + [whole(a.shape) for a in args[3:]]
    scratch = [pltpu.VMEM((8, features + LANES), F32)] * 2 if extra else []
    shape = (groups, run + (8 if extra else 0), features)

    def kernel(*refs):
        ins, (out_ref, *more) = refs[: len(args)], refs[len(args) :]
        route_kernel(share, len(extra) > 0, *ins, *more, out_ref)

    return pl.pallas_call(
        kernel,
        grid_spec=pltpu.PrefetchScalarGridSpec(
            num_scalar_prefetch=1,
            grid=(1,),
            in_specs=in_specs,
            out_specs=whole(shape),
            scratch_shapes=scratch,
        ),
        out_shape=jax.ShapeDtypeStruct(shape, BF16),
        cost_estimate=cost(4 * half * half * features, 6 * half * features),
        compiler_params=params(),
        name="route",
    )(*args)


def exchange(values):
    return lax.all_to_all(values, "dp", split_axis=0, concat_axis=0, tiled=True)


def weave_kernel(core, mine_ref, other_ref, out_ref, *outs):
    run = out_ref.shape[2]
    out_ref[:, core[0]] = mine_ref[:, :run, :]
    out_ref[:, 1 - core[0]] = other_ref[:, :run, :]
    if not outs:
        return
    pieces = []
    for q in range(6):
        at = slice(q * LANES, (q + 1) * LANES)
        both = [jnp.sum(r[:, run:, at].astype(F32), axis=0) for r in (mine_ref, other_ref)]
        pieces.append(both[0] + both[1])
    first, more = [pieces[4 + b] + pieces[2 + b] + pieces[b] for b in range(2)]
    each = outs[0].shape[1]
    share = 2 * each
    low = core[0] == 0

    def half_of(values):
        return jnp.where(low, values[:, :each], values[:, each:share])

    for out, row in zip(outs[:8], (6, 7, 0, 1, 2, 3, 4, 5)):
        out[...] = half_of(first[row : row + 1, :])
    pair = jnp.where(low, more[0:2, :share], more[2:4, :share])
    outs[8][:, :share] = pair[0:1, :]
    outs[8][:, share:] = pair[1:2, :]


def weave(core, part, rows_of_core, small=0):
    groups, _, features = part.shape
    outs = [jax.ShapeDtypeStruct((groups, 2, rows_of_core, features), BF16)]
    if small:
        outs += [jax.ShapeDtypeStruct((1, small), F32)] * 8
        outs.append(jax.ShapeDtypeStruct((1, 4 * small), F32))
    rows, *more = pl.pallas_call(
        weave_kernel,
        grid_spec=pltpu.PrefetchScalarGridSpec(
            num_scalar_prefetch=1,
            grid=(1,),
            in_specs=[whole(part.shape)] * 2,
            out_specs=[whole(o.shape) for o in outs],
        ),
        out_shape=outs,
        cost_estimate=cost(1, 1),
        compiler_params=params(),
        name="weave",
    )(core, part, swap(part))
    rows = rows.reshape(groups * 2 * rows_of_core, features)
    return (rows, *[m.reshape(-1) for m in more]) if small else rows


def local(
    tokens,
    token_slot,
    seq_lengths,
    query_weight,
    query_bias,
    key_weight,
    value_weight,
    value_bias,
    out_weight,
    out_bias,
    first_gain,
    first_shift,
    up_weight,
    up_bias,
    down_weight,
    down_bias,
    second_gain,
    second_shift,
    cotangent,
):
    groups = lax.axis_size("dp")
    row_count, features = tokens.shape
    run_rows = row_count // groups
    half_run = run_rows // 2
    half = row_count // 2
    mine = lax.axis_index("tensor")
    core = mine.reshape(1)
    near, far = near_groups(groups)

    def part_of(values):
        return lax.dynamic_slice_in_dim(
            values.reshape(groups, run_rows, features), mine * half_run, half_run, 1
        )

    cot_part = part_of(cotangent)
    token_rows = after(exchange(part_of(tokens)), cot_part).reshape(half, features)
    cot_raw = exchange(cot_part).reshape(half, features)

    qkv_weights = [query_weight, key_weight, value_weight]
    out_other, up_other, down_other = swap(out_weight), swap(up_weight), swap(down_weight)
    vectors = [out_bias, first_gain, first_shift, down_bias, second_gain, second_shift]
    bias_other = swap(up_bias)
    vectors = [v.reshape(1, -1) for v in vectors + [up_bias, bias_other]]
    qkv_other = [swap(w) for w in qkv_weights]
    biases = [query_bias.reshape(1, -1), value_bias.reshape(1, -1)]
    early = (out_other, up_other, down_other, qkv_other)
    token_rows, vectors, biases, early = lax.optimization_barrier(
        (token_rows, vectors, biases, early)
    )
    out_other, up_other, down_other, qkv_other = early
    token_got = swap(token_rows)

    inputs, query_rows, key_rows, value_rows = intake(
        core, token_slot, run_rows, token_rows, token_got, qkv_weights,
        biases,
    )
    mixed_mine, mixed_theirs, logsum = attention_forward(seq_lengths, core, query_rows, key_rows, value_rows)
    cot_rows = after(cot_raw, mixed_mine)
    mixed_other = swap(mixed_theirs)
    (
        output_low, hidden_low, second_low, act_mine, act_other, inner_mine, inner_other, first_grad,
        first_low, mixed_grad_mine, mixed_grad_other, sums, up_sums,
    ) = row_pass(
        core, inputs, mixed_mine, mixed_other, token_slot, run_rows, cot_rows, swap(cot_rows), vectors,
        out_weight, out_other, up_weight, up_other, down_weight, down_other,
    )
    mixed_grad_got = swap(mixed_grad_other)

    width = query_weight.shape[1]
    ff_width = up_weight.shape[1]
    output_got = swap(output_low)
    second_low, hidden_low, first_low, act_other, inner_other = after(
        (second_low, hidden_low, first_low, act_other, inner_other), output_got
    )
    second_got, act_got = swap(second_low), swap(act_other)
    hidden_got, inner_got = swap(hidden_low), swap(inner_other)
    first_got = swap(first_low)
    returned = route(core, token_slot, output_low, output_got, groups)
    kept, sent = [], []
    left = gradients([((second_low, 0), (second_got, 0), act_mine, act_got)], groups, near == 4)
    right = [
        ((hidden_low, 0), (hidden_got, 0), inner_mine, inner_got),
        ((first_low, 0), (first_got, 0), mixed_mine, mixed_theirs),
    ]
    right = gradients(right, groups, 2 * (near == 4))
    if near == 4:
        kept, sent = [left[0], right[0]], [left[1], right[1]]
    else:
        kept, sent = [left[0][None], right[0][None]], []
    mixed_grad_mine, mixed_grad_got = after(
        (mixed_grad_mine, mixed_grad_got), (returned, kept, sent)
    )
    returned = exchange(returned)
    got = [lax.ppermute(v, "dp", pairs(groups, n + 1)) for n, v in enumerate(sent)]
    qkv_mine, qkv_theirs, qv_sums = attention_backward(
        seq_lengths, core, query_rows, key_rows, value_rows, (mixed_mine, mixed_theirs), logsum,
        mixed_grad_mine, mixed_grad_got,
    )
    other_grad = swap(qkv_theirs)
    qkv_terms = gradients([((inputs, 0), (inputs, 1), qkv_mine, qkv_theirs)], groups)
    got, returned = after((got, returned), qkv_terms)
    sent = [(k[1].astype(F32) + g[1].astype(F32)).astype(BF16) for k, g in zip(kept, got)]
    first_grad = after(first_grad, (qkv_terms, sent))
    kept, first_got = [k[0].astype(F32) for k in kept], got
    qkv_got = near_sends(qkv_terms[1:], groups)
    got = [lax.ppermute(v, "dp", pairs(groups, 2 - n)) for n, v in enumerate(sent)]
    input_low = input_rows(
        first_grad, qkv_mine, other_grad, qkv_weights + qkv_other
    )
    given = route(core, token_slot, input_low, swap(input_low), groups, (sums, up_sums, qv_sums))
    got = after(got, given)
    parts = [[k] for k in kept]
    if got:
        parts = [[k, f[0], g] for k, f, g in zip(kept, first_got, got)]
    ffn_terms = [
        jnp.concatenate(half, axis=-1) for half in zip(*(far_halves_of(p, groups, 0) for p in parts))
    ]
    payload, given = given, exchange(given)
    layer_out = weave(core, after(returned, payload), half_run)
    ffn_sum = far_step(ffn_terms, groups, 0, (given, layer_out))
    qkv_got = after(qkv_got, ffn_sum)
    for bit in range(1, far.bit_length() - 1):
        ffn_sum = far_step(ffn_sum, groups, bit, qkv_got)
    qkv_sum = far_direct(sum_of(qkv_terms[0], qkv_got), groups, ffn_sum)
    (
        input_gradient, query_bias_sum, value_bias_sum, out_bias_sum, first_gain_sum,
        first_shift_sum, down_bias_sum, second_gain_sum, second_shift_sum, up_bias_sum,
    ) = weave(core, given, half_run, features // groups // 2)
    return (
        layer_out,
        input_gradient,
        qkv_sum[:, :width],
        query_bias_sum,
        qkv_sum[:, width : 2 * width],
        qkv_sum[:, 2 * width :],
        value_bias_sum,
        ffn_sum[:, 2 * ff_width :].T,
        out_bias_sum,
        first_gain_sum,
        first_shift_sum,
        ffn_sum[:, ff_width : 2 * ff_width],
        up_bias_sum,
        ffn_sum[:, :ff_width].T,
        down_bias_sum,
        second_gain_sum,
        second_shift_sum,
    )


def solution(mesh):
    rows = P("dp", None)
    in_specs = (
        rows,
        rows,
        rows,
        P(None, "tensor"),
        P("tensor"),
        P(None, "tensor"),
        P(None, "tensor"),
        P("tensor"),
        P("tensor", None),
        P(),
        P(),
        P(),
        P(None, "tensor"),
        P("tensor"),
        P("tensor", None),
        P(),
        P(),
        P(),
        rows,
    )
    spread = P(("dp", "tensor"))
    out_specs = (
        rows,
        rows,
        P("dp", "tensor"),
        spread,
        P("dp", "tensor"),
        P("dp", "tensor"),
        spread,
        P("tensor", "dp"),
        spread,
        spread,
        spread,
        P("dp", "tensor"),
        spread,
        P("tensor", "dp"),
        spread,
        spread,
        spread,
    )
    return jax.shard_map(local, mesh=mesh, in_specs=in_specs, out_specs=out_specs, check_vma=False)
```
